32 devices in a mesh: dp: 16 (over z, y, core), mp: 2 (over x).
Axes of the slice: x: 2, y: 2, z: 4, core: 2. Of those that a mesh axis runs over, the one named last changes fastest.
Arguments:
- inputs: bfloat16 [16384, 768], P('dp'), may hold values from -8 to 8
- encoded: bfloat16 [16384, 768], P('dp'), may hold values from -6 to 6
- cotangent: bfloat16 [16384, 768], P('dp'), may hold values from -6 to 6
- buckets: int32 [512], replicated, may hold values from 0 to 31, as said below
- rel_table: bfloat16 [12, 32], P('mp'), may hold values from -6 to 6
- query_self: bfloat16 [768, 768], P('dp', 'mp'), may hold values from -0.02734375 to 0.02734375
- keys_self: bfloat16 [768, 768], P('dp', 'mp'), may hold values from -0.21875 to 0.21875
- values_self: bfloat16 [768, 768], P('dp', 'mp'), may hold values from -0.21875 to 0.21875
- output_self: bfloat16 [768, 768], P('mp', 'dp'), may hold values from -0.875 to 0.875
- query_cross: bfloat16 [768, 768], P('dp', 'mp'), may hold values from -0.02734375 to 0.02734375
- keys_cross: bfloat16 [768, 768], P('dp', 'mp'), may hold values from -0.21875 to 0.21875
- values_cross: bfloat16 [768, 768], P('dp', 'mp'), may hold values from -0.21875 to 0.21875
- output_cross: bfloat16 [768, 768], P('mp', 'dp'), may hold values from -1.75 to 1.75
- gate_weight: bfloat16 [768, 2048], P('dp', 'mp'), may hold values from -0.21875 to 0.21875
- up_weight: bfloat16 [768, 2048], P('dp', 'mp'), may hold values from -0.21875 to 0.21875
- down_weight: bfloat16 [2048, 768], P('mp', 'dp'), may hold values from -0.125 to 0.125
- gain_first: bfloat16 [768], P('dp'), may hold values from 0.099609375 to 1.8984375
- gain_second: bfloat16 [768], P('dp'), may hold values from 0.099609375 to 1.8984375
- gain_third: bfloat16 [768], P('dp'), may hold values from 0.099609375 to 1.8984375
Outputs:
- layer_output: float32 [16384, 768], P('dp')
- input_gradient: float32 [16384, 768], P('dp')
- encoded_gradient: float32 [16384, 768], P('dp')
- table_gradient: float32 [12, 32], P('mp')
- query_self_gradient: float32 [768, 768], P('dp', 'mp')
- keys_self_gradient: float32 [768, 768], P('dp', 'mp')
- values_self_gradient: float32 [768, 768], P('dp', 'mp')
- output_self_gradient: float32 [768, 768], P('mp', 'dp')
- query_cross_gradient: float32 [768, 768], P('dp', 'mp')
- keys_cross_gradient: float32 [768, 768], P('dp', 'mp')
- values_cross_gradient: float32 [768, 768], P('dp', 'mp')
- output_cross_gradient: float32 [768, 768], P('mp', 'dp')
- gate_weight_gradient: float32 [768, 2048], P('dp', 'mp')
- up_weight_gradient: float32 [768, 2048], P('dp', 'mp')
- down_weight_gradient: float32 [2048, 768], P('mp', 'dp')
- gain_first_gradient: float32 [768], P('dp')
- gain_second_gradient: float32 [768], P('dp')
- gain_third_gradient: float32 [768], P('dp')
The draws below stay inside these ranges and needn't reach their ends.
Inputs may be any that keep to these rules, and one draw needn't show every extreme that they name: `buckets`: the bucket of offset o is o for o < 16; beyond it never falls, rises by at most one from one offset to the next, and is 31 at offset 512 - 1.
All inputs are finite; a program needn't handle non-finite values.
Results may differ from the reference program's by a relative error of at most 0.02.
Values may be sent and summed in bfloat16 or wider, within the bound.
No kernel may reach another device: no remote copies, remote signals or barrier semaphores. Data moves between devices by JAX's collectives and lax.ppermute only.
A program may use at most 256 MiB of HBM per device.

```python
import jax
import jax.numpy as jnp
from jax import lax

D = 768
H = 12
DH = 64
FF = 2048
NB = 32
L = 512
LE = 512
HD = 768
SEQS = 32
TOKENS = 16384


def draw_inputs(key, part):
    return jnp.clip(jax.random.normal(jax.random.fold_in(key, 3), (SEQS * L, D), jnp.float32), -6.0, 6.0).astype(jnp.bfloat16)


def draw_encoded(key, part):
    return jnp.clip(jax.random.normal(jax.random.fold_in(key, 7), (SEQS * LE, D), jnp.float32), -6.0, 6.0).astype(jnp.bfloat16)


def draw_rel_table(key, part):
    return jnp.clip(1.5 * jax.random.normal(key, (H, NB), jnp.float32), -6.0, 6.0).astype(jnp.bfloat16)


def draw_buckets(key, part):
    half = NB // 2
    order = jax.random.permutation(jax.random.fold_in(key, 5), L - half - 1)
    marks = order[:half - 1].astype(jnp.int32) + half + 1
    offsets = jnp.arange(L, dtype=jnp.int32)
    passed = jnp.sum((marks[None, :] <= offsets[:, None]).astype(jnp.int32), axis=1)
    return jnp.where(offsets < half, offsets, half + passed).astype(jnp.int32)


def raised(values, key, source, target, blocks, factor):
    def block_of(axis_at):
        return (jnp.arange(values.shape[axis_at]) // (values.shape[axis_at] // blocks)).reshape((-1,) + (1,) * (values.ndim - 1 - axis_at))

    one_side = jax.random.permutation(key, blocks)[block_of(target)]
    second = (block_of(target) + blocks // 2) % blocks
    return jnp.where((block_of(source) == one_side) | (block_of(source) == second), factor * values, values)


def block_levels(own_key, extent, shards, least, top_value):
    loudness = 1.0
    for position, blocks in shards:
        steps = jax.random.uniform(jax.random.fold_in(jax.random.fold_in(own_key, 6), position), (blocks,), jnp.float32, least / len(shards), top_value / len(shards))
        loudness = loudness * jnp.repeat(jnp.exp(steps), extent[position] // blocks).reshape((-1,) + (1,) * (len(extent) - 1 - position))
    return loudness


def gaussian(stream_key, extent, spread, most, cuts=(), held_as=jnp.bfloat16):
    array = spread * jax.random.normal(stream_key, extent, jnp.float32)
    if cuts:
        array = array * block_levels(stream_key, extent, cuts, -0.22, 0.18)
    return jnp.clip(array, -most, most).astype(held_as)


def heavy_noise(stream_key, shape, deviation, most, cuts, heavy, held_as=jnp.bfloat16):
    entries = deviation * jax.random.normal(stream_key, shape, jnp.float32)
    if cuts:
        entries = entries * block_levels(stream_key, shape, cuts, -0.22, 0.18)
    return jnp.clip(raised(entries, jax.random.fold_in(stream_key, 3), *heavy), -most, most).astype(held_as)


def setup_inputs(seed: int = 0) -> dict:
    seeds = jax.random.split(jax.random.key(seed), 20)
    inputs = draw_inputs(jax.random.fold_in(seeds[19], 71), 0)
    encoded = draw_encoded(jax.random.fold_in(seeds[19], 71), 0)
    cotangent = heavy_noise(seeds[2], (TOKENS, D), 1.0, 6.0, ((0, 16),), (0, 1, 16, 2.0))
    buckets = draw_buckets(jax.random.fold_in(seeds[19], 71), 0)
    rel_table = draw_rel_table(jax.random.fold_in(seeds[19], 71), 0)
    query_self = gaussian(seeds[5], (D, HD), (D * DH) ** -0.5, 0.02734375, ((0, 16), (1, 2)))
    keys_self = gaussian(seeds[6], (D, HD), D ** -0.5, 0.21875, ((0, 16), (1, 2)))
    values_self = gaussian(seeds[7], (D, HD), D ** -0.5, 0.21875, ((0, 16), (1, 2)))
    output_self = gaussian(seeds[8], (HD, D), (HD // 16) ** -0.5, 0.875, ((0, 2), (1, 16)))
    query_cross = gaussian(seeds[9], (D, HD), (D * DH) ** -0.5, 0.02734375, ((0, 16), (1, 2)))
    keys_cross = gaussian(seeds[10], (D, HD), D ** -0.5, 0.21875, ((0, 16), (1, 2)))
    values_cross = gaussian(seeds[11], (D, HD), D ** -0.5, 0.21875, ((0, 16), (1, 2)))
    output_cross = gaussian(seeds[12], (HD, D), (HD // 64) ** -0.5, 1.75, ((0, 2), (1, 16)))
    gate_weight = gaussian(seeds[13], (D, FF), D ** -0.5, 0.21875, ((0, 16), (1, 2)))
    up_weight = gaussian(seeds[14], (D, FF), D ** -0.5, 0.21875, ((0, 16), (1, 2)))
    down_weight = gaussian(seeds[15], (FF, D), FF ** -0.5, 0.125, ((0, 2), (1, 16)))
    gain_first = jnp.clip(1.0 + 0.18 * jax.random.normal(seeds[16], (D,), jnp.float32), 0.099609375, 1.8984375).astype(jnp.bfloat16)
    gain_second = jnp.clip(1.0 + 0.18 * jax.random.normal(seeds[17], (D,), jnp.float32), 0.099609375, 1.8984375).astype(jnp.bfloat16)
    gain_third = jnp.clip(1.0 + 0.18 * jax.random.normal(seeds[18], (D,), jnp.float32), 0.099609375, 1.8984375).astype(jnp.bfloat16)
    return dict(inputs=inputs, encoded=encoded, cotangent=cotangent, buckets=buckets, rel_table=rel_table, query_self=query_self, keys_self=keys_self, values_self=values_self, output_self=output_self, query_cross=query_cross, keys_cross=keys_cross, values_cross=values_cross, output_cross=output_cross, gate_weight=gate_weight, up_weight=up_weight, down_weight=down_weight, gain_first=gain_first, gain_second=gain_second, gain_third=gain_third)


EPS = 1e-06
NEG = -1e+30
GELU_C = 0.7978845608028654

def gelu_tanh(values):
    return 0.5 * values * (1.0 + jnp.tanh(GELU_C * (values + 0.044715 * values * values * values)))

def gated(gate_pre, up_pre):
    return gelu_tanh(gate_pre) * up_pre

def rms_scale(values, gain):
    return values * lax.rsqrt(lax.optimization_barrier(jnp.mean(values * values, axis=-1, keepdims=True)) + EPS) * gain

def rms_back(values, gain, incoming):
    result, pullback = jax.vjp(rms_scale, values, gain)
    return pullback(incoming)

def lowered(values):
    return lax.optimization_barrier(values.astype(jnp.bfloat16)).astype(jnp.float32)

def matmul(left, right):
    return jnp.dot(left, right, preferred_element_type=jnp.float32)

def matmul_tn(left, right):
    return lax.dot_general(left, right, (((0,), (0,)), ((), ())), preferred_element_type=jnp.float32)

def matmul_nt(left, right):
    return lax.dot_general(left, right, (((1,), (1,)), ((), ())), preferred_element_type=jnp.float32)

def heads_of(matrix):
    return matrix.reshape(matrix.shape[0], matrix.shape[1] // DH, DH).astype(jnp.float32)

def scores_of(queries, keys, bias, causal):
    scores = jnp.einsum('qhd,khd->hqk', heads_of(queries), heads_of(keys))
    if bias is not None:
        scores = scores + bias
    if causal:
        rows = lax.broadcasted_iota(jnp.int32, (queries.shape[0], keys.shape[0]), 0)
        cols = lax.broadcasted_iota(jnp.int32, (queries.shape[0], keys.shape[0]), 1)
        scores = jnp.where((rows >= cols)[None], scores, NEG)
    return scores

def attend(queries, keys, values, bias, causal):
    scores = scores_of(queries, keys, bias, causal)
    top = lax.optimization_barrier(jnp.max(scores, axis=-1, keepdims=True))
    lse = top + jnp.log(lax.optimization_barrier(jnp.sum(jnp.exp(scores - top), axis=-1, keepdims=True)))
    probs = lowered(jnp.exp(scores - lse))
    mixed = jnp.einsum('hqk,khd->qhd', probs, heads_of(values))
    return (mixed.reshape(queries.shape[0], -1).astype(jnp.bfloat16), lse[..., 0])

def attend_back(queries, keys, values, lse, grad_out, bias, causal):
    scores = scores_of(queries, keys, bias, causal)
    probs = jnp.exp(scores - lse[..., None])
    probs_low = lowered(probs)
    grad_heads = heads_of(grad_out)
    back_values = jnp.einsum('hqk,qhd->khd', probs_low, grad_heads)
    dprobs = jnp.einsum('qhd,khd->hqk', grad_heads, heads_of(values))
    dscores = probs * (dprobs - lax.optimization_barrier(jnp.sum(probs * dprobs, axis=-1, keepdims=True)))
    dscores_low = lowered(dscores)
    back_queries = jnp.einsum('hqk,khd->qhd', dscores_low, heads_of(keys))
    back_keys = jnp.einsum('hqk,qhd->khd', dscores_low, heads_of(queries))
    return (back_queries.reshape(queries.shape[0], -1).astype(jnp.bfloat16), back_keys.reshape(keys.shape[0], -1).astype(jnp.bfloat16), back_values.reshape(keys.shape[0], -1).astype(jnp.bfloat16), dscores)

def reference(inputs, encoded, cotangent, buckets, rel_table, query_self, keys_self, values_self, output_self, query_cross, keys_cross, values_cross, output_cross, gate_weight, up_weight, down_weight, gain_first, gain_second, gain_third):
    seqs = inputs.shape[0] // L
    positions = jnp.arange(L, dtype=jnp.int32)
    bucket_grid = buckets[jnp.clip(positions[:, None] - positions[None, :], 0, L - 1)]
    bias_grid = rel_table.astype(jnp.float32)[:, bucket_grid]
    gain_one = gain_first.astype(jnp.float32)
    gain_two = gain_second.astype(jnp.float32)
    gain_three = gain_third.astype(jnp.float32)

    def one_sequence(totals, pieces):
        input_rows, encoder_rows, tangent_rows = pieces
        resid_in = input_rows.astype(jnp.float32)
        normed_one = rms_scale(resid_in, gain_one).astype(jnp.bfloat16)
        queries_one = matmul(normed_one, query_self).astype(jnp.bfloat16)
        keys_one = matmul(normed_one, keys_self).astype(jnp.bfloat16)
        values_one = matmul(normed_one, values_self).astype(jnp.bfloat16)
        attn_one, lse_one = attend(queries_one, keys_one, values_one, bias_grid, True)
        resid_one = resid_in + matmul(attn_one, output_self)
        normed_two = rms_scale(resid_one, gain_two).astype(jnp.bfloat16)
        queries_two = matmul(normed_two, query_cross).astype(jnp.bfloat16)
        keys_two = matmul(encoder_rows, keys_cross).astype(jnp.bfloat16)
        values_two = matmul(encoder_rows, values_cross).astype(jnp.bfloat16)
        attn_two, lse_two = attend(queries_two, keys_two, values_two, None, False)
        resid_two = resid_one + matmul(attn_two, output_cross)
        normed_three = rms_scale(resid_two, gain_three).astype(jnp.bfloat16)
        gate_pre = matmul(normed_three, gate_weight)
        up_pre = matmul(normed_three, up_weight)
        hidden = gated(gate_pre, up_pre).astype(jnp.bfloat16)
        layer_rows = resid_two + matmul(hidden, down_weight)
        back_hidden = matmul_nt(tangent_rows, down_weight)
        result, gate_pullback = jax.vjp(gated, gate_pre, up_pre)
        gate_back, up_back = gate_pullback(back_hidden)
        gate_back = gate_back.astype(jnp.bfloat16)
        up_back = up_back.astype(jnp.bfloat16)
        back_three = matmul_nt(gate_back, gate_weight) + matmul_nt(up_back, up_weight)
        back_two, gain_three_term = rms_back(resid_two, gain_three, back_three)
        back_two = back_two + tangent_rows.astype(jnp.float32)
        back_two_low = back_two.astype(jnp.bfloat16)
        dattn_two = matmul_nt(back_two_low, output_cross).astype(jnp.bfloat16)
        back_queries_two, back_keys_two, back_values_two, unused = attend_back(queries_two, keys_two, values_two, lse_two, dattn_two, None, False)
        encoder_back = matmul_nt(back_keys_two, keys_cross) + matmul_nt(back_values_two, values_cross)
        back_one, gain_two_term = rms_back(resid_one, gain_two, matmul_nt(back_queries_two, query_cross))
        back_one = back_one + back_two
        back_one_low = back_one.astype(jnp.bfloat16)
        dattn_one = matmul_nt(back_one_low, output_self).astype(jnp.bfloat16)
        back_queries_one, back_keys_one, back_values_one, dscores_one = attend_back(queries_one, keys_one, values_one, lse_one, dattn_one, bias_grid, True)
        back_norm_one = matmul_nt(back_queries_one, query_self) + matmul_nt(back_keys_one, keys_self) + matmul_nt(back_values_one, values_self)
        back_in, gain_one_term = rms_back(resid_in, gain_one, back_norm_one)
        input_rows_back = back_in + back_one
        terms = (matmul_tn(normed_one, back_queries_one), matmul_tn(normed_one, back_keys_one), matmul_tn(normed_one, back_values_one), matmul_tn(attn_one, back_one_low), matmul_tn(normed_two, back_queries_two), matmul_tn(encoder_rows, back_keys_two), matmul_tn(encoder_rows, back_values_two), matmul_tn(attn_two, back_two_low), matmul_tn(normed_three, gate_back), matmul_tn(normed_three, up_back), matmul_tn(hidden, tangent_rows), gain_one_term, gain_two_term, gain_three_term, dscores_one)
        totals = tuple((total + term for total, term in zip(totals, terms)))
        return (totals, (layer_rows, input_rows_back, encoder_back))
    shapes = (query_self, keys_self, values_self, output_self, query_cross, keys_cross, values_cross, output_cross, gate_weight, up_weight, down_weight, gain_first, gain_second, gain_third)
    init = tuple((jnp.zeros(matrix.shape, jnp.float32) for matrix in shapes)) + (jnp.zeros((H, L, L), jnp.float32),)
    totals, stacked = lax.scan(one_sequence, init, (inputs.reshape(seqs, L, D), encoded.reshape(seqs, LE, D), cotangent.reshape(seqs, L, D)))
    table_gradient = jax.ops.segment_sum(totals[14].reshape(H, L * L).T, bucket_grid.reshape(-1), num_segments=NB).T
    return (stacked[0].reshape(seqs * L, D), stacked[1].reshape(seqs * L, D), stacked[2].reshape(seqs * LE, D), table_gradient, totals[0], totals[1], totals[2], totals[3], totals[4], totals[5], totals[6], totals[7], totals[8], totals[9], totals[10], totals[11], totals[12], totals[13])
```

```python
import jax
import jax.numpy as jnp
from jax import lax
from jax.experimental import pallas as pl
from jax.experimental.pallas import tpu as pltpu
from jax.sharding import PartitionSpec as P

DH = 64
NB = 32
L = 512
LANE = 128
QB = 128
EPS = 1e-06
NEG = -1e30
GELU_C = 0.7978845608028654
GELU_A = 0.044715
AXES = ("dp", "mp")
F32 = jnp.float32
BF16 = jnp.bfloat16
VMEM_LIMIT = 58 * 1024 * 1024


def nn(left, right):
    return lax.dot_general(left, right, (((1,), (0,)), ((), ())), preferred_element_type=F32)


def nt(left, right):
    return lax.dot_general(left, right, (((1,), (1,)), ((), ())), preferred_element_type=F32)


class Grid:
    def __init__(self, n_dp, n_mp):
        assert n_mp == 2 and n_dp % 8 == 0
        self.n_dp, self.n_mp = n_dp, n_mp
        self.n_z = n_dp // 4

    def perm(self, move):
        pairs = []
        for z in range(self.n_z):
            for y in range(2):
                for c in range(2):
                    for m in range(2):
                        tz, ty, tc, tm = move(z, y, c, m)
                        pairs.append(
                            (
                                (((z * 2 + y) * 2) + c) * 2 + m,
                                (((tz * 2 + ty) * 2) + tc) * 2 + tm,
                            )
                        )
        return pairs

    def swap_m(self, v):
        return lax.ppermute(v, AXES, self.perm(lambda z, y, c, m: (z, y, c, 1 - m)))

    def swap_y(self, v):
        return lax.ppermute(v, AXES, self.perm(lambda z, y, c, m: (z, 1 - y, c, m)))

    def swap_c(self, v):
        return lax.ppermute(v, AXES, self.perm(lambda z, y, c, m: (z, y, 1 - c, m)))

    def shift_z(self, v, d):
        n = self.n_z
        return lax.ppermute(v, AXES, self.perm(lambda z, y, c, m: ((z + d) % n, y, c, m)))


def place():
    dp = lax.axis_index("dp")
    return dp // 4, (dp // 2) % 2, dp % 2, lax.axis_index("mp")


def gather(grid, block):
    rows = block.shape[0]
    n = grid.n_z
    own = jnp.concatenate([block] + [grid.shift_z(block, d) for d in range(1, n)], axis=0)
    half = (n // 2) * rows
    by_m = grid.swap_m(own)
    by_y = grid.swap_y(own)
    diag_a = grid.swap_y(by_m[:half])
    diag_b = grid.swap_m(by_y[half:])
    pieces = [(own, 0, 0, 0), (by_m, 1, 0, 0), (by_y, 0, 1, 0), (diag_a, 1, 1, 0), (diag_b, 1, 1, n // 2)]
    out = [(a, m, y, 0, j) for a, m, y, j in pieces]
    out += [(grid.swap_c(a), m, y, 1, j) for a, m, y, j in pieces]
    if rows % 16 == 0:
        return out
    z, y, c, _ = place()
    cols = block.shape[1]
    stacks = []
    for m in range(2):
        for b in range(2):
            for e in range(2):
                mine = sorted((p for p in out if p[1:4] == (m, b, e)), key=lambda p: p[4])
                stacks.append(jnp.concatenate([p[0] for p in mine], axis=0).reshape(n, rows, cols))
    whole = jnp.stack(stacks).reshape(2, 2, 2, n, rows, cols)
    whole = jnp.take(whole, (z - jnp.arange(n)) % n, axis=3)
    whole = jnp.take(whole, jnp.arange(2) ^ y, axis=1)
    whole = jnp.take(whole, jnp.arange(2) ^ c, axis=2)
    whole = whole.transpose(0, 3, 1, 2, 4, 5).reshape(2, n * 4 * rows, cols)
    return [(whole, None, None, None, None)]


def load_weights(metas, refs, dest, sems, n_z, cols=None):
    z, y, c, _ = place()
    copies = []
    for (m, b, e, j0), ref in zip(metas, refs):
        if m is None:
            src = ref if cols is None else ref.at[:, :, pl.ds(*cols)]
            copies.append(pltpu.make_async_copy(src, dest, sems.at[len(copies)]))
            continue
        rows = dest.shape[1] // (4 * n_z)
        for k in range(ref.shape[0] // rows):
            dp = (lax.rem(z - (j0 + k) + n_z, n_z) * 2 + (y ^ b)) * 2 + (c ^ e)
            src = ref.at[pl.ds(k * rows, rows), :] if cols is None else ref.at[pl.ds(k * rows, rows), pl.ds(*cols)]
            start = pl.multiple_of(dp * rows, 16)
            copies.append(pltpu.make_async_copy(src, dest.at[m, pl.ds(start, rows), :], sems.at[len(copies)]))
    return copies


def n_copies(pieces, n_z):
    return 1 if pieces[0][1] is None else 8 * n_z


def rms(values, gain):
    return values * lax.rsqrt(jnp.mean(values * values, axis=-1, keepdims=True) + EPS) * gain


def rms_back(values, gain, back):
    scale = lax.rsqrt(jnp.mean(values * values, axis=-1, keepdims=True) + EPS)
    unit = values * scale
    incoming = back * gain
    grad = scale * (incoming - unit * jnp.mean(incoming * unit, axis=-1, keepdims=True))
    return grad, jnp.sum(back * unit, axis=0, keepdims=True)


def lane_masks():
    lane = lax.broadcasted_iota(jnp.int32, (1, LANE), 1)
    low = (lane < DH).astype(F32)
    return [low.astype(BF16), (1.0 - low).astype(BF16)]


def bias_strip(base, width, first):
    return pltpu.roll(jnp.broadcast_to(base, (QB, width)), 0, 1, stride=1, stride_axis=0)


def attend_loop(q_ref, k_ref, v_ref, o_ref, base_ref):
    pairs = q_ref.shape[2] // LANE
    masks = lane_masks()

    def step(t, carry):
        a = t // pairs
        p = lax.rem(t, pairs)
        at = pl.ds(pl.multiple_of(p * LANE, LANE), LANE)
        q, k, v = q_ref[a, :, at], k_ref[a, :, at], v_ref[a, :, at]
        outs = [None] * (L // QB)
        for hh in range(2):
            km, vm = k * masks[hh], v * masks[hh]
            if base_ref is not None:
                base = base_ref[pl.ds(a * 8 + p * 2 + hh, 1), :]
                strip = bias_strip(base, L, 0)
                row = lax.broadcasted_iota(jnp.int32, (QB, L), 0)
                col = lax.broadcasted_iota(jnp.int32, (QB, L), 1)
                strip = jnp.where(row + (L - QB) >= col, strip, NEG)
            for b in range(L // QB):
                n = (b + 1) * QB if base_ref is not None else k.shape[0]
                s = nt(q[b * QB : (b + 1) * QB], km[:n])
                if base_ref is not None:
                    s = s + strip[:, L - n :]
                e = jnp.exp(s - jnp.max(s, axis=-1, keepdims=True))
                mixed = nn(e.astype(BF16), vm[:n]) * (1.0 / jnp.sum(e, axis=-1, keepdims=True))
                outs[b] = mixed if hh == 0 else outs[b] + mixed
        o_ref[a, :, at] = jnp.concatenate(outs, axis=0).astype(BF16)
        return carry

    lax.fori_loop(0, 2 * pairs, step, 0)


def attend_back_loop(q_ref, k_ref, v_ref, do_ref, dq_ref, dk_ref, dv_ref, base_ref, off_ref):
    pairs = q_ref.shape[2] // LANE
    masks = lane_masks()
    causal = base_ref is not None
    wide = 256

    def step(t, carry):
        a = t // pairs
        p = lax.rem(t, pairs)
        at = pl.ds(pl.multiple_of(p * LANE, LANE), LANE)
        q, k, v, do = q_ref[a, :, at], k_ref[a, :, at], v_ref[a, :, at], do_ref[a, :, at]
        kt = k.T
        dq = [None] * (L // wide)
        dk = dv = None
        for hh in range(2):
            km, vm, qm, dom = k * masks[hh], v * masks[hh], q * masks[hh], do * masks[hh]
            ktm = jnp.concatenate([kt[:DH], jnp.zeros_like(kt[DH:])] if hh == 0 else [jnp.zeros_like(kt[:DH]), kt[DH:]], axis=0)
            band = None
            if causal:
                base = base_ref[pl.ds(a * 8 + p * 2 + hh, 1), :]
                strip = bias_strip(base, L, 0)
                row = lax.broadcasted_iota(jnp.int32, (QB, L), 0)
                col = lax.broadcasted_iota(jnp.int32, (QB, L), 1)
                strip = jnp.where(col >= row, strip, NEG)
            for b in range(L // wide):
                n = (b + 1) * wide if causal else k.shape[0]
                cols = slice(b * wide, (b + 1) * wide)
                s = nt(km[:n], q[cols])
                if causal:
                    parts = []
                    for kb in range(n // QB):
                        lo = b * wide - kb * QB
                        if lo >= 0:
                            parts.append(strip[:, lo : lo + wide])
                        else:
                            parts.append(jnp.concatenate([jnp.full((QB, -lo), NEG, F32), strip[:, : wide + lo]], axis=1))
                    s = s + jnp.concatenate(parts, axis=0)
                e = jnp.exp(s - jnp.max(s, axis=0, keepdims=True))
                prob = e * (1.0 / jnp.sum(e, axis=0, keepdims=True))
                dvb = nn(prob.astype(BF16), dom[cols])
                dp = nt(vm[:n], do[cols])
                ds = prob * (dp - jnp.sum(prob * dp, axis=0, keepdims=True))
                low = ds.astype(BF16)
                dkb = nn(low, qm[cols])
                dqb = nn(ktm[:, :n], low)
                dq[b] = dqb if hh == 0 else dq[b] + dqb
                if n < k.shape[0]:
                    pad = jnp.zeros((k.shape[0] - n, LANE), F32)
                    dvb, dkb = jnp.concatenate([dvb, pad], axis=0), jnp.concatenate([dkb, pad], axis=0)
                dk = dkb if dk is None else dk + dkb
                dv = dvb if dv is None else dv + dvb
                if causal:
                    for kb in range(n // QB):
                        lo = b * wide - kb * QB
                        part = ds[kb * QB : (kb + 1) * QB]
                        if lo < 0:
                            part, lo = part[:, -lo:], 0
                        pieces = []
                        if lo:
                            pieces.append(jnp.zeros((QB, lo), F32))
                        pieces.append(part)
                        if lo + part.shape[1] < L:
                            pieces.append(jnp.zeros((QB, L - lo - part.shape[1]), F32))
                        part = jnp.concatenate(pieces, axis=1) if len(pieces) > 1 else part
                        band = part if band is None else band + part
            if causal:
                row = lax.broadcasted_iota(jnp.int32, (QB, L), 0)
                for bit in range(QB.bit_length() - 1):
                    moved = pltpu.roll(band, L - (1 << bit), 1)
                    band = jnp.where(((row >> bit) & 1) == 1, moved, band)
                off_ref[pl.ds(a * 8 + p * 2 + hh, 1), :] = jnp.sum(band, axis=0, keepdims=True)
        dq_ref[a, :, at] = jnp.concatenate(dq, axis=1).T.astype(BF16)
        dk_ref[a, :, at] = dk.astype(BF16)
        dv_ref[a, :, at] = dv.astype(BF16)
        return carry

    lax.fori_loop(0, 2 * pairs, step, 0)


def call(body, outs, args, scratch, name, flops):
    return pl.pallas_call(
        body,
        out_shape=tuple(jax.ShapeDtypeStruct(s, d) for s, d in outs),
        in_specs=[pl.BlockSpec(memory_space=pl.ANY if far else pltpu.VMEM) for _, far in args],
        out_specs=tuple(pl.BlockSpec(memory_space=pltpu.VMEM) for _ in outs),
        scratch_shapes=scratch,
        compiler_params=pltpu.CompilerParams(vmem_limit_bytes=VMEM_LIMIT),
        cost_estimate=pl.CostEstimate(flops=flops, transcendentals=0, bytes_accessed=20_000_000),
        name=name,
    )(*[a for a, _ in args])


def sequence_copy(ref, dest, sem):
    m = lax.axis_index("mp")
    return pltpu.make_async_copy(ref.at[pl.ds(pl.multiple_of(m * L, L), L), :], dest, sem)


def far(pieces):
    return [(p[0], True) for p in pieces]


def metas(pieces):
    return [p[1:] for p in pieces]


def self_forward(grid, inputs, base_hot, pieces, d, hd):
    meta, npc = metas(pieces), len(pieces)

    def body(*refs):
        x_ref, hot_ref = refs[:2]
        w_refs = refs[2 : 2 + npc]
        n1_ref, q_ref, k_ref, v_ref, o_ref, gain_ref, base_ref = refs[2 + npc : 9 + npc]
        x_v, w, fwd_base, sem_x, sem_w = refs[9 + npc :]
        cx = sequence_copy(x_ref, x_v, sem_x)
        cx.start()
        copies = load_weights(meta, w_refs, w, sem_w, grid.n_z)
        for cp in copies:
            cp.start()
        cx.wait()
        x = x_v[...].astype(F32)
        for cp in copies:
            cp.wait()
        extra = w[0, :, 3 * hd : 3 * hd + LANE]
        pick = (
            lax.broadcasted_iota(jnp.int32, (16, LANE), 1) == lax.broadcasted_iota(jnp.int32, (16, LANE), 0) + NB
        ).astype(F32).astype(BF16)
        gains = nt(pick, extra)[:8]
        gain_ref[...] = gains
        for a in range(2):
            table = w[a, 0:16, 3 * hd : 3 * hd + LANE]
            both = nn(table, hot_ref[...])[:8]
            fwd_base[a * 8 : a * 8 + 8, :] = both[:, :L]
            base_ref[a * 8 : a * 8 + 8, :] = both[:, L:]
        n1 = rms(x, gains[0:1]).astype(BF16)
        n1_ref[...] = n1
        for a in range(2):
            q_ref[a] = nn(n1, w[a, :, 0:hd]).astype(BF16)
            k_ref[a] = nn(n1, w[a, :, hd : 2 * hd]).astype(BF16)
            v_ref[a] = nn(n1, w[a, :, 2 * hd : 3 * hd]).astype(BF16)
        attend_loop(q_ref, k_ref, v_ref, o_ref, fwd_base)

    heads = ((2, L, hd), BF16)
    return call(
        body,
        [((L, d), BF16), heads, heads, heads, heads, ((8, d), F32), ((16, L), F32)],
        [(inputs, True), (base_hot, False)] + far(pieces),
        [
            pltpu.VMEM((L, d), BF16),
            pltpu.VMEM((2, d, 3 * hd + LANE), BF16),
            pltpu.VMEM((16, L), F32),
            pltpu.SemaphoreType.DMA,
            pltpu.SemaphoreType.DMA((n_copies(pieces, grid.n_z),)),
        ],
        "self_forward",
        3_000_000_000,
    )


def cross_forward(grid, inputs, encoded, attn_one, gains, pieces, d, hd):
    meta, npc = metas(pieces), len(pieces)

    def body(*refs):
        x_ref, enc_ref, a1_ref, gain_ref = refs[:4]
        w_refs = refs[4 : 4 + npc]
        r1_ref, r2_ref, n2_ref, q_ref, k_ref, v_ref, o_ref, n3_ref = refs[4 + npc : 12 + npc]
        x_v, enc_v, w, sem_x, sem_e, sem_w = refs[12 + npc :]
        cx = sequence_copy(x_ref, x_v, sem_x)
        ce = sequence_copy(enc_ref, enc_v, sem_e)
        cx.start()
        ce.start()
        copies = load_weights(meta, w_refs, w, sem_w, grid.n_z)
        for cp in copies:
            cp.start()
        cx.wait()
        ce.wait()
        for cp in copies:
            cp.wait()
        r1 = x_v[...].astype(F32)
        for a in range(2):
            r1 = r1 + nt(a1_ref[a], w[a, :, 0:hd])
        r1_ref[...] = r1
        n2 = rms(r1, gain_ref[1:2, :]).astype(BF16)
        n2_ref[...] = n2
        enc = enc_v[...]
        for a in range(2):
            q_ref[a] = nn(n2, w[a, :, hd : 2 * hd]).astype(BF16)
            k_ref[a] = nn(enc, w[a, :, 2 * hd : 3 * hd]).astype(BF16)
            v_ref[a] = nn(enc, w[a, :, 3 * hd : 4 * hd]).astype(BF16)
        attend_loop(q_ref, k_ref, v_ref, o_ref, None)
        r2 = r1_ref[...]
        for a in range(2):
            r2 = r2 + nt(o_ref[a], w[a, :, 4 * hd : 5 * hd])
        r2_ref[...] = r2
        n3_ref[...] = rms(r2, gain_ref[2:3, :]).astype(BF16)

    heads = ((2, L, hd), BF16)
    row = ((L, d), BF16)
    return call(
        body,
        [((L, d), F32), ((L, d), F32), row, heads, heads, heads, heads, row],
        [(inputs, True), (encoded, True), (attn_one, False), (gains, False)] + far(pieces),
        [
            pltpu.VMEM((L, d), BF16),
            pltpu.VMEM((L, d), BF16),
            pltpu.VMEM((2, d, 5 * hd), BF16),
            pltpu.SemaphoreType.DMA,
            pltpu.SemaphoreType.DMA,
            pltpu.SemaphoreType.DMA((n_copies(pieces, grid.n_z),)),
        ],
        "cross_forward",
        5_000_000_000,
    )


def feed_forward(grid, cotangent, n3, r2, gains, pieces, d, ff):
    meta, npc = metas(pieces), len(pieces)
    tile = min(512, ff)

    def body(*refs):
        cot_ref, n3_ref, r2_ref, gain_ref = refs[:4]
        w_refs = refs[4 : 4 + npc]
        y_ref, b2_ref, g_ref, dg_ref = refs[4 + npc : 8 + npc]
        cot_v, w, cot_t, n3_t, y_acc, b3_acc, sem_c, sem_w = refs[8 + npc :]
        cc = sequence_copy(cot_ref, cot_v, sem_c)
        cc.start()
        copies = load_weights(meta, w_refs, w, sem_w, grid.n_z)
        for cp in copies:
            cp.start()
        cc.wait()
        cot_t[...] = cot_v[...].T
        n3_t[...] = n3_ref[...].T
        y_acc[...] = r2_ref[...]
        b3_acc[...] = jnp.zeros_like(b3_acc)
        for cp in copies:
            cp.wait()
        per = ff // tile

        def step(t, carry):
            a = t // per
            j = lax.rem(t, per) * tile
            gate_at = pl.ds(pl.multiple_of(j, LANE), tile)
            up_at = pl.ds(pl.multiple_of(ff + j, LANE), tile)
            down_at = pl.ds(pl.multiple_of(2 * ff + j, LANE), tile)
            u = nn(n3_ref[...], w[a, :, gate_at])
            up = nn(n3_ref[...], w[a, :, up_at])
            bh = nn(cot_v[...], w[a, :, down_at])
            sq = u * u
            th = jnp.tanh(GELU_C * (u + GELU_A * (sq * u)))
            half = 0.5 * (1.0 + th)
            gelu = u * half
            slope = half + 0.5 * u * (1.0 - th * th) * (GELU_C * (1.0 + (3.0 * GELU_A) * sq))
            hidden = (gelu * up).astype(BF16)
            gate_low = (bh * up * slope).astype(BF16)
            up_low = (bh * gelu).astype(BF16)
            y_acc[...] += nt(hidden, w[a, :, down_at])
            b3_acc[...] += nt(gate_low, w[a, :, gate_at]) + nt(up_low, w[a, :, up_at])
            g_ref[a, :, gate_at] = nn(n3_t[...], gate_low).astype(BF16)
            g_ref[a, :, up_at] = nn(n3_t[...], up_low).astype(BF16)
            g_ref[a, :, down_at] = nn(cot_t[...], hidden).astype(BF16)
            return carry

        lax.fori_loop(0, 2 * per, step, 0)
        y_ref[...] = y_acc[...].astype(BF16)
        grad, dg = rms_back(r2_ref[...], gain_ref[2:3, :], b3_acc[...])
        b2_ref[...] = cot_v[...].astype(F32) + grad
        dg_ref[...] = dg

    return call(
        body,
        [((L, d), BF16), ((L, d), F32), ((2, d, 3 * ff), BF16), ((1, d), F32)],
        [(cotangent, True), (n3, False), (r2, False), (gains, False)] + far(pieces),
        [
            pltpu.VMEM((L, d), BF16),
            pltpu.VMEM((2, d, 3 * ff), BF16),
            pltpu.VMEM((d, L), BF16),
            pltpu.VMEM((d, L), BF16),
            pltpu.VMEM((L, d), F32),
            pltpu.VMEM((L, d), F32),
            pltpu.SemaphoreType.DMA,
            pltpu.SemaphoreType.DMA((n_copies(pieces, grid.n_z),)),
        ],
        "feed_forward",
        15_000_000_000,
    )


def cross_backward(grid, encoded, b2, r1, n2, q, k, v, attn, gains, pieces, d, hd):
    meta, npc = metas(pieces), len(pieces)

    def body(*refs):
        enc_ref, b2_ref, r1_ref, n2_ref, q_ref, k_ref, v_ref, at_ref, gain_ref = refs[:9]
        w_refs = refs[9 : 9 + npc]
        b1_ref, eg_ref, g_ref, dg_ref = refs[9 + npc : 13 + npc]
        enc_v, w, do, dq, dk, dv, sem_e, sem_w = refs[13 + npc :]
        ce = sequence_copy(enc_ref, enc_v, sem_e)
        ce.start()
        copies = load_weights(meta, w_refs, w, sem_w, grid.n_z, (hd, 4 * hd))
        for cp in copies:
            cp.start()
        ce.wait()
        for cp in copies:
            cp.wait()
        low = b2_ref[...].astype(BF16)
        for a in range(2):
            do[a] = nn(low, w[a, :, 3 * hd : 4 * hd]).astype(BF16)
        attend_back_loop(q_ref, k_ref, v_ref, do, dq, dk, dv, None, None)
        eg = jnp.zeros((L, d), F32)
        back = jnp.zeros((L, d), F32)
        for a in range(2):
            back = back + nt(dq[a], w[a, :, 0:hd])
            eg = eg + nt(dk[a], w[a, :, hd : 2 * hd]) + nt(dv[a], w[a, :, 2 * hd : 3 * hd])
        eg_ref[...] = eg.astype(BF16)
        grad, dg = rms_back(r1_ref[...], gain_ref[1:2, :], back)
        dg_ref[...] = dg
        b1_ref[...] = b2_ref[...] + grad
        n2_t = n2_ref[...].T
        for a in range(2):
            g_ref[a, :, 0:hd] = nn(n2_t, dq[a]).astype(BF16)
        enc_t = enc_v[...].T
        for a in range(2):
            g_ref[a, :, hd : 2 * hd] = nn(enc_t, dk[a]).astype(BF16)
            g_ref[a, :, 2 * hd : 3 * hd] = nn(enc_t, dv[a]).astype(BF16)
        low_t = b2_ref[...].astype(BF16).T
        for a in range(2):
            g_ref[a, :, 3 * hd : 4 * hd] = nn(low_t, at_ref[a]).astype(BF16)

    heads = pltpu.VMEM((2, L, hd), BF16)
    return call(
        body,
        [((L, d), F32), ((L, d), BF16), ((2, d, 4 * hd), BF16), ((1, d), F32)],
        [(encoded, True)] + [(t, False) for t in (b2, r1, n2, q, k, v, attn, gains)] + far(pieces),
        [
            pltpu.VMEM((L, d), BF16),
            pltpu.VMEM((2, d, 4 * hd), BF16),
            heads,
            heads,
            heads,
            heads,
            pltpu.SemaphoreType.DMA,
            pltpu.SemaphoreType.DMA((n_copies(pieces, grid.n_z),)),
        ],
        "cross_backward",
        8_000_000_000,
    )


def self_backward(grid, inputs, b1, n1, q, k, v, attn, gains, base, pieces, out_pieces, d, hd):
    meta, npc = metas(pieces), len(pieces)
    out_meta = metas(out_pieces)

    def body(*refs):
        x_ref, b1_ref, n1_ref, q_ref, k_ref, v_ref, at_ref, gain_ref, base_ref = refs[:9]
        w_refs = refs[9 : 9 + npc]
        wo_refs = refs[9 + npc : 9 + 2 * npc]
        dx_ref, g_ref, dg_ref, off_ref = refs[9 + 2 * npc : 13 + 2 * npc]
        x_v, w, wo, do, dq, dk, dv, sem_x, sem_w, sem_o = refs[13 + 2 * npc :]
        cx = sequence_copy(x_ref, x_v, sem_x)
        cx.start()
        out_copies = load_weights(out_meta, wo_refs, wo, sem_o, grid.n_z, (0, hd))
        copies = load_weights(meta, w_refs, w, sem_w, grid.n_z, (0, 3 * hd))
        for cp in out_copies + copies:
            cp.start()
        off_ref[...] = jnp.zeros_like(off_ref)
        low = b1_ref[...].astype(BF16)
        for cp in out_copies:
            cp.wait()
        for a in range(2):
            do[a] = nn(low, wo[a]).astype(BF16)
        attend_back_loop(q_ref, k_ref, v_ref, do, dq, dk, dv, base_ref, off_ref)
        cx.wait()
        for cp in copies:
            cp.wait()
        n1_t = n1_ref[...].T
        for a in range(2):
            g_ref[a, :, 0:hd] = nn(n1_t, dq[a]).astype(BF16)
            g_ref[a, :, hd : 2 * hd] = nn(n1_t, dk[a]).astype(BF16)
            g_ref[a, :, 2 * hd : 3 * hd] = nn(n1_t, dv[a]).astype(BF16)
        low_t = b1_ref[...].astype(BF16).T
        for a in range(2):
            g_ref[a, :, 3 * hd : 4 * hd] = nn(low_t, at_ref[a]).astype(BF16)
        back = jnp.zeros((L, d), F32)
        for a in range(2):
            back = back + nt(dq[a], w[a, :, 0:hd]) + nt(dk[a], w[a, :, hd : 2 * hd]) + nt(dv[a], w[a, :, 2 * hd : 3 * hd])
        grad, dg = rms_back(x_v[...].astype(F32), gain_ref[0:1, :], back)
        dg_ref[...] = dg
        dx_ref[...] = (b1_ref[...] + grad).astype(BF16)

    heads = pltpu.VMEM((2, L, hd), BF16)
    count = n_copies(pieces, grid.n_z)
    return call(
        body,
        [((L, d), BF16), ((2, d, 4 * hd), BF16), ((1, d), F32), ((16, L), F32)],
        [(inputs, True)] + [(t, False) for t in (b1, n1, q, k, v, attn, gains, base)] + far(pieces) + far(out_pieces),
        [
            pltpu.VMEM((L, d), BF16),
            pltpu.VMEM((2, d, 3 * hd), BF16),
            pltpu.VMEM((2, d, hd), BF16),
            heads,
            heads,
            heads,
            heads,
            pltpu.SemaphoreType.DMA,
            pltpu.SemaphoreType.DMA((count,)),
            pltpu.SemaphoreType.DMA((count,)),
        ],
        "self_backward",
        8_000_000_000,
    )


def added(left, right):
    return (left.astype(F32) + right.astype(F32)).astype(BF16)


def pick(v, index, axis):
    return lax.dynamic_index_in_dim(v, index, axis, keepdims=False)


def scatter(grid, total):
    z, y, c, _ = place()
    n = grid.n_z
    cols = total.shape[2]
    rows = total.shape[1] // (4 * n)
    v = total.reshape(2, n, 2, 2, rows, cols)
    got = grid.swap_c(pick(v, 1 - c, 3))
    t = added(pick(v, c, 3), got)
    h = (cols // 2) // LANE * LANE
    ta, tb = t[..., :h], t[..., h:]
    got_a = grid.swap_m(ta[1])
    got_b = grid.swap_y(pick(tb, 1 - y, 2))
    ua = added(ta[0], got_a)
    ub = added(pick(tb, y, 2), got_b)
    got_a = grid.swap_y(pick(ua, 1 - y, 1))
    got_b = grid.swap_m(ub[1])
    wa = added(pick(ua, y, 1), got_a)
    wb = added(ub[0], got_b)
    w = jnp.concatenate([wa, wb], axis=2)
    out = pick(w, z, 0).astype(F32)
    for d in range(1, n):
        out = out + grid.shift_z(pick(w, (z + d) % n, 0), d).astype(F32)
    return out


def total_of(grid, v):
    v = v + grid.swap_c(v)
    v = v + grid.swap_m(v)
    v = v + grid.swap_y(v)
    return v + sum(grid.shift_z(v, d) for d in range(1, grid.n_z))


def both_sequences(grid, mine):
    other = grid.swap_m(mine)
    first = lax.axis_index("mp") == 0
    low = jnp.where(first, mine, other)
    high = jnp.where(first, other, mine)
    return jnp.concatenate([low, high], axis=0).astype(F32)


def make(grid):
    def per_device(
        inputs,
        encoded,
        cotangent,
        buckets,
        rel_table,
        query_self,
        keys_self,
        values_self,
        output_self,
        query_cross,
        keys_cross,
        values_cross,
        output_cross,
        gate_weight,
        up_weight,
        down_weight,
        gain_first,
        gain_second,
        gain_third,
    ):
        d = inputs.shape[1]
        hd = query_self.shape[1]
        ff = gate_weight.shape[1]
        rows = query_self.shape[0]
        heads = rel_table.shape[0]
        assert inputs.shape[0] == 2 * L and heads <= min(rows, 8)
        extra = jnp.concatenate(
            [
                jnp.pad(rel_table, ((0, rows - heads), (0, 0))),
                gain_first[:, None],
                gain_second[:, None],
                gain_third[:, None],
                jnp.zeros((rows, LANE - NB - 3), BF16),
            ],
            axis=1,
        )
        group_one = jnp.concatenate([query_self, keys_self, values_self, extra], axis=1)
        group_two = jnp.concatenate([output_self.T, query_cross, keys_cross, values_cross, output_cross.T], axis=1)
        group_three = jnp.concatenate([gate_weight, up_weight, down_weight.T], axis=1)
        pieces_one = gather(grid, group_one)
        pieces_two = gather(grid, group_two)
        pieces_three = gather(grid, group_three)

        turned = jnp.roll(buckets[::-1], L - QB + 1)
        both = jnp.concatenate([turned, buckets])
        base_hot = (both[None, :] == lax.broadcasted_iota(jnp.int32, (LANE, 2 * L), 0)).astype(BF16)

        n1, q1, k1, v1, at1, gains, base = self_forward(grid, inputs, base_hot, pieces_one, d, hd)
        r1, r2, n2, q2, k2, v2, at2, n3 = cross_forward(grid, inputs, encoded, at1, gains, pieces_two, d, hd)
        y, b2, g3, dg3 = feed_forward(grid, cotangent, n3, r2, gains, pieces_three, d, ff)
        layer_output = both_sequences(grid, y)
        s3 = scatter(grid, g3)
        b1, eg, g2, dg2 = cross_backward(grid, encoded, b2, r1, n2, q2, k2, v2, at2, gains, pieces_two, d, hd)
        encoded_gradient = both_sequences(grid, eg)
        s2 = scatter(grid, g2)
        dx, g1, dg1, off = self_backward(
            grid, inputs, b1, n1, q1, k1, v1, at1, gains, base, pieces_one, pieces_two, d, hd
        )
        s1 = scatter(grid, g1)
        input_gradient = both_sequences(grid, dx)

        m = lax.axis_index("mp")
        off = off.reshape(2, 8, L)
        off = jnp.where(m == 0, off, off[::-1])
        small = jnp.concatenate([dg1.reshape(-1), dg2.reshape(-1), dg3.reshape(-1), off.reshape(-1)]).reshape(-1, LANE)
        small = total_of(grid, small).reshape(-1)
        dp = lax.axis_index("dp")
        dgs = [lax.dynamic_slice(small, (i * d + dp * rows,), (rows,)) for i in range(3)]
        off = lax.dynamic_slice(small, (3 * d + m * 8 * L,), (8 * L,)).reshape(8, L)[:heads]
        hot = (buckets[:, None] == lax.broadcasted_iota(jnp.int32, (L, NB), 1)).astype(F32)
        table_gradient = jnp.dot(off, hot, precision=lax.Precision.HIGHEST)
        return (
            layer_output,
            input_gradient,
            encoded_gradient,
            table_gradient,
            s1[:, :hd],
            s1[:, hd : 2 * hd],
            s1[:, 2 * hd : 3 * hd],
            s1[:, 3 * hd :].T,
            s2[:, :hd],
            s2[:, hd : 2 * hd],
            s2[:, 2 * hd : 3 * hd],
            s2[:, 3 * hd :].T,
            s3[:, :ff],
            s3[:, ff : 2 * ff],
            s3[:, 2 * ff :].T,
            dgs[0],
            dgs[1],
            dgs[2],
        )

    return per_device


def solution(mesh):
    weight, turned, row, gain = P("dp", "mp"), P("mp", "dp"), P("dp", None), P("dp")
    weights = (weight, weight, weight, turned, weight, weight, weight, turned, weight, weight, turned)
    gains = (gain, gain, gain)
    return jax.shard_map(
        make(Grid(mesh.shape["dp"], mesh.shape["mp"])),
        mesh=mesh,
        in_specs=(row, row, row, P(), P("mp", None)) + weights + gains,
        out_specs=(row, row, row, P("mp", None)) + weights + gains,
        check_vma=False,
    )
```

```python
import jax
import jax.numpy as jnp
from jax import lax
from jax.experimental import pallas as pl
from jax.experimental.pallas import tpu as pltpu
from jax.sharding import PartitionSpec as P


DH = 64
NB = 32
L = 512
LANE = 128
QB = 128
EPS = 1e-06
NEG = -1e30
GELU_C = 0.7978845608028654
GELU_A = 0.044715
AXES = ("dp", "mp")
F32 = jnp.float32
BF16 = jnp.bfloat16
VMEM_LIMIT = 58 * 1024 * 1024


def nn(left, right):
    return lax.dot_general(left, right, (((1,), (0,)), ((), ())), preferred_element_type=F32)


def nt(left, right):
    return lax.dot_general(left, right, (((1,), (1,)), ((), ())), preferred_element_type=F32)


class Grid:
    def __init__(self, n_dp, n_mp):
        assert n_mp == 2 and n_dp % 8 == 0
        self.n_dp, self.n_mp = n_dp, n_mp
        self.n_z = n_dp // 4

    def perm(self, move):
        pairs = []
        for z in range(self.n_z):
            for y in range(2):
                for c in range(2):
                    for m in range(2):
                        tz, ty, tc, tm = move(z, y, c, m)
                        pairs.append(
                            (
                                (((z * 2 + y) * 2) + c) * 2 + m,
                                (((tz * 2 + ty) * 2) + tc) * 2 + tm,
                            )
                        )
        return pairs

    def send(self, v, move):
        return lax.ppermute(v, AXES, self.perm(move))

    def swap_m(self, v):
        return self.send(v, lambda z, y, c, m: (z, y, c, 1 - m))

    def swap_y(self, v):
        return self.send(v, lambda z, y, c, m: (z, 1 - y, c, m))

    def swap_c(self, v):
        return self.send(v, lambda z, y, c, m: (z, y, 1 - c, m))

    def shift_z(self, v, d):
        n = self.n_z
        return self.send(v, lambda z, y, c, m: ((z + d) % n, y, c, m))


def place():
    dp = lax.axis_index("dp")
    return dp // 4, (dp // 2) % 2, dp % 2, lax.axis_index("mp")


def gather(grid, block):
    rows, cols = block.shape
    n = grid.n_z
    z, y, c, _ = place()
    got = [block] + [grid.shift_z(block, d) for d in range(1, n)]
    own = jnp.zeros((n, rows, cols), block.dtype)
    for d in range(n):
        own = lax.dynamic_update_slice(own, got[d][None], (lax.rem(z - d + n, n), 0, 0))
    half = n // 2
    by_m = grid.swap_m(own)
    by_y = grid.swap_y(own)
    part_a = by_m[:half]
    part_b = by_y[half:]
    diag_a = grid.swap_y(part_a)
    diag_b = grid.swap_m(part_b)
    pieces = [(own, 0, 0, 0), (by_y, 0, 1, 0), (by_m, 1, 0, 0), (diag_a, 1, 1, 0), (diag_b, 1, 1, half)]
    out = [(a, m, b, 0, j) for a, m, b, j in pieces]
    out += [(grid.swap_c(p[0]),) + p[1:3] + (1, p[3]) for p in pieces]
    if rows % 16 == 0:
        return out
    stacks = []
    for m in range(2):
        for b in range(2):
            for e in range(2):
                mine = sorted((p for p in out if p[1:4] == (m, b, e)), key=lambda p: p[4])
                stacks.append(jnp.concatenate([p[0] for p in mine], axis=0))
    whole = jnp.stack(stacks).reshape(2, 2, 2, n, rows, cols)
    whole = jnp.take(whole, jnp.arange(2) ^ y, axis=1)
    whole = jnp.take(whole, jnp.arange(2) ^ c, axis=2)
    whole = whole.transpose(0, 3, 1, 2, 4, 5).reshape(2, n * 4 * rows, cols)
    return [(whole[m], m, None, None, 0) for m in range(2)]


class Weights:
    def __init__(self, pieces, n_z, half=None):
        chosen = [p for p in pieces if half is None or p[1] == half]
        self.arrays = [p[0] for p in chosen]
        self.metas = [p[1:] for p in chosen]
        self.packed = self.metas[0][1] is None
        self.n_z = n_z
        self.rows = pieces[0][0].shape[1] if not self.packed else pieces[0][0].shape[0] // (4 * n_z)
        self.half = half

    def specs(self):
        return [(a, True) for a in self.arrays]

    def scratch(self, n):
        if self.packed:
            return pltpu.VMEM((4 * self.n_z * self.rows, n), BF16)
        return pltpu.VMEM((self.n_z, 2, 2, self.rows, n), BF16)

    def sems(self):
        return pltpu.SemaphoreType.DMA((len(self.arrays),))

    def start(self, refs, dest, sems, src, n, at=0):
        _, y, c, _ = place()
        copies = []
        for i, ((m, b, e, j), ref) in enumerate(zip(self.metas, refs)):
            to = pl.ds(at + (0 if self.half is not None else m * n), n)
            if self.packed:
                cp = pltpu.make_async_copy(ref.at[:, pl.ds(src, n)], dest.at[:, to], sems.at[i])
            else:
                k = ref.shape[0]
                cp = pltpu.make_async_copy(
                    ref.at[:, :, pl.ds(src, n)], dest.at[pl.ds(j, k), y ^ b, c ^ e, :, to], sems.at[i]
                )
            cp.start()
            copies.append(cp)
        return copies

    def value(self, dest, first, last):
        if self.packed:
            return dest[:, first:last]
        return dest[:, :, :, :, first:last].reshape(4 * self.n_z * self.rows, last - first)

    def columns(self, dest, first, size):
        if self.packed:
            return dest[:, pl.ds(first, size)]
        return dest[:, :, :, :, pl.ds(first, size)].reshape(4 * self.n_z * self.rows, size)


def wait(copies):
    for cp in copies:
        cp.wait()


def rms(values, gain):
    return values * lax.rsqrt(jnp.mean(values * values, axis=-1, keepdims=True) + EPS) * gain


def rms_back(values, gain, back):
    scale = lax.rsqrt(jnp.mean(values * values, axis=-1, keepdims=True) + EPS)
    unit = values * scale
    incoming = back * gain
    grad = scale * (incoming - unit * jnp.mean(incoming * unit, axis=-1, keepdims=True))
    return grad, jnp.sum(back * unit, axis=0, keepdims=True)


def lane_masks():
    lane = lax.broadcasted_iota(jnp.int32, (1, LANE), 1)
    low = (lane < DH).astype(F32)
    return [low.astype(BF16), (1.0 - low).astype(BF16)]


def bias_strip(base):
    first = pltpu.roll(jnp.broadcast_to(base, (8, L)), 0, 1, stride=1, stride_axis=0)
    return jnp.concatenate([first] + [pltpu.roll(first, 8 * g, 1) for g in range(1, QB // 8)], axis=0)


def fold_band(band):
    total = band[0:8]
    for g in range(1, QB // 8):
        total = total + pltpu.roll(band[8 * g : 8 * g + 8], L - 8 * g, 1)
    row = lax.broadcasted_iota(jnp.int32, (8, L), 0)
    for bit in range(3):
        total = jnp.where(((row >> bit) & 1) == 1, pltpu.roll(total, L - (1 << bit), 1), total)
    return jnp.sum(total, axis=0, keepdims=True)


def attend_loop(q_ref, k_ref, v_ref, o_ref, base_ref):
    masks = lane_masks()

    def step(t, carry):
        at = pl.ds(pl.multiple_of(t * LANE, LANE), LANE)
        q, k, v = q_ref[:, at], k_ref[:, at], v_ref[:, at]
        outs = [None] * (L // QB)
        for hh in range(2):
            km, vm = k * masks[hh], v * masks[hh]
            if base_ref is not None:
                strip = bias_strip(base_ref[pl.ds(t * 2 + hh, 1), :])
                row = lax.broadcasted_iota(jnp.int32, (QB, L), 0)
                col = lax.broadcasted_iota(jnp.int32, (QB, L), 1)
                strip = jnp.where(row + (L - QB) >= col, strip, NEG)
            for b in range(L // QB):
                n = (b + 1) * QB if base_ref is not None else k.shape[0]
                s = nt(q[b * QB : (b + 1) * QB], km[:n])
                if base_ref is not None:
                    s = s + strip[:, L - n :]
                e = jnp.exp(s - jnp.max(s, axis=-1, keepdims=True))
                mixed = nn(e.astype(BF16), vm[:n]) * (1.0 / jnp.sum(e, axis=-1, keepdims=True))
                outs[b] = mixed if hh == 0 else outs[b] + mixed
        o_ref[:, at] = jnp.concatenate(outs, axis=0).astype(BF16)
        return carry

    lax.fori_loop(0, q_ref.shape[1] // LANE, step, 0)


def attend_back_loop(q_ref, k_ref, v_ref, do_ref, dq_ref, dk_ref, dv_ref, base_ref, off_ref):
    masks = lane_masks()
    causal = base_ref is not None
    wide = 256

    def step(t, carry):
        at = pl.ds(pl.multiple_of(t * LANE, LANE), LANE)
        q, k, v, do = q_ref[:, at], k_ref[:, at], v_ref[:, at], do_ref[:, at]
        kt = k.T
        dq = [None] * (L // wide)
        dk = dv = None
        for hh in range(2):
            km, vm, qm, dom = k * masks[hh], v * masks[hh], q * masks[hh], do * masks[hh]
            none = jnp.zeros_like(kt[:DH])
            ktm = jnp.concatenate([kt[:DH], none] if hh == 0 else [none, kt[DH:]], axis=0)
            band = None
            if causal:
                strip = bias_strip(base_ref[pl.ds(t * 2 + hh, 1), :])
                row = lax.broadcasted_iota(jnp.int32, (QB, L), 0)
                col = lax.broadcasted_iota(jnp.int32, (QB, L), 1)
                strip = jnp.where(col >= row, strip, NEG)
            for b in range(L // wide):
                n = (b + 1) * wide if causal else k.shape[0]
                cols = slice(b * wide, (b + 1) * wide)
                s = nt(km[:n], q[cols])
                if causal:
                    parts = []
                    for kb in range(n // QB):
                        lo = b * wide - kb * QB
                        if lo >= 0:
                            parts.append(strip[:, lo : lo + wide])
                        else:
                            parts.append(
                                jnp.concatenate([jnp.full((QB, -lo), NEG, F32), strip[:, : wide + lo]], axis=1)
                            )
                    s = s + jnp.concatenate(parts, axis=0)
                e = jnp.exp(s - jnp.max(s, axis=0, keepdims=True))
                prob = e * (1.0 / jnp.sum(e, axis=0, keepdims=True))
                dvb = nn(prob.astype(BF16), dom[cols])
                dp = nt(vm[:n], do[cols])
                ds = prob * (dp - jnp.sum(prob * dp, axis=0, keepdims=True))
                low = ds.astype(BF16)
                dkb = nn(low, qm[cols])
                dqb = nn(ktm[:, :n], low)
                dq[b] = dqb if hh == 0 else dq[b] + dqb
                if n < k.shape[0]:
                    pad = jnp.zeros((k.shape[0] - n, LANE), F32)
                    dvb, dkb = jnp.concatenate([dvb, pad], axis=0), jnp.concatenate([dkb, pad], axis=0)
                dk = dkb if dk is None else dk + dkb
                dv = dvb if dv is None else dv + dvb
                if causal:
                    for kb in range(n // QB):
                        lo = b * wide - kb * QB
                        part = ds[kb * QB : (kb + 1) * QB]
                        if lo < 0:
                            part, lo = part[:, -lo:], 0
                        sides = []
                        if lo:
                            sides.append(jnp.zeros((QB, lo), F32))
                        sides.append(part)
                        if lo + part.shape[1] < L:
                            sides.append(jnp.zeros((QB, L - lo - part.shape[1]), F32))
                        part = jnp.concatenate(sides, axis=1) if len(sides) > 1 else part
                        band = part if band is None else band + part
            if causal:
                off_ref[pl.ds(t * 2 + hh, 1), :] = fold_band(band)
        dq_ref[:, at] = jnp.concatenate(dq, axis=1).T.astype(BF16)
        dk_ref[:, at] = dk.astype(BF16)
        dv_ref[:, at] = dv.astype(BF16)
        return carry

    lax.fori_loop(0, q_ref.shape[1] // LANE, step, 0)


def call(body, outs, args, scratch, flops):
    return pl.pallas_call(
        body,
        out_shape=tuple(jax.ShapeDtypeStruct(s, d) for s, d in outs),
        in_specs=[pl.BlockSpec(memory_space=pl.ANY if far else pltpu.VMEM) for _, far in args],
        out_specs=tuple(pl.BlockSpec(memory_space=pltpu.VMEM) for _ in outs),
        scratch_shapes=scratch,
        compiler_params=pltpu.CompilerParams(vmem_limit_bytes=VMEM_LIMIT),
        cost_estimate=pl.CostEstimate(flops=flops, transcendentals=0, bytes_accessed=10_000_000),
    )(*[a for a, _ in args])


def sequence_copy(ref, dest, sem):
    m = lax.axis_index("mp")
    cp = pltpu.make_async_copy(ref.at[pl.ds(pl.multiple_of(m * L, L), L), :], dest, sem)
    cp.start()
    return cp


def near(*arrays):
    return [(a, False) for a in arrays]


class Parts:
    def __init__(self, grid, d, cols, halves):
        self.n = grid.n_z
        self.rows = d // (4 * self.n)
        self.sorted = self.rows % 16 == 0
        self.d, self.cols, self.halves = d, cols, halves

    def outs(self):
        lead = (2,) if self.halves else ()
        if self.sorted:
            return [(lead + (2, self.n, self.rows, self.cols), BF16)] * 2
        return [(lead + (self.d, self.cols), BF16)]

    def count(self):
        return 2 if self.sorted else 1

    def put(self, refs, half, at, value):
        low = value.astype(BF16)
        size = low.shape[1]
        cols = pl.ds(at, size)
        if not self.sorted:
            if half is None:
                refs[0][:, cols] = low
            else:
                refs[0][half, :, cols] = low
            return
        z, y, c, _ = place()
        low = low.reshape(self.n, 2, 2, self.rows, size)
        for i in range(self.n):
            for b in range(2):
                first, second = low[i, b, 0], low[i, b, 1]
                where = (b ^ y, lax.rem(i - z + self.n, self.n), slice(None), cols)
                if half is not None:
                    where = (half,) + where
                refs[0][where] = lax.select(c == 0, first, second)
                refs[1][where] = lax.select(c == 0, second, first)

    def put_halves(self, refs, at, n, value):
        self.put(refs, 0, at, value[:, :n])
        self.put(refs, 1, at, value[:, n:])

    def split(self, arrays):
        if self.sorted:
            return arrays
        z, y, c, _ = place()
        v = arrays[0]
        v = v.reshape(v.shape[:-2] + (self.n, 2, 2, self.rows, self.cols))
        lead = v.ndim - 5
        v = jnp.moveaxis(v, (lead + 2, lead + 1, lead), (0, lead + 1, lead + 2))
        v = jnp.take(v, (z + jnp.arange(self.n)) % self.n, axis=lead + 2)
        v = jnp.take(v, jnp.arange(2) ^ y, axis=lead + 1)
        v = jnp.take(v, jnp.arange(2) ^ c, axis=0)
        return v[0], v[1]


DMA = pltpu.SemaphoreType.DMA


def self_forward(grid, inputs, base_hot, pieces, d, hd, heads):
    ws = Weights(pieces, grid.n_z)
    k = len(ws.arrays)
    w2 = 2 * hd

    def body(*refs):
        x_ref, hot_ref = refs[:2]
        w_refs = refs[2 : 2 + k]
        n1_ref, q_ref, k_ref, v_ref, o_ref, gain_ref, base_ref = refs[2 + k : 9 + k]
        x_v, we, wq, wk, wv, fwd_base, sem_x, s_e, s_q, s_k, s_v = refs[9 + k :]
        cx = sequence_copy(x_ref, x_v, sem_x)
        ce = ws.start(w_refs, we, s_e, 3 * hd, LANE)
        cq = ws.start(w_refs, wq, s_q, 0, hd)
        ck = ws.start(w_refs, wk, s_k, hd, hd)
        cv = ws.start(w_refs, wv, s_v, 2 * hd, hd)
        cx.wait()
        x = x_v[...].astype(F32)
        scaled = x * lax.rsqrt(jnp.mean(x * x, axis=-1, keepdims=True) + EPS)
        wait(ce)
        extra = ws.value(we, 0, 2 * LANE)
        rows = ws.rows
        lane = lax.broadcasted_iota(jnp.int32, (LANE, d), 0)
        column = lax.broadcasted_iota(jnp.int32, (LANE, d), 1)
        spread = (lane == lax.rem(column, rows)).astype(F32).astype(BF16)
        wide = nn(extra[:, :LANE], spread)
        row = lax.broadcasted_iota(jnp.int32, (d, d), 0)
        column = lax.broadcasted_iota(jnp.int32, (d, d), 1)
        gains = [
            jnp.sum(jnp.where(row == (column // rows) * rows + heads + i, wide, 0.0), axis=0, keepdims=True)
            for i in range(3)
        ]
        gains = jnp.concatenate(gains + [jnp.zeros((5, d), F32)], axis=0)
        gain_ref[...] = gains
        fwd_base[...] = jnp.zeros_like(fwd_base)
        base_ref[...] = jnp.zeros_like(base_ref)
        for a in range(2):
            both = nn(extra[0:16, a * LANE : (a + 1) * LANE], hot_ref[...])[:heads]
            fwd_base[a * heads : (a + 1) * heads, :] = both[:, :L]
            base_ref[a * heads : (a + 1) * heads, :] = both[:, L:]
        n1 = (scaled * gains[0:1]).astype(BF16)
        n1_ref[...] = n1
        wait(cq)
        q_ref[...] = nn(n1, ws.value(wq, 0, w2)).astype(BF16)
        wait(ck)
        k_ref[...] = nn(n1, ws.value(wk, 0, w2)).astype(BF16)
        wait(cv)
        v_ref[...] = nn(n1, ws.value(wv, 0, w2)).astype(BF16)
        attend_loop(q_ref, k_ref, v_ref, o_ref, fwd_base)

    row = ((L, w2), BF16)
    return call(
        body,
        [((L, d), BF16), row, row, row, row, ((8, d), F32), ((16, L), F32)],
        [(inputs, True), (base_hot, False)] + ws.specs(),
        [
            pltpu.VMEM((L, d), BF16),
            ws.scratch(2 * LANE),
            ws.scratch(w2),
            ws.scratch(w2),
            ws.scratch(w2),
            pltpu.VMEM((16, L), F32),
            DMA,
            ws.sems(),
            ws.sems(),
            ws.sems(),
            ws.sems(),
        ],
        3_000_000_000,
    )


def cross_forward(grid, inputs, encoded, attn_one, gains, pieces, d, hd):
    ws = Weights(pieces, grid.n_z)
    k = len(ws.arrays)
    w2 = 2 * hd

    def body(*refs):
        x_ref, enc_ref, a1_ref, gain_ref = refs[:4]
        w_refs = refs[4 : 4 + k]
        r1_ref, r2_ref, n2_ref, q_ref, k_ref, v_ref, o_ref, n3_ref = refs[4 + k : 12 + k]
        x_v, enc_v, w1, wq, wk, wv, w2v, sem_x, sem_e, s_1, s_q, s_k, s_v, s_2 = refs[12 + k :]
        ce = sequence_copy(enc_ref, enc_v, sem_e)
        ck = ws.start(w_refs, wk, s_k, 2 * hd, hd)
        cv = ws.start(w_refs, wv, s_v, 3 * hd, hd)
        cx = sequence_copy(x_ref, x_v, sem_x)
        c1 = ws.start(w_refs, w1, s_1, 0, hd)
        cq = ws.start(w_refs, wq, s_q, hd, hd)
        c2 = ws.start(w_refs, w2v, s_2, 4 * hd, hd)
        ce.wait()
        wait(ck)
        k_ref[...] = nn(enc_v[...], ws.value(wk, 0, w2)).astype(BF16)
        wait(cv)
        v_ref[...] = nn(enc_v[...], ws.value(wv, 0, w2)).astype(BF16)
        cx.wait()
        wait(c1)
        r1 = x_v[...].astype(F32) + nt(a1_ref[...], ws.value(w1, 0, w2))
        r1_ref[...] = r1
        n2 = rms(r1, gain_ref[1:2, :]).astype(BF16)
        n2_ref[...] = n2
        wait(cq)
        q_ref[...] = nn(n2, ws.value(wq, 0, w2)).astype(BF16)
        attend_loop(q_ref, k_ref, v_ref, o_ref, None)
        wait(c2)
        r2 = r1_ref[...] + nt(o_ref[...], ws.value(w2v, 0, w2))
        r2_ref[...] = r2
        n3_ref[...] = rms(r2, gain_ref[2:3, :]).astype(BF16)

    row = ((L, w2), BF16)
    wide = ((L, d), BF16)
    return call(
        body,
        [((L, d), F32), ((L, d), F32), wide, row, row, row, row, wide],
        [(inputs, True), (encoded, True)] + near(attn_one, gains) + ws.specs(),
        [pltpu.VMEM((L, d), BF16), pltpu.VMEM((L, d), BF16)]
        + [ws.scratch(w2) for _ in range(5)]
        + [DMA, DMA]
        + [ws.sems() for _ in range(5)],
        5_000_000_000,
    )


def feed_forward(grid, cotangent, n3, r2, gains, carried, pieces, half, d, ff):
    ws = Weights(pieces, grid.n_z, half)
    k = len(ws.arrays)
    tile = min(512, ff)
    last = carried is not None
    extra_in = 4 if last else 0
    parts = Parts(grid, d, 3 * ff, False)
    ng = parts.count()

    def body(*refs):
        cot_ref, n3_ref = refs[:2]
        w_refs = refs[2 + extra_in : 2 + extra_in + k]
        rest = refs[2 + extra_in + k :]
        if last:
            r2_ref, gain_ref, yin_ref, bin_ref = refs[2:6]
            y_ref, b2_ref, dg_ref, y_acc, b3_acc = rest[ng : ng + 5]
        else:
            y_acc, b3_acc = rest[ng : ng + 2]
        g_refs, rest = rest[:ng], rest[ng + (5 if last else 2) :]
        cot_v, wg, wu, wd, cot_t, n3_t, sem_c, s_g, s_u, s_d = rest
        cc = sequence_copy(cot_ref, cot_v, sem_c)
        cg = ws.start(w_refs, wg, s_g, 0, ff)
        cu = ws.start(w_refs, wu, s_u, ff, ff)
        cd = ws.start(w_refs, wd, s_d, 2 * ff, ff)
        if last:
            y_acc[...] = r2_ref[...] + yin_ref[...]
            b3_acc[...] = bin_ref[...]
        else:
            y_acc[...] = jnp.zeros_like(y_acc)
            b3_acc[...] = jnp.zeros_like(b3_acc)
        n3_t[...] = n3_ref[...].T
        cc.wait()
        cot_t[...] = cot_v[...].T
        wait(cg)
        wait(cu)
        wait(cd)

        def step(t, carry):
            at = pl.multiple_of(t * tile, LANE)
            gate, upw, down = ws.columns(wg, at, tile), ws.columns(wu, at, tile), ws.columns(wd, at, tile)
            u = nn(n3_ref[...], gate)
            up = nn(n3_ref[...], upw)
            bh = nn(cot_v[...], down)
            sq = u * u
            th = jnp.tanh(GELU_C * (u + GELU_A * (sq * u)))
            both = 0.5 * (1.0 + th)
            gelu = u * both
            slope = both + 0.5 * u * (1.0 - th * th) * (GELU_C * (1.0 + (3.0 * GELU_A) * sq))
            hidden = (gelu * up).astype(BF16)
            gate_low = (bh * up * slope).astype(BF16)
            up_low = (bh * gelu).astype(BF16)
            y_acc[...] += nt(hidden, down)
            b3_acc[...] += nt(gate_low, gate) + nt(up_low, upw)
            parts.put(g_refs, None, at, nn(n3_t[...], gate_low))
            parts.put(g_refs, None, pl.multiple_of(ff + at, LANE), nn(n3_t[...], up_low))
            parts.put(g_refs, None, pl.multiple_of(2 * ff + at, LANE), nn(cot_t[...], hidden))
            return carry

        lax.fori_loop(0, ff // tile, step, 0)
        if last:
            y_ref[...] = y_acc[...].astype(BF16)
            grad, dg = rms_back(r2_ref[...], gain_ref[2:3, :], b3_acc[...])
            b2_ref[...] = cot_v[...].astype(F32) + grad
            dg_ref[...] = dg

    full = ((L, d), F32)
    outs = parts.outs()
    outs += [((L, d), BF16), full, ((1, d), F32)] if last else [full, full]
    scratch = [pltpu.VMEM((L, d), F32), pltpu.VMEM((L, d), F32)] if last else []
    result = call(
        body,
        outs,
        [(cotangent, True)] + near(n3) + (near(r2, gains, *carried) if last else []) + ws.specs(),
        scratch
        + [
            pltpu.VMEM((L, d), BF16),
            ws.scratch(ff),
            ws.scratch(ff),
            ws.scratch(ff),
            pltpu.VMEM((d, L), BF16),
            pltpu.VMEM((d, L), BF16),
            DMA,
            ws.sems(),
            ws.sems(),
            ws.sems(),
        ],
        7_500_000_000,
    )
    return parts.split(result[:ng]), result[ng:]


def attention_backward(grid, back, q, k, v, base, pieces, first_col, hd):
    ws = Weights(pieces, grid.n_z)
    n = len(ws.arrays)
    w2 = 2 * hd
    causal = base is not None

    def body(*refs):
        b_ref, q_ref, k_ref, v_ref = refs[:4]
        base_ref = refs[4] if causal else None
        refs = refs[5 if causal else 4 :]
        w_refs = refs[:n]
        dq_ref, dk_ref, dv_ref = refs[n : n + 3]
        off_ref = refs[n + 3] if causal else None
        wo, do, s_o = refs[n + (4 if causal else 3) :]
        co = ws.start(w_refs, wo, s_o, first_col, hd)
        if causal:
            off_ref[...] = jnp.zeros_like(off_ref)
        low = b_ref[...].astype(BF16)
        wait(co)
        do[...] = nn(low, ws.value(wo, 0, w2)).astype(BF16)
        attend_back_loop(q_ref, k_ref, v_ref, do, dq_ref, dk_ref, dv_ref, base_ref, off_ref)

    row = ((L, w2), BF16)
    return call(
        body,
        [row, row, row] + ([((16, L), F32)] if causal else []),
        near(back, q, k, v) + (near(base) if causal else []) + ws.specs(),
        [ws.scratch(w2), pltpu.VMEM((L, w2), BF16), ws.sems()],
        3_000_000_000,
    )


def cross_finish(grid, encoded, b2, r1, n2, dq, dk, dv, attn_one, attn_two, gains, pieces, d, hd):
    ws = Weights(pieces, grid.n_z)
    k = len(ws.arrays)
    w2 = 2 * hd
    parts = Parts(grid, d, 5 * hd, True)
    ng = parts.count()

    def body(*refs):
        enc_ref, b2_ref, r1_ref, n2_ref, dq_ref, dk_ref, dv_ref, a1_ref, a2_ref, gain_ref = refs[:10]
        w_refs = refs[10 : 10 + k]
        b1_ref, eg_ref, dg_ref = refs[10 + k : 13 + k]
        g_refs = refs[13 + k : 13 + k + ng]
        enc_v, wq, wk, wv, sem_e, s_q, s_k, s_v = refs[13 + k + ng :]
        cq = ws.start(w_refs, wq, s_q, hd, hd)
        ce = sequence_copy(enc_ref, enc_v, sem_e)
        ck = ws.start(w_refs, wk, s_k, 2 * hd, hd)
        cv = ws.start(w_refs, wv, s_v, 3 * hd, hd)
        parts.put_halves(g_refs, hd, hd, nn(n2_ref[...].T, dq_ref[...]))
        wait(cq)
        grad, dg = rms_back(r1_ref[...], gain_ref[1:2, :], nt(dq_ref[...], ws.value(wq, 0, w2)))
        dg_ref[...] = dg
        b1 = b2_ref[...] + grad
        b1_ref[...] = b1
        parts.put_halves(g_refs, 0, hd, nn(b1.astype(BF16).T, a1_ref[...]))
        ce.wait()
        enc_t = enc_v[...].T
        parts.put_halves(g_refs, 2 * hd, hd, nn(enc_t, dk_ref[...]))
        parts.put_halves(g_refs, 3 * hd, hd, nn(enc_t, dv_ref[...]))
        parts.put_halves(g_refs, 4 * hd, hd, nn(b2_ref[...].astype(BF16).T, a2_ref[...]))
        wait(ck)
        wait(cv)
        eg = nt(dk_ref[...], ws.value(wk, 0, w2)) + nt(dv_ref[...], ws.value(wv, 0, w2))
        eg_ref[...] = eg.astype(BF16)

    result = call(
        body,
        [((L, d), F32), ((L, d), BF16), ((1, d), F32)] + parts.outs(),
        [(encoded, True)] + near(b2, r1, n2, dq, dk, dv, attn_one, attn_two, gains) + ws.specs(),
        [pltpu.VMEM((L, d), BF16)]
        + [ws.scratch(w2) for _ in range(3)]
        + [DMA]
        + [ws.sems() for _ in range(3)],
        5_000_000_000,
    )
    return result[:3], parts.split(result[3:])


def self_finish(grid, inputs, b1, n1, dq, dk, dv, off, dg2, dg3, base_hot, gains, pieces, d, hd, heads):
    ws = Weights(pieces, grid.n_z)
    k = len(ws.arrays)
    w2 = 2 * hd
    parts = Parts(grid, d, 3 * hd + LANE, True)
    ng = parts.count()

    def body(*refs):
        x_ref, b1_ref, n1_ref, dq_ref, dk_ref, dv_ref, off_ref, dg2_ref, dg3_ref, hot_ref, gain_ref = refs[:11]
        w_refs = refs[11 : 11 + k]
        dx_ref = refs[11 + k]
        g_refs = refs[12 + k : 12 + k + ng]
        x_v, wq, wk, wv, sem_x, s_q, s_k, s_v = refs[12 + k + ng :]
        cq = ws.start(w_refs, wq, s_q, 0, hd)
        ck = ws.start(w_refs, wk, s_k, hd, hd)
        cv = ws.start(w_refs, wv, s_v, 2 * hd, hd)
        cx = sequence_copy(x_ref, x_v, sem_x)
        n1_t = n1_ref[...].T
        parts.put_halves(g_refs, 0, hd, nn(n1_t, dq_ref[...]))
        parts.put_halves(g_refs, hd, hd, nn(n1_t, dk_ref[...]))
        parts.put_halves(g_refs, 2 * hd, hd, nn(n1_t, dv_ref[...]))
        wait(cq)
        back = nt(dq_ref[...], ws.value(wq, 0, w2))
        wait(ck)
        back = back + nt(dk_ref[...], ws.value(wk, 0, w2))
        wait(cv)
        back = back + nt(dv_ref[...], ws.value(wv, 0, w2))
        cx.wait()
        grad, dg = rms_back(x_v[...].astype(F32), gain_ref[0:1, :], back)
        dx_ref[...] = (b1_ref[...] + grad).astype(BF16)
        dgs = jnp.concatenate([dg, dg2_ref[...], dg3_ref[...], jnp.zeros((5, d), F32)], axis=0)
        turned = jnp.concatenate([jnp.zeros((NB, d), F32), dgs, jnp.zeros((LANE - NB - 8, d), F32)], axis=0).T
        hot = hot_ref[:, L:]
        sums = off_ref[...]
        table = jnp.zeros((16, LANE), F32)
        for _ in range(3):
            low = sums.astype(BF16)
            table = table + nt(low, hot)
            sums = sums - low.astype(F32)
        table = table.astype(BF16)
        shard_row = lax.rem(lax.broadcasted_iota(jnp.int32, (d, 16), 0), parts.rows)
        column = lax.broadcasted_iota(jnp.int32, (d, 16), 1)
        for a in range(2):
            spread = ((shard_row + a * heads == column) & (shard_row < heads)).astype(F32).astype(BF16)
            parts.put(g_refs, a, 3 * hd, nn(spread, table) + turned)

    result = call(
        body,
        [((L, d), BF16)] + parts.outs(),
        [(inputs, True)] + near(b1, n1, dq, dk, dv, off, dg2, dg3, base_hot, gains) + ws.specs(),
        [pltpu.VMEM((L, d), BF16)]
        + [ws.scratch(w2) for _ in range(3)]
        + [DMA]
        + [ws.sems() for _ in range(3)],
        4_000_000_000,
    )
    return result[0], parts.split(result[1:])


def added(left, right):
    return (left.astype(F32) + right.astype(F32)).astype(BF16)


def scatter(grid, own, own_got, other, other_got, first):
    n = grid.n_z
    got = grid.swap_m(added(other[..., :first], other_got[..., :first]))
    got_own = grid.swap_y(added(own[1, ..., first:], own_got[1, ..., first:]))
    got_other = grid.swap_y(added(other[1, ..., first:], other_got[1, ..., first:]))

    def a_sum(i):
        return added3(own[i, ..., :first], own_got[i, ..., :first], got[i])

    def b_sum(v, v_got, v_far):
        return added3(v[0, ..., first:], v_got[0, ..., first:], v_far)

    far_a = grid.swap_y(a_sum(1))
    far_b = grid.swap_m(b_sum(other, other_got, got_other))
    wa, wb = a_sum(0), b_sum(own, own_got, got_own)
    w = [
        jnp.concatenate([added(wa[d], far_a[d]), added(wb[d], far_b[d])], axis=-1) for d in range(n)
    ]
    return w


def settle(grid, w, gate=None):
    sent = w[1:]
    if gate is not None:
        sent, gate = lax.optimization_barrier((sent, gate))
    return [w[0]] + [grid.shift_z(v, d + 1) for d, v in enumerate(sent)], gate


def summed(arrays):
    out = arrays[0].astype(F32)
    for v in arrays[1:]:
        out = out + v.astype(F32)
    return out


def added3(a, b, c):
    return (a.astype(F32) + b.astype(F32) + c.astype(F32)).astype(BF16)


def both_sequences(mine, other):
    first = lax.axis_index("mp") == 0
    low = jnp.where(first, mine, other)
    high = jnp.where(first, other, mine)
    return jnp.concatenate([low, high], axis=0).astype(F32)


def make(grid):
    def step(
        inputs,
        encoded,
        cotangent,
        buckets,
        rel_table,
        query_self,
        keys_self,
        values_self,
        output_self,
        query_cross,
        keys_cross,
        values_cross,
        output_cross,
        gate_weight,
        up_weight,
        down_weight,
        gain_first,
        gain_second,
        gain_third,
    ):
        d = inputs.shape[1]
        hd = query_self.shape[1]
        ff = gate_weight.shape[1]
        rows = query_self.shape[0]
        heads = rel_table.shape[0]
        assert inputs.shape[0] == 2 * L and heads + 3 <= rows <= LANE and heads <= 8
        extra = jnp.concatenate(
            [
                jnp.pad(rel_table, ((0, 0), (0, LANE - NB))),
                jnp.pad(jnp.stack([gain_first, gain_second, gain_third]), ((0, rows - heads - 3), (0, LANE - rows))),
            ],
            axis=0,
        )
        group_one = jnp.concatenate([query_self, keys_self, values_self, extra], axis=1)
        group_two = jnp.concatenate([output_self.T, query_cross, keys_cross, values_cross, output_cross.T], axis=1)
        group_three = jnp.concatenate([gate_weight, up_weight, down_weight.T], axis=1)
        pieces_one = gather(grid, group_one)
        pieces_two = gather(grid, group_two)
        pieces_three = gather(grid, group_three)

        turned = jnp.roll(buckets[::-1], L - QB + 1)
        both = jnp.concatenate([turned, buckets])
        base_hot = (both[None, :] == lax.broadcasted_iota(jnp.int32, (LANE, 2 * L), 0)).astype(BF16)

        n1, q1, k1, v1, at1, gains, base = self_forward(grid, inputs, base_hot, pieces_one, d, hd, heads)
        r1, r2, n2, q2, k2, v2, at2, n3 = cross_forward(grid, inputs, encoded, at1, gains, pieces_two, d, hd)
        (own3, gone), (ya, ba) = feed_forward(grid, cotangent, n3, r2, gains, None, pieces_three, 0, d, ff)
        own3_got = grid.swap_c(gone)
        (other3, gone), (y, b2, dg3) = feed_forward(
            grid, cotangent, n3, r2, gains, (ya, ba), pieces_three, 1, d, ff
        )
        other3_got = grid.swap_c(gone)
        y_far = grid.swap_m(y)
        w3 = scatter(grid, own3, own3_got, other3, other3_got, ff * 3 // 4 // LANE * LANE)
        dq, dk, dv = attention_backward(grid, b2, q2, k2, v2, None, pieces_two, 4 * hd, hd)
        (b1, eg, dg2), (kept, gone) = cross_finish(
            grid, encoded, b2, r1, n2, dq, dk, dv, at1, at2, gains, pieces_two, d, hd
        )
        eg_far = grid.swap_m(eg)
        got = grid.swap_c(gone)
        z3, _ = settle(grid, w3)
        w2 = scatter(grid, kept[0], got[0], kept[1], got[1], 4 * LANE)
        dq, dk, dv, off = attention_backward(grid, b1, q1, k1, v1, base, pieces_two, 0, hd)
        dx, (kept, gone) = self_finish(
            grid, inputs, b1, n1, dq, dk, dv, off, dg2, dg3, base_hot, gains, pieces_one, d, hd, heads
        )
        got = grid.swap_c(gone)
        z2, _ = settle(grid, w2)
        w1 = scatter(grid, kept[0], got[0], kept[1], got[1], 4 * LANE)
        dx_far = grid.swap_m(dx)
        z1, (y, eg, z20, z30) = settle(grid, w1, (y, eg, z2[0], z3[0]))
        layer_output = both_sequences(y, y_far)
        encoded_gradient = both_sequences(eg, eg_far)
        input_gradient = both_sequences(dx, dx_far)
        s3 = summed([z30] + z3[1:])
        s2 = summed([z20] + z2[1:])
        s1 = summed(z1)
        small = s1[:, 3 * hd :]
        table_gradient = small[:heads, :NB]
        dgs = [small[:, NB + i] for i in range(3)]
        return (
            layer_output,
            input_gradient,
            encoded_gradient,
            table_gradient,
            s1[:, :hd],
            s1[:, hd : 2 * hd],
            s1[:, 2 * hd : 3 * hd],
            s2[:, :hd].T,
            s2[:, hd : 2 * hd],
            s2[:, 2 * hd : 3 * hd],
            s2[:, 3 * hd : 4 * hd],
            s2[:, 4 * hd :].T,
            s3[:, :ff],
            s3[:, ff : 2 * ff],
            s3[:, 2 * ff :].T,
            dgs[0],
            dgs[1],
            dgs[2],
        )

    return step


def solution(mesh):
    weight, turned, row, gain = P("dp", "mp"), P("mp", "dp"), P("dp", None), P("dp")
    weights = (weight, weight, weight, turned, weight, weight, weight, turned, weight, weight, turned)
    gains = (gain, gain, gain)
    return jax.shard_map(
        make(Grid(mesh.shape["dp"], mesh.shape["mp"])),
        mesh=mesh,
        in_specs=(row, row, row, P(), P("mp", None)) + weights + gains,
        out_specs=(row, row, row, P("mp", None)) + weights + gains,
        check_vma=False,
    )
```

```python
import jax
import jax.numpy as jnp
from jax import lax
from jax.experimental import pallas as pl
from jax.experimental.pallas import tpu as pltpu
from jax.sharding import PartitionSpec as P


DH = 64
NB = 32
L = 512
LANE = 128
QB = 128
EPS = 1e-06
NEG = -1e30
GELU_C = 0.7978845608028654
GELU_A = 0.044715
AXES = ("dp", "mp")
F32 = jnp.float32
BF16 = jnp.bfloat16
MIB = 1024 * 1024
VMEM_LIMIT = {"ka": 13, "kb": 16, "kca": 20, "kcb": 22, "kd1": 12, "kd2": 18, "ke1": 12, "ke2": 16}


def nn(left, right):
    return lax.dot_general(left, right, (((1,), (0,)), ((), ())), preferred_element_type=F32)


def nt(left, right):
    return lax.dot_general(left, right, (((1,), (1,)), ((), ())), preferred_element_type=F32)


class Grid:
    def __init__(self, n_dp, n_mp):
        assert n_mp == 2 and n_dp % 8 == 0
        self.n_dp, self.n_mp = n_dp, n_mp
        self.n_z = n_dp // 4

    def perm(self, move):
        pairs = []
        for z in range(self.n_z):
            for y in range(2):
                for c in range(2):
                    for m in range(2):
                        tz, ty, tc, tm = move(z, y, c, m)
                        pairs.append(
                            (
                                (((z * 2 + y) * 2) + c) * 2 + m,
                                (((tz * 2 + ty) * 2) + tc) * 2 + tm,
                            )
                        )
        return pairs

    def send(self, v, move):
        return lax.ppermute(v, AXES, self.perm(move))

    def swap_m(self, v):
        return self.send(v, lambda z, y, c, m: (z, y, c, 1 - m))

    def swap_y(self, v):
        return self.send(v, lambda z, y, c, m: (z, 1 - y, c, m))

    def swap_c(self, v):
        return self.send(v, lambda z, y, c, m: (z, y, 1 - c, m))

    def shift_z(self, v, d):
        n = self.n_z
        return self.send(v, lambda z, y, c, m: ((z + d) % n, y, c, m))


def place():
    dp = lax.axis_index("dp")
    return dp // 4, (dp // 2) % 2, dp % 2, lax.axis_index("mp")


def gather(grid, block):
    rows, cols = block.shape
    n = grid.n_z
    z, y, c, _ = place()
    got = [block] + [grid.shift_z(block, d) for d in range(1, n)]
    own = jnp.zeros((n, rows, cols), block.dtype)
    for d in range(n):
        own = lax.dynamic_update_slice(own, got[d][None], (lax.rem(z - d + n, n), 0, 0))
    half = n // 2
    by_m = grid.swap_m(own)
    by_y = grid.swap_y(own)
    part_a = by_m[:half]
    part_b = by_y[half:]
    diag_a = grid.swap_y(part_a)
    diag_b = grid.swap_m(part_b)
    pieces = [(own, 0, 0, 0), (by_y, 0, 1, 0), (by_m, 1, 0, 0), (diag_a, 1, 1, 0), (diag_b, 1, 1, half)]
    out = [(a, m, b, 0, j) for a, m, b, j in pieces]
    out += [(grid.swap_c(p[0]),) + p[1:3] + (1, p[3]) for p in pieces]
    if rows % 16 == 0:
        return out
    stacks = []
    for m in range(2):
        for b in range(2):
            for e in range(2):
                mine = sorted((p for p in out if p[1:4] == (m, b, e)), key=lambda p: p[4])
                stacks.append(jnp.concatenate([p[0] for p in mine], axis=0))
    whole = jnp.stack(stacks).reshape(2, 2, 2, n, rows, cols)
    whole = jnp.take(whole, jnp.arange(2) ^ y, axis=1)
    whole = jnp.take(whole, jnp.arange(2) ^ c, axis=2)
    whole = whole.transpose(0, 3, 1, 2, 4, 5).reshape(2, n * 4 * rows, cols)
    return [(whole[m], m, None, None, 0) for m in range(2)]


class Weights:
    def __init__(self, pieces, n_z, half=None):
        chosen = [p for p in pieces if half is None or p[1] == half]
        self.arrays = [p[0] for p in chosen]
        self.metas = [p[1:] for p in chosen]
        self.packed = self.metas[0][1] is None
        self.n_z = n_z
        self.rows = pieces[0][0].shape[1] if not self.packed else pieces[0][0].shape[0] // (4 * n_z)
        self.half = half

    def specs(self):
        return [(a, True) for a in self.arrays]

    def scratch(self, n):
        if self.packed:
            return pltpu.VMEM((4 * self.n_z * self.rows, n), BF16)
        return pltpu.VMEM((self.n_z, 2, 2, self.rows, n), BF16)

    def sems(self):
        return pltpu.SemaphoreType.DMA((len(self.arrays),))

    def start(self, refs, dest, sems, src, n, at=0):
        _, y, c, _ = place()
        copies = []
        for i, ((m, b, e, j), ref) in enumerate(zip(self.metas, refs)):
            to = pl.ds(at + (0 if self.half is not None else m * n), n)
            if self.packed:
                cp = pltpu.make_async_copy(ref.at[:, pl.ds(src, n)], dest.at[:, to], sems.at[i])
            else:
                k = ref.shape[0]
                cp = pltpu.make_async_copy(
                    ref.at[:, :, pl.ds(src, n)], dest.at[pl.ds(j, k), y ^ b, c ^ e, :, to], sems.at[i]
                )
            cp.start()
            copies.append(cp)
        return copies

    def value(self, dest, first, last):
        if self.packed:
            return dest[:, first:last]
        return dest[:, :, :, :, first:last].reshape(4 * self.n_z * self.rows, last - first)

    def columns(self, dest, first, size):
        if self.packed:
            return dest[:, pl.ds(first, size)]
        return dest[:, :, :, :, pl.ds(first, size)].reshape(4 * self.n_z * self.rows, size)


def wait(copies):
    for cp in copies:
        cp.wait()


def rms(values, gain):
    return values * lax.rsqrt(jnp.mean(values * values, axis=-1, keepdims=True) + EPS) * gain


def rms_back(values, gain, back):
    scale = lax.rsqrt(jnp.mean(values * values, axis=-1, keepdims=True) + EPS)
    unit = values * scale
    incoming = back * gain
    grad = scale * (incoming - unit * jnp.mean(incoming * unit, axis=-1, keepdims=True))
    return grad, jnp.sum(back * unit, axis=0, keepdims=True)


def lane_masks():
    lane = lax.broadcasted_iota(jnp.int32, (1, LANE), 1)
    low = (lane < DH).astype(F32)
    return [low.astype(BF16), (1.0 - low).astype(BF16)]


def bias_strip(base):
    first = pltpu.roll(jnp.broadcast_to(base, (8, L)), 0, 1, stride=1, stride_axis=0)
    return jnp.concatenate([first] + [pltpu.roll(first, 8 * g, 1) for g in range(1, QB // 8)], axis=0)


def fold_band(band):
    total = band[0:8]
    for g in range(1, QB // 8):
        total = total + pltpu.roll(band[8 * g : 8 * g + 8], L - 8 * g, 1)
    row = lax.broadcasted_iota(jnp.int32, (8, L), 0)
    for bit in range(3):
        total = jnp.where(((row >> bit) & 1) == 1, pltpu.roll(total, L - (1 << bit), 1), total)
    return jnp.sum(total, axis=0, keepdims=True)


WIDE = 256


def masked_strip(base_ref, row):
    strip = bias_strip(base_ref[pl.ds(row, 1), :])
    at_row = lax.broadcasted_iota(jnp.int32, (QB, L), 0)
    at_col = lax.broadcasted_iota(jnp.int32, (QB, L), 1)
    return jnp.where(at_col >= at_row, strip, NEG)


def bias_tile(strip, first_key, keys, first_query):
    parts = []
    for k in range(first_key, first_key + keys, QB):
        lo = first_query - k
        if lo >= 0:
            parts.append(strip[:, lo : lo + WIDE])
        else:
            parts.append(jnp.concatenate([jnp.full((QB, -lo), NEG, F32), strip[:, : WIDE + lo]], axis=1))
    return jnp.concatenate(parts, axis=0)


def half_rows(turned):
    none = jnp.zeros_like(turned[:DH])
    return [jnp.concatenate([turned[:DH], none], axis=0), jnp.concatenate([none, turned[DH:]], axis=0)]


def attend_loop(q_ref, k_ref, v_ref, o_ref, lse_ref, base_ref):
    masks = lane_masks()
    causal = base_ref is not None

    def step(t, carry):
        at = pl.ds(pl.multiple_of(t * LANE, LANE), LANE)
        q, k, v = q_ref[:, at], k_ref[:, at], v_ref[:, at]
        vt = half_rows(v.T)
        outs = [None] * (L // WIDE)
        keys = [k * masks[hh] for hh in range(2)]
        strips = [masked_strip(base_ref, t * 2 + hh) if causal else None for hh in range(2)]
        order = [(hh, b) for b in range(L // WIDE) for hh in range(2)]

        def scores(hh, b):
            n = (b + 1) * WIDE if causal else k.shape[0]
            s = nt(keys[hh][:n], q[b * WIDE : (b + 1) * WIDE])
            return s + bias_tile(strips[hh], 0, n, b * WIDE) if causal else s

        ahead = scores(*order[0])
        for i, (hh, b) in enumerate(order):
            s = ahead
            if i + 1 < len(order):
                ahead = scores(*order[i + 1])
            top = jnp.max(s, axis=0, keepdims=True)
            e = jnp.exp(s - top)
            total = jnp.sum(e, axis=0, keepdims=True)
            mixed = nn(vt[hh][:, : s.shape[0]], e.astype(BF16)) * (1.0 / total)
            outs[b] = mixed if outs[b] is None else outs[b] + mixed
            lse_ref[pl.ds(t * 2 + hh, 1), b * WIDE : (b + 1) * WIDE] = top + jnp.log(total)
        o_ref[:, at] = jnp.concatenate(outs, axis=1).T.astype(BF16)
        return carry

    lax.fori_loop(0, q_ref.shape[1] // LANE, step, 0)


def attend_back_loop(q_ref, k_ref, v_ref, o_ref, do_ref, lse_ref, dq_ref, dk_ref, dv_ref, p_ref, ds_ref, base_ref, off_ref, band_ref):
    masks = lane_masks()
    causal = base_ref is not None
    blocks = L // WIDE

    def step(t, carry):
        at = pl.ds(pl.multiple_of(t * LANE, LANE), LANE)
        q, k, v, do = q_ref[:, at], k_ref[:, at], v_ref[:, at], do_ref[:, at]
        prod = (do.astype(F32) * o_ref[:, at].astype(F32)).T
        kt = half_rows(k.T)
        for hh in range(2):
            km, vm = k * masks[hh], v * masks[hh]
            lse = lse_ref[pl.ds(t * 2 + hh, 1), :]
            delta = jnp.sum(prod[hh * DH : (hh + 1) * DH], axis=0, keepdims=True)
            if causal:
                strip = masked_strip(base_ref, t * 2 + hh)
                band_ref[...] = jnp.zeros_like(band_ref)
            for b in range(blocks):
                cols = slice(b * WIDE, (b + 1) * WIDE)
                to = slice((b * 2 + hh) * WIDE, (b * 2 + hh + 1) * WIDE)
                for kb in range(b + 1 if causal else k.shape[0] // WIDE):
                    rows = slice(kb * WIDE, (kb + 1) * WIDE)
                    s = nt(km[rows], q[cols])
                    if causal:
                        s = s + bias_tile(strip, kb * WIDE, WIDE, b * WIDE)
                    prob = jnp.exp(s - lse[:, cols])
                    p_ref[rows, to] = prob.astype(BF16)
                    ds = prob * (nt(vm[rows], do[cols]) - delta[:, cols])
                    ds_ref[rows, to] = ds.astype(BF16)
                    if causal:
                        for i in range(WIDE // QB):
                            lo = b * WIDE - kb * WIDE - i * QB
                            part = ds[i * QB : (i + 1) * QB]
                            if lo < 0:
                                part, lo = part[:, -lo:], 0
                            band_ref[:, lo : lo + part.shape[1]] += part
            if causal:
                off_ref[pl.ds(t * 2 + hh, 1), :] = fold_band(band_ref[...])
        do2 = jnp.concatenate([do[b * WIDE : (b + 1) * WIDE] * masks[hh] for b in range(blocks) for hh in range(2)], axis=0)
        q2 = jnp.concatenate([q[b * WIDE : (b + 1) * WIDE] * masks[hh] for b in range(blocks) for hh in range(2)], axis=0)
        if causal:
            for kb in range(blocks):
                rows = slice(kb * WIDE, (kb + 1) * WIDE)
                dv_ref[rows, at] = nn(p_ref[rows, kb * 2 * WIDE :], do2[kb * 2 * WIDE :]).astype(BF16)
                dk_ref[rows, at] = nn(ds_ref[rows, kb * 2 * WIDE :], q2[kb * 2 * WIDE :]).astype(BF16)
        else:
            dv_ref[:, at] = nn(p_ref[...], do2).astype(BF16)
            dk_ref[:, at] = nn(ds_ref[...], q2).astype(BF16)
        dq = []
        for b in range(blocks):
            n = (b + 1) * WIDE if causal else k.shape[0]
            dq.append(
                sum(nn(kt[hh][:, :n], ds_ref[:n, (b * 2 + hh) * WIDE : (b * 2 + hh + 1) * WIDE]) for hh in range(2))
            )
        dq_ref[:, at] = jnp.concatenate(dq, axis=1).T.astype(BF16)
        return carry

    lax.fori_loop(0, q_ref.shape[1] // LANE, step, 0)


def call(body, outs, args, scratch, name, flops):
    return pl.pallas_call(
        body,
        out_shape=tuple(jax.ShapeDtypeStruct(s, d) for s, d in outs),
        in_specs=[pl.BlockSpec(memory_space=pltpu.HBM if far else pltpu.VMEM) for _, far in args],
        out_specs=tuple(pl.BlockSpec(memory_space=pltpu.VMEM) for _ in outs),
        scratch_shapes=scratch,
        compiler_params=pltpu.CompilerParams(vmem_limit_bytes=VMEM_LIMIT[name] * MIB),
        cost_estimate=pl.CostEstimate(flops=flops, transcendentals=0, bytes_accessed=10_000_000),
    )(*[pltpu.with_memory_space_constraint(a, pltpu.HBM) if far else a for a, far in args])


def sequence_copy(ref, dest, sem):
    m = lax.axis_index("mp")
    cp = pltpu.make_async_copy(ref.at[pl.ds(pl.multiple_of(m * L, L), L), :], dest, sem)
    cp.start()
    return cp


def near(*arrays):
    return [(a, False) for a in arrays]


class Parts:
    def __init__(self, grid, d, cols, halves):
        self.n = grid.n_z
        self.rows = d // (4 * self.n)
        self.sorted = self.rows % 16 == 0
        self.d, self.cols, self.halves = d, cols, halves

    def outs(self):
        lead = (2,) if self.halves else ()
        if self.sorted:
            return [(lead + (2, self.n, self.rows, self.cols), BF16)] * 2
        return [(lead + (self.d, self.cols), BF16)]

    def count(self):
        return 2 if self.sorted else 1

    def put(self, refs, half, at, value):
        low = value.astype(BF16)
        size = low.shape[1]
        cols = pl.ds(at, size)
        if not self.sorted:
            if half is None:
                refs[0][:, cols] = low
            else:
                refs[0][half, :, cols] = low
            return
        z, y, c, _ = place()
        low = low.reshape(self.n, 2, 2, self.rows, size)
        for i in range(self.n):
            for b in range(2):
                first, second = low[i, b, 0], low[i, b, 1]
                where = (b ^ y, lax.rem(i - z + self.n, self.n), slice(None), cols)
                if half is not None:
                    where = (half,) + where
                refs[0][where] = lax.select(c == 0, first, second)
                refs[1][where] = lax.select(c == 0, second, first)

    def put_halves(self, refs, at, n, value):
        self.put(refs, 0, at, value[:, :n])
        self.put(refs, 1, at, value[:, n:])

    def split(self, arrays):
        if self.sorted:
            return arrays
        z, y, c, _ = place()
        v = arrays[0]
        v = v.reshape(v.shape[:-2] + (self.n, 2, 2, self.rows, self.cols))
        lead = v.ndim - 5
        v = jnp.moveaxis(v, (lead + 2, lead + 1, lead), (0, lead + 1, lead + 2))
        v = jnp.take(v, (z + jnp.arange(self.n)) % self.n, axis=lead + 2)
        v = jnp.take(v, jnp.arange(2) ^ y, axis=lead + 1)
        v = jnp.take(v, jnp.arange(2) ^ c, axis=0)
        return v[0], v[1]


DMA = pltpu.SemaphoreType.DMA


def self_forward(grid, inputs, base_hot, pieces, d, hd, heads):
    ws = Weights(pieces, grid.n_z)
    k = len(ws.arrays)
    w2 = 2 * hd

    def body(*refs):
        x_ref, hot_ref = refs[:2]
        w_refs = refs[2 : 2 + k]
        n1_ref, q_ref, k_ref, v_ref, o_ref, gain_ref, base_ref, lse_ref = refs[2 + k : 10 + k]
        x_v, we, wq, wk, wv, sem_x, s_e, s_q, s_k, s_v = refs[10 + k :]
        cx = sequence_copy(x_ref, x_v, sem_x)
        ce = ws.start(w_refs, we, s_e, 3 * hd, LANE)
        cq = ws.start(w_refs, wq, s_q, 0, hd)
        ck = ws.start(w_refs, wk, s_k, hd, hd)
        cv = ws.start(w_refs, wv, s_v, 2 * hd, hd)
        cx.wait()
        x = x_v[...].astype(F32)
        scaled = x * lax.rsqrt(jnp.mean(x * x, axis=-1, keepdims=True) + EPS)
        wait(ce)
        extra = ws.value(we, 0, 2 * LANE)
        rows = ws.rows
        shards = d // rows
        column = lax.broadcasted_iota(jnp.int32, (3 * shards, d), 1)
        row = lax.broadcasted_iota(jnp.int32, (3 * shards, d), 0)
        wanted = lax.rem(row, shards) * rows + heads + row // shards
        packed = nn((column == wanted).astype(F32).astype(BF16), extra[:, :LANE]).astype(BF16)
        lane = lax.broadcasted_iota(jnp.int32, (LANE, d), 0)
        column = lax.broadcasted_iota(jnp.int32, (LANE, d), 1)
        wide = nn(packed, (lane == lax.rem(column, rows)).astype(F32).astype(BF16))
        column = lax.broadcasted_iota(jnp.int32, (shards, d), 1)
        mine = column // rows == lax.broadcasted_iota(jnp.int32, (shards, d), 0)
        gains = [
            jnp.sum(jnp.where(mine, wide[i * shards : (i + 1) * shards], 0.0), axis=0, keepdims=True) for i in range(3)
        ]
        gains = jnp.concatenate(gains + [jnp.zeros((5, d), F32)], axis=0)
        gain_ref[...] = gains
        lse_ref[...] = jnp.zeros_like(lse_ref)
        base_ref[...] = jnp.zeros_like(base_ref)
        for a in range(2):
            base_ref[a * heads : (a + 1) * heads, :] = nn(extra[0:16, a * LANE : (a + 1) * LANE], hot_ref[...])[:heads]
        n1 = (scaled * gains[0:1]).astype(BF16)
        n1_ref[...] = n1
        wait(cq)
        q_ref[...] = nn(n1_ref[...], ws.value(wq, 0, w2)).astype(BF16)
        wait(ck)
        k_ref[...] = nn(n1_ref[...], ws.value(wk, 0, w2)).astype(BF16)
        wait(cv)
        v_ref[...] = nn(n1_ref[...], ws.value(wv, 0, w2)).astype(BF16)
        attend_loop(q_ref, k_ref, v_ref, o_ref, lse_ref, base_ref)

    row = ((L, w2), BF16)
    return call(
        body,
        [((L, d), BF16), row, row, row, row, ((8, d), F32), ((16, L), F32), ((16, L), F32)],
        [(inputs, True), (base_hot, False)] + ws.specs(),
        [
            pltpu.VMEM((L, d), BF16),
            ws.scratch(2 * LANE),
            ws.scratch(w2),
            ws.scratch(w2),
            ws.scratch(w2),
            DMA,
            ws.sems(),
            ws.sems(),
            ws.sems(),
            ws.sems(),
        ],
        "ka",
        3_000_000_000,
    )


def cross_forward(grid, inputs, encoded, attn_one, gains, pieces, d, hd):
    ws = Weights(pieces, grid.n_z)
    k = len(ws.arrays)
    w2 = 2 * hd

    def body(*refs):
        x_ref, enc_ref, a1_ref, gain_ref = refs[:4]
        w_refs = refs[4 : 4 + k]
        r1_ref, r2_ref, n2_ref, q_ref, k_ref, v_ref, o_ref, n3_ref, lse_ref = refs[4 + k : 13 + k]
        x_v, enc_v, w1, wq, wk, wv, w2v, sem_x, sem_e, s_1, s_q, s_k, s_v, s_2 = refs[13 + k :]
        ce = sequence_copy(enc_ref, enc_v, sem_e)
        ck = ws.start(w_refs, wk, s_k, 2 * hd, hd)
        cv = ws.start(w_refs, wv, s_v, 3 * hd, hd)
        cx = sequence_copy(x_ref, x_v, sem_x)
        c1 = ws.start(w_refs, w1, s_1, 0, hd)
        cq = ws.start(w_refs, wq, s_q, hd, hd)
        c2 = ws.start(w_refs, w2v, s_2, 4 * hd, hd)
        ce.wait()
        wait(ck)
        k_ref[...] = nn(enc_v[...], ws.value(wk, 0, w2)).astype(BF16)
        wait(cv)
        v_ref[...] = nn(enc_v[...], ws.value(wv, 0, w2)).astype(BF16)
        cx.wait()
        wait(c1)
        r1 = x_v[...].astype(F32) + nt(a1_ref[...], ws.value(w1, 0, w2))
        r1_ref[...] = r1
        n2 = rms(r1, gain_ref[1:2, :]).astype(BF16)
        n2_ref[...] = n2
        wait(cq)
        q_ref[...] = nn(n2, ws.value(wq, 0, w2)).astype(BF16)
        lse_ref[...] = jnp.zeros_like(lse_ref)
        attend_loop(q_ref, k_ref, v_ref, o_ref, lse_ref, None)
        wait(c2)
        r2 = r1_ref[...] + nt(o_ref[...], ws.value(w2v, 0, w2))
        r2_ref[...] = r2
        n3_ref[...] = rms(r2, gain_ref[2:3, :]).astype(BF16)

    row = ((L, w2), BF16)
    wide = ((L, d), BF16)
    return call(
        body,
        [((L, d), F32), ((L, d), F32), wide, row, row, row, row, wide, ((16, L), F32)],
        [(inputs, True), (encoded, True)] + near(attn_one, gains) + ws.specs(),
        [pltpu.VMEM((L, d), BF16), pltpu.VMEM((L, d), BF16)]
        + [ws.scratch(w2) for _ in range(5)]
        + [DMA, DMA]
        + [ws.sems() for _ in range(5)],
        "kb",
        5_000_000_000,
    )


def feed_forward(grid, cotangent, n3, r2, gains, carried, pieces, half, d, ff):
    ws = Weights(pieces, grid.n_z, half)
    k = len(ws.arrays)
    tile = min(256, ff)
    last = carried is not None
    extra_in = 4 if last else 0
    parts = Parts(grid, d, 3 * ff, False)
    ng = parts.count()

    def body(*refs):
        cot_ref, n3_ref = refs[:2]
        w_refs = refs[2 + extra_in : 2 + extra_in + k]
        rest = refs[2 + extra_in + k :]
        if last:
            r2_ref, gain_ref, yin_ref, bin_ref = refs[2:6]
            y_ref, b2_ref, dg_ref, y_acc, b3_acc = rest[ng : ng + 5]
        else:
            y_acc, b3_acc = rest[ng : ng + 2]
        g_refs, rest = rest[:ng], rest[ng + (5 if last else 2) :]
        cot_v, wg, wu, wd, cot_t, n3_t, sem_c, s_g, s_u, s_d = rest
        cc = sequence_copy(cot_ref, cot_v, sem_c)
        cg = ws.start(w_refs, wg, s_g, 0, ff)
        cu = ws.start(w_refs, wu, s_u, ff, ff)
        cd = ws.start(w_refs, wd, s_d, 2 * ff, ff)
        if last:
            y_acc[...] = r2_ref[...] + yin_ref[...]
            b3_acc[...] = bin_ref[...]
        else:
            y_acc[...] = jnp.zeros_like(y_acc)
            b3_acc[...] = jnp.zeros_like(b3_acc)
        n3_t[...] = n3_ref[...].T
        cc.wait()
        cot_t[...] = cot_v[...].T
        wait(cg)
        wait(cu)
        wait(cd)

        def step(t, carry):
            at = pl.multiple_of(t * tile, LANE)
            gate, upw, down = ws.columns(wg, at, tile), ws.columns(wu, at, tile), ws.columns(wd, at, tile)
            u = nn(n3_ref[...], gate)
            up = nn(n3_ref[...], upw)
            bh = nn(cot_v[...], down)
            sq = u * u
            th = jnp.tanh(GELU_C * (u + GELU_A * (sq * u)))
            both = 0.5 * (1.0 + th)
            gelu = u * both
            slope = both + 0.5 * u * (1.0 - th * th) * (GELU_C * (1.0 + (3.0 * GELU_A) * sq))
            hidden = (gelu * up).astype(BF16)
            gate_low = (bh * up * slope).astype(BF16)
            up_low = (bh * gelu).astype(BF16)
            y_acc[...] += nt(hidden, down)
            b3_acc[...] += nt(gate_low, gate) + nt(up_low, upw)
            parts.put(g_refs, None, at, nn(n3_t[...], gate_low))
            parts.put(g_refs, None, pl.multiple_of(ff + at, LANE), nn(n3_t[...], up_low))
            parts.put(g_refs, None, pl.multiple_of(2 * ff + at, LANE), nn(cot_t[...], hidden))
            return carry

        lax.fori_loop(0, ff // tile, step, 0)
        if last:
            y_ref[...] = y_acc[...].astype(BF16)
            grad, dg = rms_back(r2_ref[...], gain_ref[2:3, :], b3_acc[...])
            b2_ref[...] = cot_v[...].astype(F32) + grad
            dg_ref[...] = dg

    full = ((L, d), F32)
    outs = parts.outs()
    outs += [((L, d), BF16), full, ((1, d), F32)] if last else [full, full]
    scratch = [pltpu.VMEM((L, d), F32), pltpu.VMEM((L, d), F32)] if last else []
    result = call(
        body,
        outs,
        [(cotangent, True)] + near(n3) + (near(r2, gains, *carried) if last else []) + ws.specs(),
        scratch
        + [
            pltpu.VMEM((L, d), BF16),
            ws.scratch(ff),
            ws.scratch(ff),
            ws.scratch(ff),
            pltpu.VMEM((d, L), BF16),
            pltpu.VMEM((d, L), BF16),
            DMA,
            ws.sems(),
            ws.sems(),
            ws.sems(),
        ],
        "kcb" if last else "kca",
        7_500_000_000,
    )
    return parts.split(result[:ng]), result[ng:]


def attention_backward(grid, back, q, k, v, attn, lse, base, pieces, first_col, hd, name):
    ws = Weights(pieces, grid.n_z)
    n = len(ws.arrays)
    w2 = 2 * hd
    causal = base is not None

    def body(*refs):
        b_ref, q_ref, k_ref, v_ref, o_ref, lse_ref = refs[:6]
        base_ref = refs[6] if causal else None
        refs = refs[7 if causal else 6 :]
        w_refs = refs[:n]
        dq_ref, dk_ref, dv_ref = refs[n : n + 3]
        off_ref = refs[n + 3] if causal else None
        wo, do, p_ref, ds_ref = refs[n + (4 if causal else 3) : n + (8 if causal else 7)]
        band_ref, s_o = refs[-2:]
        co = ws.start(w_refs, wo, s_o, first_col, hd)
        if causal:
            off_ref[...] = jnp.zeros_like(off_ref)
        low = b_ref[...].astype(BF16)
        wait(co)
        do[...] = nn(low, ws.value(wo, 0, w2)).astype(BF16)
        attend_back_loop(
            q_ref, k_ref, v_ref, o_ref, do, lse_ref, dq_ref, dk_ref, dv_ref, p_ref, ds_ref, base_ref, off_ref, band_ref
        )

    row = ((L, w2), BF16)
    return call(
        body,
        [row, row, row] + ([((16, L), F32)] if causal else []),
        near(back, q, k, v, attn, lse) + (near(base) if causal else []) + ws.specs(),
        [
            ws.scratch(w2),
            pltpu.VMEM((L, w2), BF16),
            pltpu.VMEM((L, 2 * L), BF16),
            pltpu.VMEM((L, 2 * L), BF16),
            pltpu.VMEM((QB, L), F32),
            ws.sems(),
        ],
        name,
        3_000_000_000,
    )


def cross_finish(grid, encoded, b2, r1, n2, dq, dk, dv, attn_one, attn_two, gains, pieces, d, hd):
    ws = Weights(pieces, grid.n_z)
    k = len(ws.arrays)
    w2 = 2 * hd
    parts = Parts(grid, d, 5 * hd, True)
    ng = parts.count()

    def body(*refs):
        enc_ref, b2_ref, r1_ref, n2_ref, dq_ref, dk_ref, dv_ref, a1_ref, a2_ref, gain_ref = refs[:10]
        w_refs = refs[10 : 10 + k]
        b1_ref, eg_ref, dg_ref = refs[10 + k : 13 + k]
        g_refs = refs[13 + k : 13 + k + ng]
        enc_v, wq, wk, wv, sem_e, s_q, s_k, s_v = refs[13 + k + ng :]
        cq = ws.start(w_refs, wq, s_q, hd, hd)
        ce = sequence_copy(enc_ref, enc_v, sem_e)
        ck = ws.start(w_refs, wk, s_k, 2 * hd, hd)
        cv = ws.start(w_refs, wv, s_v, 3 * hd, hd)
        parts.put_halves(g_refs, hd, hd, nn(n2_ref[...].T, dq_ref[...]))
        wait(cq)
        grad, dg = rms_back(r1_ref[...], gain_ref[1:2, :], nt(dq_ref[...], ws.value(wq, 0, w2)))
        dg_ref[...] = dg
        b1 = b2_ref[...] + grad
        b1_ref[...] = b1
        parts.put_halves(g_refs, 0, hd, nn(b1.astype(BF16).T, a1_ref[...]))
        ce.wait()
        enc_t = enc_v[...].T
        parts.put_halves(g_refs, 2 * hd, hd, nn(enc_t, dk_ref[...]))
        parts.put_halves(g_refs, 3 * hd, hd, nn(enc_t, dv_ref[...]))
        parts.put_halves(g_refs, 4 * hd, hd, nn(b2_ref[...].astype(BF16).T, a2_ref[...]))
        wait(ck)
        wait(cv)
        eg = nt(dk_ref[...], ws.value(wk, 0, w2)) + nt(dv_ref[...], ws.value(wv, 0, w2))
        eg_ref[...] = eg.astype(BF16)

    result = call(
        body,
        [((L, d), F32), ((L, d), BF16), ((1, d), F32)] + parts.outs(),
        [(encoded, True)] + near(b2, r1, n2, dq, dk, dv, attn_one, attn_two, gains) + ws.specs(),
        [pltpu.VMEM((L, d), BF16)]
        + [ws.scratch(w2) for _ in range(3)]
        + [DMA]
        + [ws.sems() for _ in range(3)],
        "kd2",
        5_000_000_000,
    )
    return result[:3], parts.split(result[3:])


def self_finish(grid, inputs, b1, n1, dq, dk, dv, off, dg2, dg3, base_hot, gains, pieces, d, hd, heads):
    ws = Weights(pieces, grid.n_z)
    k = len(ws.arrays)
    w2 = 2 * hd
    parts = Parts(grid, d, 3 * hd + LANE, True)
    ng = parts.count()

    def body(*refs):
        x_ref, b1_ref, n1_ref, dq_ref, dk_ref, dv_ref, off_ref, dg2_ref, dg3_ref, hot_ref, gain_ref = refs[:11]
        w_refs = refs[11 : 11 + k]
        dx_ref = refs[11 + k]
        g_refs = refs[12 + k : 12 + k + ng]
        x_v, wq, wk, wv, sem_x, s_q, s_k, s_v = refs[12 + k + ng :]
        cq = ws.start(w_refs, wq, s_q, 0, hd)
        ck = ws.start(w_refs, wk, s_k, hd, hd)
        cv = ws.start(w_refs, wv, s_v, 2 * hd, hd)
        cx = sequence_copy(x_ref, x_v, sem_x)
        n1_t = n1_ref[...].T
        parts.put_halves(g_refs, 0, hd, nn(n1_t, dq_ref[...]))
        parts.put_halves(g_refs, hd, hd, nn(n1_t, dk_ref[...]))
        parts.put_halves(g_refs, 2 * hd, hd, nn(n1_t, dv_ref[...]))
        wait(cq)
        back = nt(dq_ref[...], ws.value(wq, 0, w2))
        wait(ck)
        back = back + nt(dk_ref[...], ws.value(wk, 0, w2))
        wait(cv)
        back = back + nt(dv_ref[...], ws.value(wv, 0, w2))
        cx.wait()
        grad, dg = rms_back(x_v[...].astype(F32), gain_ref[0:1, :], back)
        dx_ref[...] = (b1_ref[...] + grad).astype(BF16)
        dgs = jnp.concatenate([dg, dg2_ref[...], dg3_ref[...], jnp.zeros((5, d), F32)], axis=0)
        turned = jnp.concatenate([jnp.zeros((NB, d), F32), dgs, jnp.zeros((LANE - NB - 8, d), F32)], axis=0).T
        hot = hot_ref[...]
        sums = off_ref[...]
        table = jnp.zeros((16, LANE), F32)
        for _ in range(3):
            low = sums.astype(BF16)
            table = table + nt(low, hot)
            sums = sums - low.astype(F32)
        table = table.astype(BF16)
        shard_row = lax.rem(lax.broadcasted_iota(jnp.int32, (d, 16), 0), parts.rows)
        column = lax.broadcasted_iota(jnp.int32, (d, 16), 1)
        for a in range(2):
            spread = ((shard_row + a * heads == column) & (shard_row < heads)).astype(F32).astype(BF16)
            parts.put(g_refs, a, 3 * hd, nn(spread, table) + turned)

    result = call(
        body,
        [((L, d), BF16)] + parts.outs(),
        [(inputs, True)] + near(b1, n1, dq, dk, dv, off, dg2, dg3, base_hot, gains) + ws.specs(),
        [pltpu.VMEM((L, d), BF16)]
        + [ws.scratch(w2) for _ in range(3)]
        + [DMA]
        + [ws.sems() for _ in range(3)],
        "ke2",
        4_000_000_000,
    )
    return result[0], parts.split(result[1:])


def added(left, right):
    return (left.astype(F32) + right.astype(F32)).astype(BF16)


def scatter(grid, own, own_got, other, other_got, first, held=None):
    sent_a = added(other[..., :first], other_got[..., :first])
    sent_b = jnp.stack([added(v[1, ..., first:], g[1, ..., first:]) for v, g in ((own, own_got), (other, other_got))])
    if held is not None:
        sent_a, sent_b, held = lax.optimization_barrier((sent_a, sent_b, held))
    got = grid.swap_m(sent_a)
    got_b = grid.swap_y(sent_b)

    def a_sum(i):
        return added3(own[i, ..., :first], own_got[i, ..., :first], got[i])

    far_a = grid.swap_y(a_sum(1))
    far_b = grid.swap_m(added3(other[0, ..., first:], other_got[0, ..., first:], got_b[1]))
    wa, wb = a_sum(0), added3(own[0, ..., first:], own_got[0, ..., first:], got_b[0])
    return (wa, wb), (far_a, far_b), held


def joined(kept, far):
    return [
        jnp.concatenate([added(v[d], f[d]) for v, f in zip(kept, far)], axis=-1) for d in range(kept[0].shape[0])
    ]


def scatter_wide(grid, own, own_got, other, other_got, first):
    n = grid.n_z
    got_own = grid.swap_y(added(own[1, ..., first:], own_got[1, ..., first:]))
    got_other = grid.swap_y(added(other[1, ..., first:], other_got[1, ..., first:]))
    got = grid.swap_m(added(other[..., :first], other_got[..., :first]))

    def a_sum(i):
        return added3(own[i, ..., :first], own_got[i, ..., :first], got[i])

    far_a = grid.swap_y(a_sum(1))
    wa = a_sum(0)
    parts = []
    for v, g, far in ((own, own_got, got_own), (other, other_got, got_other)):
        w = [added3(v[0, d, :, first:], g[0, d, :, first:], far[d]) for d in range(n)]
        parts.append([w[0]] + [grid.shift_z(w[d], d) for d in range(1, n)])
    a = [added(wa[d], far_a[d]) for d in range(n)]
    a = [a[0]] + [grid.shift_z(a[d], d) for d in range(1, n)]
    return a, parts[0], parts[1]


def settle(grid, w, gate=None):
    sent = w[1:]
    if gate is not None:
        sent, gate = lax.optimization_barrier((sent, gate))
    return [w[0]] + [grid.shift_z(v, d + 1) for d, v in enumerate(sent)], gate


def summed(arrays):
    out = arrays[0].astype(F32)
    for v in arrays[1:]:
        out = out + v.astype(F32)
    return out


def added3(a, b, c):
    return (a.astype(F32) + b.astype(F32) + c.astype(F32)).astype(BF16)


def both_sequences(mine, other):
    first = lax.axis_index("mp") == 0
    low = jnp.where(first, mine, other)
    high = jnp.where(first, other, mine)
    return jnp.concatenate([low, high], axis=0).astype(F32)


def make(grid):
    def step(
        inputs,
        encoded,
        cotangent,
        buckets,
        rel_table,
        query_self,
        keys_self,
        values_self,
        output_self,
        query_cross,
        keys_cross,
        values_cross,
        output_cross,
        gate_weight,
        up_weight,
        down_weight,
        gain_first,
        gain_second,
        gain_third,
    ):
        d = inputs.shape[1]
        hd = query_self.shape[1]
        ff = gate_weight.shape[1]
        rows = query_self.shape[0]
        heads = rel_table.shape[0]
        assert inputs.shape[0] == 2 * L and heads + 3 <= rows <= LANE and heads <= 8
        extra = jnp.concatenate(
            [
                jnp.pad(rel_table, ((0, 0), (0, LANE - NB))),
                jnp.pad(jnp.stack([gain_first, gain_second, gain_third]), ((0, rows - heads - 3), (0, LANE - rows))),
            ],
            axis=0,
        )
        group_one = jnp.concatenate([query_self, keys_self, values_self, extra], axis=1)
        group_two = jnp.concatenate([output_self.T, query_cross, keys_cross, values_cross, output_cross.T], axis=1)
        group_three = jnp.concatenate([gate_weight, up_weight, down_weight.T], axis=1)
        pieces_one = gather(grid, group_one)
        pieces_two = gather(grid, group_two)
        pieces_three = gather(grid, group_three)

        base_hot = (buckets[None, :] == lax.broadcasted_iota(jnp.int32, (LANE, L), 0)).astype(BF16)

        n1, q1, k1, v1, at1, gains, base, lse1 = self_forward(grid, inputs, base_hot, pieces_one, d, hd, heads)
        r1, r2, n2, q2, k2, v2, at2, n3, lse2 = cross_forward(grid, inputs, encoded, at1, gains, pieces_two, d, hd)
        (own3, gone), (ya, ba) = feed_forward(grid, cotangent, n3, r2, gains, None, pieces_three, 0, d, ff)
        own3_got = grid.swap_c(gone)
        (other3, gone), (y, b2, dg3) = feed_forward(
            grid, cotangent, n3, r2, gains, (ya, ba), pieces_three, 1, d, ff
        )
        other3_got = grid.swap_c(gone)
        y_far = grid.swap_m(y)
        a3, bo3, bt3 = scatter_wide(grid, own3, own3_got, other3, other3_got, ff * 3 // 4 // LANE * LANE)
        dq, dk, dv = attention_backward(grid, b2, q2, k2, v2, at2, lse2, None, pieces_two, 4 * hd, hd, "kd1")
        (b1, eg, dg2), (kept, gone) = cross_finish(
            grid, encoded, b2, r1, n2, dq, dk, dv, at1, at2, gains, pieces_two, d, hd
        )
        eg_far = grid.swap_m(eg)
        got = grid.swap_c(gone)
        kept2, far2, _ = scatter(grid, kept[0], got[0], kept[1], got[1], 7 * LANE)
        dq, dk, dv, off = attention_backward(grid, b1, q1, k1, v1, at1, lse1, base, pieces_two, 0, hd, "ke1")
        dx, (kept, gone) = self_finish(
            grid, inputs, b1, n1, dq, dk, dv, off, dg2, dg3, base_hot, gains, pieces_one, d, hd, heads
        )
        got = grid.swap_c(gone)
        kept1, far1, (kept2, bt30, y, eg) = scatter(
            grid, kept[0], got[0], kept[1], got[1], 5 * LANE, (kept2, bt3[0], y, eg)
        )
        b3 = bo3 + [grid.swap_m(summed([bt30] + bt3[1:]).astype(BF16))]
        z2, _ = settle(grid, joined(kept2, far2))
        w1 = joined(kept1, far1)
        dx_far = grid.swap_m(dx)
        z1, (z20, a30, b30) = settle(grid, w1, (z2[0], a3[0], b3[0]))
        layer_output = both_sequences(y, y_far)
        encoded_gradient = both_sequences(eg, eg_far)
        input_gradient = both_sequences(dx, dx_far)
        s3 = jnp.concatenate([summed([a30] + a3[1:]), summed([b30] + b3[1:])], axis=-1)
        s2 = summed([z20] + z2[1:])
        s1 = summed(z1)
        small = s1[:, 3 * hd :]
        table_gradient = small[:heads, :NB]
        dgs = [small[:, NB + i] for i in range(3)]
        return (
            layer_output,
            input_gradient,
            encoded_gradient,
            table_gradient,
            s1[:, :hd],
            s1[:, hd : 2 * hd],
            s1[:, 2 * hd : 3 * hd],
            s2[:, :hd].T,
            s2[:, hd : 2 * hd],
            s2[:, 2 * hd : 3 * hd],
            s2[:, 3 * hd : 4 * hd],
            s2[:, 4 * hd :].T,
            s3[:, :ff],
            s3[:, ff : 2 * ff],
            s3[:, 2 * ff :].T,
            dgs[0],
            dgs[1],
            dgs[2],
        )

    return step


def solution(mesh):
    weight, turned, row, gain = P("dp", "mp"), P("mp", "dp"), P("dp", None), P("dp")
    weights = (weight, weight, weight, turned, weight, weight, weight, turned, weight, weight, turned)
    gains = (gain, gain, gain)
    return jax.shard_map(
        make(Grid(mesh.shape["dp"], mesh.shape["mp"])),
        mesh=mesh,
        in_specs=(row, row, row, P(), P("mp", None)) + weights + gains,
        out_specs=(row, row, row, P("mp", None)) + weights + gains,
        check_vma=False,
    )
```

```python
import jax
import jax.numpy as jnp
from jax import lax
from jax.experimental import pallas as pl
from jax.experimental.pallas import tpu as pltpu
from jax.sharding import PartitionSpec as P


DH = 64
NB = 32
L = 512
LANE = 128
QB = 128
EPS = 1e-06
NEG = -1e30
GELU_C = 0.7978845608028654
GELU_A = 0.044715
AXES = ("dp", "mp")
F32 = jnp.float32
BF16 = jnp.bfloat16
MIB = 1024 * 1024
VMEM_LIMIT = {"ka": 13, "kb": 16, "kca": 20, "kcb": 22, "kd1": 12, "kd2": 20, "ke1": 12, "ke2": 16}


def nn(left, right):
    return lax.dot_general(left, right, (((1,), (0,)), ((), ())), preferred_element_type=F32)


def nt(left, right):
    return lax.dot_general(left, right, (((1,), (1,)), ((), ())), preferred_element_type=F32)


class Grid:
    def __init__(self, n_dp, n_mp):
        assert n_mp == 2 and n_dp % 8 == 0
        self.n_dp, self.n_mp = n_dp, n_mp
        self.n_z = n_dp // 4

    def perm(self, move):
        pairs = []
        for z in range(self.n_z):
            for y in range(2):
                for c in range(2):
                    for m in range(2):
                        tz, ty, tc, tm = move(z, y, c, m)
                        pairs.append(
                            (
                                (((z * 2 + y) * 2) + c) * 2 + m,
                                (((tz * 2 + ty) * 2) + tc) * 2 + tm,
                            )
                        )
        return pairs

    def send(self, v, move):
        return lax.ppermute(v, AXES, self.perm(move))

    def swap_m(self, v):
        return self.send(v, lambda z, y, c, m: (z, y, c, 1 - m))

    def swap_y(self, v):
        return self.send(v, lambda z, y, c, m: (z, 1 - y, c, m))

    def swap_c(self, v):
        return self.send(v, lambda z, y, c, m: (z, y, 1 - c, m))

    def shift_z(self, v, d):
        n = self.n_z
        return self.send(v, lambda z, y, c, m: ((z + d) % n, y, c, m))


def place():
    dp = lax.axis_index("dp")
    return dp // 4, (dp // 2) % 2, dp % 2, lax.axis_index("mp")


def gather(grid, block):
    rows, cols = block.shape
    n = grid.n_z
    z, y, c, _ = place()
    got = [block] + [grid.shift_z(block, d) for d in range(1, n)]
    own = jnp.zeros((n, rows, cols), block.dtype)
    for d in range(n):
        own = lax.dynamic_update_slice(own, got[d][None], (lax.rem(z - d + n, n), 0, 0))
    half = n // 2
    by_m = grid.swap_m(own)
    by_y = grid.swap_y(own)
    part_a = by_m[:half]
    part_b = by_y[half:]
    diag_a = grid.swap_y(part_a)
    diag_b = grid.swap_m(part_b)
    pieces = [(own, 0, 0, 0), (by_y, 0, 1, 0), (by_m, 1, 0, 0), (diag_a, 1, 1, 0), (diag_b, 1, 1, half)]
    out = [(a, m, b, 0, j) for a, m, b, j in pieces]
    out += [(grid.swap_c(p[0]),) + p[1:3] + (1, p[3]) for p in pieces]
    if rows % 16 == 0:
        return out
    stacks = []
    for m in range(2):
        for b in range(2):
            for e in range(2):
                mine = sorted((p for p in out if p[1:4] == (m, b, e)), key=lambda p: p[4])
                stacks.append(jnp.concatenate([p[0] for p in mine], axis=0))
    whole = jnp.stack(stacks).reshape(2, 2, 2, n, rows, cols)
    whole = jnp.take(whole, jnp.arange(2) ^ y, axis=1)
    whole = jnp.take(whole, jnp.arange(2) ^ c, axis=2)
    whole = whole.transpose(0, 3, 1, 2, 4, 5).reshape(2, n * 4 * rows, cols)
    return [(whole[m], m, None, None, 0) for m in range(2)]


class Weights:
    def __init__(self, pieces, n_z, half=None):
        chosen = [p for p in pieces if half is None or p[1] == half]
        self.arrays = [p[0] for p in chosen]
        self.metas = [p[1:] for p in chosen]
        self.packed = self.metas[0][1] is None
        self.n_z = n_z
        self.rows = pieces[0][0].shape[1] if not self.packed else pieces[0][0].shape[0] // (4 * n_z)
        self.half = half

    def specs(self):
        return [(a, True) for a in self.arrays]

    def scratch(self, n, count=None):
        lead = () if count is None else (count,)
        if self.packed:
            return pltpu.VMEM(lead + (4 * self.n_z * self.rows, n), BF16)
        return pltpu.VMEM(lead + (self.n_z, 2, 2, self.rows, n), BF16)

    def sems(self, count=1):
        return pltpu.SemaphoreType.DMA((count * len(self.arrays),))

    def start(self, refs, dest, sems, src, n, at=0, slot=0):
        _, y, c, _ = place()
        copies = []
        for i, ((m, b, e, j), ref) in enumerate(zip(self.metas, refs)):
            to = pl.ds(at + (0 if self.half is not None else m * n), n)
            if self.packed:
                cp = pltpu.make_async_copy(ref.at[:, pl.ds(src, n)], dest.at[:, to], sems.at[slot * len(self.arrays) + i])
            else:
                k = ref.shape[0]
                cp = pltpu.make_async_copy(
                    ref.at[:, :, pl.ds(src, n)], dest.at[pl.ds(j, k), y ^ b, c ^ e, :, to], sems.at[slot * len(self.arrays) + i]
                )
            cp.start()
            copies.append(cp)
        return copies

    def value(self, dest, first, last):
        if self.packed:
            return dest[:, first:last]
        return dest[:, :, :, :, first:last].reshape(4 * self.n_z * self.rows, last - first)

    def columns(self, dest, first, size):
        if self.packed:
            return dest[:, pl.ds(first, size)]
        return dest[:, :, :, :, pl.ds(first, size)].reshape(4 * self.n_z * self.rows, size)


def wait(copies):
    for cp in copies:
        cp.wait()


def wait_for(turn, groups):
    for i, copies in enumerate(groups):

        @pl.when(turn == i)
        def _(copies=copies):
            wait(copies)


def rms(values, gain):
    return values * lax.rsqrt(jnp.mean(values * values, axis=-1, keepdims=True) + EPS) * gain


def rms_back(values, gain, back):
    scale = lax.rsqrt(jnp.mean(values * values, axis=-1, keepdims=True) + EPS)
    unit = values * scale
    incoming = back * gain
    grad = scale * (incoming - unit * jnp.mean(incoming * unit, axis=-1, keepdims=True))
    return grad, jnp.sum(back * unit, axis=0, keepdims=True)


def lane_masks():
    lane = lax.broadcasted_iota(jnp.int32, (1, LANE), 1)
    low = (lane < DH).astype(F32)
    return [low.astype(BF16), (1.0 - low).astype(BF16)]


def bias_strip(base):
    first = pltpu.roll(jnp.broadcast_to(base, (8, L)), 0, 1, stride=1, stride_axis=0)
    return jnp.concatenate([first] + [pltpu.roll(first, 8 * g, 1) for g in range(1, QB // 8)], axis=0)


def fold_band(band):
    total = band[0:8]
    for g in range(1, QB // 8):
        total = total + pltpu.roll(band[8 * g : 8 * g + 8], L - 8 * g, 1)
    row = lax.broadcasted_iota(jnp.int32, (8, L), 0)
    for bit in range(3):
        total = jnp.where(((row >> bit) & 1) == 1, pltpu.roll(total, L - (1 << bit), 1), total)
    return jnp.sum(total, axis=0, keepdims=True)


WIDE = 256


def masked_strip(base_ref, row):
    strip = bias_strip(base_ref[pl.ds(row, 1), :])
    at_row = lax.broadcasted_iota(jnp.int32, (QB, L), 0)
    at_col = lax.broadcasted_iota(jnp.int32, (QB, L), 1)
    return jnp.where(at_col >= at_row, strip, NEG)


def bias_tile(strip, first_key, keys, first_query):
    parts = []
    for k in range(first_key, first_key + keys, QB):
        lo = first_query - k
        if lo >= 0:
            parts.append(strip[:, lo : lo + WIDE])
        else:
            parts.append(jnp.concatenate([jnp.full((QB, -lo), NEG, F32), strip[:, : WIDE + lo]], axis=1))
    return jnp.concatenate(parts, axis=0)


def half_rows(turned):
    none = jnp.zeros_like(turned[:DH])
    return [jnp.concatenate([turned[:DH], none], axis=0), jnp.concatenate([none, turned[DH:]], axis=0)]


def attend_loop(q_ref, k_ref, v_ref, o_ref, lse_ref, base_ref):
    masks = lane_masks()
    causal = base_ref is not None

    def step(t, carry):
        at = pl.ds(pl.multiple_of(t * LANE, LANE), LANE)
        q, k, v = q_ref[:, at], k_ref[:, at], v_ref[:, at]
        vt = half_rows(v.T)
        outs = [None] * (L // WIDE)
        keys = [k * masks[hh] for hh in range(2)]
        strips = [masked_strip(base_ref, t * 2 + hh) if causal else None for hh in range(2)]
        order = [(hh, b) for b in range(L // WIDE) for hh in range(2)]

        def scores(hh, b):
            n = (b + 1) * WIDE if causal else k.shape[0]
            s = nt(keys[hh][:n], q[b * WIDE : (b + 1) * WIDE])
            return s + bias_tile(strips[hh], 0, n, b * WIDE) if causal else s

        ahead = scores(*order[0])
        for i, (hh, b) in enumerate(order):
            s = ahead
            if i + 1 < len(order):
                ahead = scores(*order[i + 1])
            top = jnp.max(s, axis=0, keepdims=True)
            e = jnp.exp(s - top)
            total = jnp.sum(e, axis=0, keepdims=True)
            mixed = nn(vt[hh][:, : s.shape[0]], e.astype(BF16)) * (1.0 / total)
            outs[b] = mixed if outs[b] is None else outs[b] + mixed
            lse_ref[pl.ds(t * 2 + hh, 1), b * WIDE : (b + 1) * WIDE] = top + jnp.log(total)
        o_ref[:, at] = jnp.concatenate(outs, axis=1).T.astype(BF16)
        return carry

    lax.fori_loop(0, q_ref.shape[1] // LANE, step, 0)


def attend_back_loop(q_ref, k_ref, v_ref, o_ref, do_ref, lse_ref, dq_ref, dk_ref, dv_ref, p_ref, ds_ref, base_ref, off_ref, band_ref):
    masks = lane_masks()
    causal = base_ref is not None
    blocks = L // WIDE

    def step(t, carry):
        at = pl.ds(pl.multiple_of(t * LANE, LANE), LANE)
        q, k, v, do = q_ref[:, at], k_ref[:, at], v_ref[:, at], do_ref[:, at]
        prod = (do.astype(F32) * o_ref[:, at].astype(F32)).T
        kt = half_rows(k.T)
        for hh in range(2):
            km, vm = k * masks[hh], v * masks[hh]
            lse = lse_ref[pl.ds(t * 2 + hh, 1), :]
            delta = jnp.sum(prod[hh * DH : (hh + 1) * DH], axis=0, keepdims=True)
            if causal:
                strip = masked_strip(base_ref, t * 2 + hh)
                band_ref[...] = jnp.zeros_like(band_ref)
            for b in range(blocks):
                cols = slice(b * WIDE, (b + 1) * WIDE)
                to = slice((b * 2 + hh) * WIDE, (b * 2 + hh + 1) * WIDE)
                for kb in range(b + 1 if causal else k.shape[0] // WIDE):
                    rows = slice(kb * WIDE, (kb + 1) * WIDE)
                    s = nt(km[rows], q[cols])
                    if causal:
                        s = s + bias_tile(strip, kb * WIDE, WIDE, b * WIDE)
                    prob = jnp.exp(s - lse[:, cols])
                    p_ref[rows, to] = prob.astype(BF16)
                    ds = prob * (nt(vm[rows], do[cols]) - delta[:, cols])
                    ds_ref[rows, to] = ds.astype(BF16)
                    if causal:
                        for i in range(WIDE // QB):
                            lo = b * WIDE - kb * WIDE - i * QB
                            part = ds[i * QB : (i + 1) * QB]
                            if lo < 0:
                                part, lo = part[:, -lo:], 0
                            band_ref[:, lo : lo + part.shape[1]] += part
            if causal:
                off_ref[pl.ds(t * 2 + hh, 1), :] = fold_band(band_ref[...])
        do2 = jnp.concatenate([do[b * WIDE : (b + 1) * WIDE] * masks[hh] for b in range(blocks) for hh in range(2)], axis=0)
        q2 = jnp.concatenate([q[b * WIDE : (b + 1) * WIDE] * masks[hh] for b in range(blocks) for hh in range(2)], axis=0)
        if causal:
            for kb in range(blocks):
                rows = slice(kb * WIDE, (kb + 1) * WIDE)
                dv_ref[rows, at] = nn(p_ref[rows, kb * 2 * WIDE :], do2[kb * 2 * WIDE :]).astype(BF16)
                dk_ref[rows, at] = nn(ds_ref[rows, kb * 2 * WIDE :], q2[kb * 2 * WIDE :]).astype(BF16)
        else:
            dv_ref[:, at] = nn(p_ref[...], do2).astype(BF16)
            dk_ref[:, at] = nn(ds_ref[...], q2).astype(BF16)
        dq = []
        for b in range(blocks):
            n = (b + 1) * WIDE if causal else k.shape[0]
            dq.append(
                sum(nn(kt[hh][:, :n], ds_ref[:n, (b * 2 + hh) * WIDE : (b * 2 + hh + 1) * WIDE]) for hh in range(2))
            )
        dq_ref[:, at] = jnp.concatenate(dq, axis=1).T.astype(BF16)
        return carry

    lax.fori_loop(0, q_ref.shape[1] // LANE, step, 0)


def call(body, outs, args, scratch, name, flops):
    return pl.pallas_call(
        body,
        out_shape=tuple(jax.ShapeDtypeStruct(s, d) for s, d in outs),
        in_specs=[pl.BlockSpec(memory_space=pltpu.HBM if far else pltpu.VMEM) for _, far in args],
        out_specs=tuple(pl.BlockSpec(memory_space=pltpu.VMEM) for _ in outs),
        scratch_shapes=scratch,
        compiler_params=pltpu.CompilerParams(vmem_limit_bytes=VMEM_LIMIT[name] * MIB),
        cost_estimate=pl.CostEstimate(flops=flops, transcendentals=0, bytes_accessed=10_000_000),
    )(*[pltpu.with_memory_space_constraint(a, pltpu.HBM) if far else a for a, far in args])


def sequence_copy(ref, dest, sem):
    m = lax.axis_index("mp")
    cp = pltpu.make_async_copy(ref.at[pl.ds(pl.multiple_of(m * L, L), L), :], dest, sem)
    cp.start()
    return cp


def near(*arrays):
    return [(a, False) for a in arrays]


class Parts:
    def __init__(self, grid, d, cols, halves):
        self.n = grid.n_z
        self.rows = d // (4 * self.n)
        self.sorted = self.rows % 16 == 0
        self.d, self.cols, self.halves = d, cols, halves

    def outs(self):
        lead = (2,) if self.halves else ()
        if self.sorted:
            return [(lead + (2, self.n, self.rows, self.cols), BF16)] * 2
        return [(lead + (self.d, self.cols), BF16)]

    def count(self):
        return 2 if self.sorted else 1

    def put(self, refs, half, at, value):
        low = value.astype(BF16)
        size = low.shape[1]
        cols = pl.ds(at, size)
        if not self.sorted:
            if half is None:
                refs[0][:, cols] = low
            else:
                refs[0][half, :, cols] = low
            return
        z, y, c, _ = place()
        low = low.reshape(self.n, 2, 2, self.rows, size)
        for i in range(self.n):
            for b in range(2):
                first, second = low[i, b, 0], low[i, b, 1]
                where = (b ^ y, lax.rem(i - z + self.n, self.n), slice(None), cols)
                if half is not None:
                    where = (half,) + where
                refs[0][where] = lax.select(c == 0, first, second)
                refs[1][where] = lax.select(c == 0, second, first)

    def put_halves(self, refs, at, n, value):
        self.put(refs, 0, at, value[:, :n])
        self.put(refs, 1, at, value[:, n:])

    def split(self, arrays):
        if self.sorted:
            return arrays
        z, y, c, _ = place()
        v = arrays[0]
        v = v.reshape(v.shape[:-2] + (self.n, 2, 2, self.rows, self.cols))
        lead = v.ndim - 5
        v = jnp.moveaxis(v, (lead + 2, lead + 1, lead), (0, lead + 1, lead + 2))
        v = jnp.take(v, (z + jnp.arange(self.n)) % self.n, axis=lead + 2)
        v = jnp.take(v, jnp.arange(2) ^ y, axis=lead + 1)
        v = jnp.take(v, jnp.arange(2) ^ c, axis=0)
        return v[0], v[1]


DMA = pltpu.SemaphoreType.DMA


def self_forward(grid, inputs, base_hot, pieces, d, hd, heads):
    ws = Weights(pieces, grid.n_z)
    k = len(ws.arrays)
    w2 = 2 * hd

    def body(*refs):
        x_ref, hot_ref = refs[:2]
        w_refs = refs[2 : 2 + k]
        n1_ref, qkv_ref, o_ref, gain_ref, base_ref, lse_ref = refs[2 + k : 8 + k]
        x_v, we, w, sem_x, s_e, s_w = refs[8 + k :]
        cx = sequence_copy(x_ref, x_v, sem_x)
        ce = ws.start(w_refs, we, s_e, 3 * hd, LANE)
        cw = [ws.start(w_refs, w.at[g], s_w, g * hd, hd, slot=g) for g in range(3)]
        cx.wait()
        x = x_v[...].astype(F32)
        scaled = x * lax.rsqrt(jnp.mean(x * x, axis=-1, keepdims=True) + EPS)
        wait(ce)
        extra = ws.value(we, 0, 2 * LANE)
        rows = ws.rows
        shards = d // rows
        column = lax.broadcasted_iota(jnp.int32, (3 * shards, d), 1)
        row = lax.broadcasted_iota(jnp.int32, (3 * shards, d), 0)
        wanted = lax.rem(row, shards) * rows + heads + row // shards
        packed = nn((column == wanted).astype(F32).astype(BF16), extra[:, :LANE]).astype(BF16)
        lane = lax.broadcasted_iota(jnp.int32, (LANE, d), 0)
        column = lax.broadcasted_iota(jnp.int32, (LANE, d), 1)
        wide = nn(packed, (lane == lax.rem(column, rows)).astype(F32).astype(BF16))
        column = lax.broadcasted_iota(jnp.int32, (shards, d), 1)
        mine = column // rows == lax.broadcasted_iota(jnp.int32, (shards, d), 0)
        gains = [
            jnp.sum(jnp.where(mine, wide[i * shards : (i + 1) * shards], 0.0), axis=0, keepdims=True) for i in range(3)
        ]
        gains = jnp.concatenate(gains + [jnp.zeros((5, d), F32)], axis=0)
        gain_ref[...] = gains
        lse_ref[...] = jnp.zeros_like(lse_ref)
        base_ref[...] = jnp.zeros_like(base_ref)
        for a in range(2):
            base_ref[a * heads : (a + 1) * heads, :] = nn(extra[0:16, a * LANE : (a + 1) * LANE], hot_ref[...])[:heads]
        n1_ref[...] = (scaled * gains[0:1]).astype(BF16)

        def project(g, carry):
            wait_for(g, cw)
            qkv_ref[g] = nn(n1_ref[...], ws.value(w.at[g], 0, w2)).astype(BF16)
            return carry

        lax.fori_loop(0, 3, project, 0)
        attend_loop(qkv_ref.at[0], qkv_ref.at[1], qkv_ref.at[2], o_ref, lse_ref, base_ref)

    row = ((L, w2), BF16)
    return call(
        body,
        [((L, d), BF16), ((3, L, w2), BF16), row, ((8, d), F32), ((16, L), F32), ((16, L), F32)],
        [(inputs, True), (base_hot, False)] + ws.specs(),
        [
            pltpu.VMEM((L, d), BF16),
            ws.scratch(2 * LANE),
            ws.scratch(w2, 3),
            DMA,
            ws.sems(),
            ws.sems(3),
        ],
        "ka",
        3_000_000_000,
    )


def cross_forward(grid, inputs, encoded, attn_one, gains, pieces, d, hd):
    ws = Weights(pieces, grid.n_z)
    k = len(ws.arrays)
    w2 = 2 * hd

    def body(*refs):
        x_ref, enc_ref, a1_ref, gain_ref = refs[:4]
        w_refs = refs[4 : 4 + k]
        r1_ref, r2_ref, n2_ref, qkv_ref, o_ref, n3_ref, lse_ref = refs[4 + k : 11 + k]
        x_v, enc_v, w, sem_x, sem_e, s_w = refs[11 + k :]
        ce = sequence_copy(enc_ref, enc_v, sem_e)
        cw = {g: ws.start(w_refs, w.at[g], s_w, g * hd, hd, slot=g) for g in (2, 3)}
        cx = sequence_copy(x_ref, x_v, sem_x)
        cw.update({g: ws.start(w_refs, w.at[g], s_w, g * hd, hd, slot=g) for g in (0, 1, 4)})
        ce.wait()

        def project(g, carry):
            wait_for(g, [cw[2], cw[3]])
            qkv_ref[g + 1] = nn(enc_v[...], ws.value(w.at[g + 2], 0, w2)).astype(BF16)
            return carry

        lax.fori_loop(0, 2, project, 0)
        cx.wait()
        wait(cw[0])
        wait(cw[1])

        def resume(t, carry):
            rows = pl.ds(pl.multiple_of(t * WIDE, WIDE), WIDE)
            r1 = x_v[rows, :].astype(F32) + nt(a1_ref[rows, :], ws.value(w.at[0], 0, w2))
            r1_ref[rows, :] = r1
            n2 = rms(r1, gain_ref[1:2, :]).astype(BF16)
            n2_ref[rows, :] = n2
            qkv_ref[0, rows, :] = nn(n2, ws.value(w.at[1], 0, w2)).astype(BF16)
            return carry

        lax.fori_loop(0, L // WIDE, resume, 0)
        lse_ref[...] = jnp.zeros_like(lse_ref)
        attend_loop(qkv_ref.at[0], qkv_ref.at[1], qkv_ref.at[2], o_ref, lse_ref, None)
        wait(cw[4])

        def close(t, carry):
            rows = pl.ds(pl.multiple_of(t * WIDE, WIDE), WIDE)
            r2 = r1_ref[rows, :] + nt(o_ref[rows, :], ws.value(w.at[4], 0, w2))
            r2_ref[rows, :] = r2
            n3_ref[rows, :] = rms(r2, gain_ref[2:3, :]).astype(BF16)
            return carry

        lax.fori_loop(0, L // WIDE, close, 0)

    row = ((L, w2), BF16)
    wide = ((L, d), BF16)
    return call(
        body,
        [((L, d), F32), ((L, d), F32), wide, ((3, L, w2), BF16), row, wide, ((16, L), F32)],
        [(inputs, True), (encoded, True)] + near(attn_one, gains) + ws.specs(),
        [
            pltpu.VMEM((L, d), BF16),
            pltpu.VMEM((L, d), BF16),
            ws.scratch(w2, 5),
            DMA,
            DMA,
            ws.sems(5),
        ],
        "kb",
        5_000_000_000,
    )


def feed_forward(grid, cotangent, n3, r2, gains, carried, pieces, half, d, ff):
    ws = Weights(pieces, grid.n_z, half)
    k = len(ws.arrays)
    tile = min(256, ff)
    last = carried is not None
    extra_in = 4 if last else 0
    parts = Parts(grid, d, 3 * ff, False)
    ng = parts.count()

    def body(*refs):
        cot_ref, n3_ref = refs[:2]
        w_refs = refs[2 + extra_in : 2 + extra_in + k]
        rest = refs[2 + extra_in + k :]
        if last:
            r2_ref, gain_ref, yin_ref, bin_ref = refs[2:6]
            y_ref, b2_ref, dg_ref, y_acc, b3_acc = rest[ng : ng + 5]
        else:
            y_acc, b3_acc = rest[ng : ng + 2]
        g_refs, rest = rest[:ng], rest[ng + (5 if last else 2) :]
        cot_v, wg, wu, wd, turned, lows, sem_c, s_g, s_u, s_d = rest
        cc = sequence_copy(cot_ref, cot_v, sem_c)
        cg = ws.start(w_refs, wg, s_g, 0, ff)
        cu = ws.start(w_refs, wu, s_u, ff, ff)
        cd = ws.start(w_refs, wd, s_d, 2 * ff, ff)
        if last:
            y_acc[...] = r2_ref[...] + yin_ref[...]
            b3_acc[...] = bin_ref[...]
        else:
            y_acc[...] = jnp.zeros_like(y_acc)
            b3_acc[...] = jnp.zeros_like(b3_acc)
        turned[0] = n3_ref[...].T
        cc.wait()
        turned[1] = cot_v[...].T
        wait(cg)
        wait(cu)
        wait(cd)

        def step(t, carry):
            at = pl.multiple_of(t * tile, LANE)
            gate, upw, down = ws.columns(wg, at, tile), ws.columns(wu, at, tile), ws.columns(wd, at, tile)
            u = nn(n3_ref[...], gate)
            up = nn(n3_ref[...], upw)
            bh = nn(cot_v[...], down)
            sq = u * u
            th = jnp.tanh(GELU_C * (u + GELU_A * (sq * u)))
            both = 0.5 * (1.0 + th)
            gelu = u * both
            slope = both + 0.5 * u * (1.0 - th * th) * (GELU_C * (1.0 + (3.0 * GELU_A) * sq))
            lows[2] = (gelu * up).astype(BF16)
            lows[0] = (bh * up * slope).astype(BF16)
            lows[1] = (bh * gelu).astype(BF16)
            y_acc[...] += nt(lows[2], down)
            b3_acc[...] += nt(lows[0], gate) + nt(lows[1], upw)

            def weight(g, inner):
                parts.put(g_refs, None, pl.multiple_of(g * ff + at, LANE), nn(turned[g // 2], lows[g]))
                return inner

            lax.fori_loop(0, 3, weight, 0)
            return carry

        lax.fori_loop(0, ff // tile, step, 0)
        if last:
            dg_ref[...] = jnp.zeros_like(dg_ref)

            def finish(t, carry):
                rows = pl.ds(pl.multiple_of(t * QB, QB), QB)
                y_ref[rows, :] = y_acc[rows, :].astype(BF16)
                grad, dg = rms_back(r2_ref[rows, :], gain_ref[2:3, :], b3_acc[rows, :])
                b2_ref[rows, :] = cot_v[rows, :].astype(F32) + grad
                dg_ref[...] += dg
                return carry

            lax.fori_loop(0, L // QB, finish, 0)

    full = ((L, d), F32)
    outs = parts.outs()
    outs += [((L, d), BF16), full, ((1, d), F32)] if last else [full, full]
    scratch = [pltpu.VMEM((L, d), F32), pltpu.VMEM((L, d), F32)] if last else []
    result = call(
        body,
        outs,
        [(cotangent, True)] + near(n3) + (near(r2, gains, *carried) if last else []) + ws.specs(),
        scratch
        + [
            pltpu.VMEM((L, d), BF16),
            ws.scratch(ff),
            ws.scratch(ff),
            ws.scratch(ff),
            pltpu.VMEM((2, d, L), BF16),
            pltpu.VMEM((3, L, tile), BF16),
            DMA,
            ws.sems(),
            ws.sems(),
            ws.sems(),
        ],
        "kcb" if last else "kca",
        7_500_000_000,
    )
    return parts.split(result[:ng]), result[ng:]


def attention_backward(grid, back, qkv, attn, lse, base, pieces, first_col, hd, name):
    ws = Weights(pieces, grid.n_z)
    n = len(ws.arrays)
    w2 = 2 * hd
    causal = base is not None

    def body(*refs):
        b_ref, qkv_ref, o_ref, lse_ref = refs[:4]
        base_ref = refs[4] if causal else None
        refs = refs[5 if causal else 4 :]
        w_refs = refs[:n]
        out_ref = refs[n]
        off_ref = refs[n + 1] if causal else None
        wo, do, p_ref, ds_ref, band_ref, s_o = refs[-6:]
        co = ws.start(w_refs, wo, s_o, first_col, hd)
        if causal:
            off_ref[...] = jnp.zeros_like(off_ref)
        low = b_ref[...].astype(BF16)
        wait(co)
        do[...] = nn(low, ws.value(wo, 0, w2)).astype(BF16)
        attend_back_loop(
            qkv_ref.at[0],
            qkv_ref.at[1],
            qkv_ref.at[2],
            o_ref,
            do,
            lse_ref,
            out_ref.at[0],
            out_ref.at[1],
            out_ref.at[2],
            p_ref,
            ds_ref,
            base_ref,
            off_ref,
            band_ref,
        )

    return call(
        body,
        [((3, L, w2), BF16)] + ([((16, L), F32)] if causal else []),
        near(back, qkv, attn, lse) + (near(base) if causal else []) + ws.specs(),
        [
            ws.scratch(w2),
            pltpu.VMEM((L, w2), BF16),
            pltpu.VMEM((L, 2 * L), BF16),
            pltpu.VMEM((L, 2 * L), BF16),
            pltpu.VMEM((QB, L), F32),
            ws.sems(),
        ],
        name,
        3_000_000_000,
    )


def cross_finish(grid, encoded, b2, r1, n2, grads, attn_one, attn_two, gains, pieces, d, hd):
    ws = Weights(pieces, grid.n_z)
    k = len(ws.arrays)
    w2 = 2 * hd
    parts = Parts(grid, d, 5 * hd, True)
    ng = parts.count()

    def body(*refs):
        enc_ref, b2_ref, r1_ref, n2_ref, dy_ref, a1_ref, a2_ref, gain_ref = refs[:8]
        w_refs = refs[8 : 8 + k]
        b1_ref, eg_ref, dg_ref = refs[8 + k : 11 + k]
        g_refs = refs[11 + k : 11 + k + ng]
        enc_v, w, turned, right, sem_e, s_w = refs[11 + k + ng :]
        ce = sequence_copy(enc_ref, enc_v, sem_e)
        cw = [ws.start(w_refs, w.at[g], s_w, (g + 1) * hd, hd, slot=g) for g in range(3)]
        turned[3] = b2_ref[...].astype(BF16).T
        right[1] = a2_ref[...]
        right[0] = a1_ref[...]
        turned[0] = n2_ref[...].T
        wait(cw[0])
        dg_ref[...] = jnp.zeros_like(dg_ref)

        def resume(t, carry):
            rows = pl.ds(pl.multiple_of(t * WIDE, WIDE), WIDE)
            grad, dg = rms_back(r1_ref[rows, :], gain_ref[1:2, :], nt(dy_ref[0, rows, :], ws.value(w.at[0], 0, w2)))
            dg_ref[...] += dg
            b1_ref[rows, :] = b2_ref[rows, :] + grad
            return carry

        lax.fori_loop(0, L // WIDE, resume, 0)
        turned[2] = b1_ref[...].astype(BF16).T
        ce.wait()
        turned[1] = enc_v[...].T

        def inner(g, carry):
            parts.put_halves(g_refs, pl.multiple_of((g + 1) * hd, LANE), hd, nn(turned[jnp.minimum(g, 1)], dy_ref[g]))
            return carry

        lax.fori_loop(0, 3, inner, 0)

        def outer(g, carry):
            parts.put_halves(g_refs, pl.multiple_of(g * 4 * hd, LANE), hd, nn(turned[2 + g], right[g]))
            return carry

        lax.fori_loop(0, 2, outer, 0)
        wait(cw[1])
        wait(cw[2])

        def encoder(t, carry):
            rows = pl.ds(pl.multiple_of(t * WIDE, WIDE), WIDE)
            eg = nt(dy_ref[1, rows, :], ws.value(w.at[1], 0, w2)) + nt(dy_ref[2, rows, :], ws.value(w.at[2], 0, w2))
            eg_ref[rows, :] = eg.astype(BF16)
            return carry

        lax.fori_loop(0, L // WIDE, encoder, 0)

    result = call(
        body,
        [((L, d), F32), ((L, d), BF16), ((1, d), F32)] + parts.outs(),
        [(encoded, True)] + near(b2, r1, n2, grads, attn_one, attn_two, gains) + ws.specs(),
        [
            pltpu.VMEM((L, d), BF16),
            ws.scratch(w2, 3),
            pltpu.VMEM((4, d, L), BF16),
            pltpu.VMEM((2, L, w2), BF16),
            DMA,
            ws.sems(3),
        ],
        "kd2",
        5_000_000_000,
    )
    return result[:3], parts.split(result[3:])


def self_finish(grid, inputs, b1, n1, grads, off, dg2, dg3, base_hot, gains, pieces, d, hd, heads):
    ws = Weights(pieces, grid.n_z)
    k = len(ws.arrays)
    w2 = 2 * hd
    parts = Parts(grid, d, 3 * hd + LANE, True)
    ng = parts.count()

    def body(*refs):
        x_ref, b1_ref, n1_ref, dy_ref, off_ref, dg2_ref, dg3_ref, hot_ref, gain_ref = refs[:9]
        w_refs = refs[9 : 9 + k]
        dx_ref = refs[9 + k]
        g_refs = refs[10 + k : 10 + k + ng]
        x_v, w, turned, back, sem_x, s_w = refs[10 + k + ng :]
        cw = [ws.start(w_refs, w.at[g], s_w, g * hd, hd, slot=g) for g in range(3)]
        cx = sequence_copy(x_ref, x_v, sem_x)
        turned[...] = n1_ref[...].T
        back[...] = jnp.zeros_like(back)

        def inner(g, carry):
            parts.put_halves(g_refs, pl.multiple_of(g * hd, LANE), hd, nn(turned[...], dy_ref[g]))
            wait_for(g, cw)
            back[...] += nt(dy_ref[g], ws.value(w.at[g], 0, w2))
            return carry

        lax.fori_loop(0, 3, inner, 0)
        cx.wait()
        grad, dg = rms_back(x_v[...].astype(F32), gain_ref[0:1, :], back[...])
        dx_ref[...] = (b1_ref[...] + grad).astype(BF16)
        dgs = jnp.concatenate([dg, dg2_ref[...], dg3_ref[...], jnp.zeros((5, d), F32)], axis=0)
        columns = jnp.concatenate([jnp.zeros((NB, d), F32), dgs, jnp.zeros((LANE - NB - 8, d), F32)], axis=0).T
        hot = hot_ref[...]
        sums = off_ref[...]
        table = jnp.zeros((16, LANE), F32)
        for _ in range(3):
            low = sums.astype(BF16)
            table = table + nt(low, hot)
            sums = sums - low.astype(F32)
        table = table.astype(BF16)
        shard_row = lax.rem(lax.broadcasted_iota(jnp.int32, (d, 16), 0), parts.rows)
        column = lax.broadcasted_iota(jnp.int32, (d, 16), 1)
        for a in range(2):
            spread = ((shard_row + a * heads == column) & (shard_row < heads)).astype(F32).astype(BF16)
            parts.put(g_refs, a, 3 * hd, nn(spread, table) + columns)

    result = call(
        body,
        [((L, d), BF16)] + parts.outs(),
        [(inputs, True)] + near(b1, n1, grads, off, dg2, dg3, base_hot, gains) + ws.specs(),
        [
            pltpu.VMEM((L, d), BF16),
            ws.scratch(w2, 3),
            pltpu.VMEM((d, L), BF16),
            pltpu.VMEM((L, d), F32),
            DMA,
            ws.sems(3),
        ],
        "ke2",
        4_000_000_000,
    )
    return result[0], parts.split(result[1:])


def added(left, right):
    return (left.astype(F32) + right.astype(F32)).astype(BF16)


def scatter(grid, own, own_got, other, other_got, first, held=None):
    sent_a = added(other[..., :first], other_got[..., :first])
    sent_b = jnp.stack([added(v[1, ..., first:], g[1, ..., first:]) for v, g in ((own, own_got), (other, other_got))])
    if held is not None:
        sent_a, sent_b, held = lax.optimization_barrier((sent_a, sent_b, held))
    got = grid.swap_m(sent_a)
    got_b = grid.swap_y(sent_b)

    def a_sum(i):
        return added3(own[i, ..., :first], own_got[i, ..., :first], got[i])

    far_a = grid.swap_y(a_sum(1))
    far_b = grid.swap_m(added3(other[0, ..., first:], other_got[0, ..., first:], got_b[1]))
    wa, wb = a_sum(0), added3(own[0, ..., first:], own_got[0, ..., first:], got_b[0])
    return (wa, wb), (far_a, far_b), held


def joined(kept, far):
    return [
        jnp.concatenate([added(v[d], f[d]) for v, f in zip(kept, far)], axis=-1) for d in range(kept[0].shape[0])
    ]


def scatter_wide(grid, own, own_got, other, other_got, first):
    n = grid.n_z
    got_own = grid.swap_y(added(own[1, ..., first:], own_got[1, ..., first:]))
    got_other = grid.swap_y(added(other[1, ..., first:], other_got[1, ..., first:]))
    got = grid.swap_m(added(other[..., :first], other_got[..., :first]))

    def a_sum(i):
        return added3(own[i, ..., :first], own_got[i, ..., :first], got[i])

    far_a = grid.swap_y(a_sum(1))
    wa = a_sum(0)
    parts = []
    for v, g, far in ((own, own_got, got_own), (other, other_got, got_other)):
        w = [added3(v[0, d, :, first:], g[0, d, :, first:], far[d]) for d in range(n)]
        parts.append([w[0]] + [grid.shift_z(w[d], d) for d in range(1, n)])
    a = [added(wa[d], far_a[d]) for d in range(n)]
    a = [a[0]] + [grid.shift_z(a[d], d) for d in range(1, n)]
    return a, parts[0], parts[1]


def settle(grid, w, gate=None):
    sent = w[1:]
    if gate is not None:
        sent, gate = lax.optimization_barrier((sent, gate))
    return [w[0]] + [grid.shift_z(v, d + 1) for d, v in enumerate(sent)], gate


def summed(arrays):
    out = arrays[0].astype(F32)
    for v in arrays[1:]:
        out = out + v.astype(F32)
    return out


def added3(a, b, c):
    return (a.astype(F32) + b.astype(F32) + c.astype(F32)).astype(BF16)


def both_sequences(mine, other):
    first = lax.axis_index("mp") == 0
    low = jnp.where(first, mine, other)
    high = jnp.where(first, other, mine)
    return jnp.concatenate([low, high], axis=0).astype(F32)


def make(grid):
    def step(
        inputs,
        encoded,
        cotangent,
        buckets,
        rel_table,
        query_self,
        keys_self,
        values_self,
        output_self,
        query_cross,
        keys_cross,
        values_cross,
        output_cross,
        gate_weight,
        up_weight,
        down_weight,
        gain_first,
        gain_second,
        gain_third,
    ):
        d = inputs.shape[1]
        hd = query_self.shape[1]
        ff = gate_weight.shape[1]
        rows = query_self.shape[0]
        heads = rel_table.shape[0]
        assert inputs.shape[0] == 2 * L and heads + 3 <= rows <= LANE and heads <= 8
        extra = jnp.concatenate(
            [
                jnp.pad(rel_table, ((0, 0), (0, LANE - NB))),
                jnp.pad(jnp.stack([gain_first, gain_second, gain_third]), ((0, rows - heads - 3), (0, LANE - rows))),
            ],
            axis=0,
        )
        group_one = jnp.concatenate([query_self, keys_self, values_self, extra], axis=1)
        group_two = jnp.concatenate([output_self.T, query_cross, keys_cross, values_cross, output_cross.T], axis=1)
        group_three = jnp.concatenate([gate_weight, up_weight, down_weight.T], axis=1)
        pieces_one = gather(grid, group_one)
        pieces_two = gather(grid, group_two)
        pieces_three = gather(grid, group_three)

        base_hot = (buckets[None, :] == lax.broadcasted_iota(jnp.int32, (LANE, L), 0)).astype(BF16)

        n1, qkv1, at1, gains, base, lse1 = self_forward(grid, inputs, base_hot, pieces_one, d, hd, heads)
        r1, r2, n2, qkv2, at2, n3, lse2 = cross_forward(grid, inputs, encoded, at1, gains, pieces_two, d, hd)
        (own3, gone), (ya, ba) = feed_forward(grid, cotangent, n3, r2, gains, None, pieces_three, 0, d, ff)
        own3_got = grid.swap_c(gone)
        (other3, gone), (y, b2, dg3) = feed_forward(
            grid, cotangent, n3, r2, gains, (ya, ba), pieces_three, 1, d, ff
        )
        other3_got = grid.swap_c(gone)
        y_far = grid.swap_m(y)
        a3, bo3, bt3 = scatter_wide(grid, own3, own3_got, other3, other3_got, ff * 5 // 4 // LANE * LANE)
        (dy,) = attention_backward(grid, b2, qkv2, at2, lse2, None, pieces_two, 4 * hd, hd, "kd1")
        (b1, eg, dg2), (kept, gone) = cross_finish(
            grid, encoded, b2, r1, n2, dy, at1, at2, gains, pieces_two, d, hd
        )
        eg_far = grid.swap_m(eg)
        got = grid.swap_c(gone)
        kept2, far2, _ = scatter(grid, kept[0], got[0], kept[1], got[1], 7 * LANE)
        dy, off = attention_backward(grid, b1, qkv1, at1, lse1, base, pieces_two, 0, hd, "ke1")
        dx, (kept, gone) = self_finish(
            grid, inputs, b1, n1, dy, off, dg2, dg3, base_hot, gains, pieces_one, d, hd, heads
        )
        got = grid.swap_c(gone)
        kept1, far1, (kept2, bt30, y, eg) = scatter(
            grid, kept[0], got[0], kept[1], got[1], 5 * LANE, (kept2, bt3[0], y, eg)
        )
        b3 = bo3 + [grid.swap_m(summed([bt30] + bt3[1:]).astype(BF16))]
        z2, _ = settle(grid, joined(kept2, far2))
        w1 = joined(kept1, far1)
        dx_far = grid.swap_m(dx)
        z1, (z20, a30, b30) = settle(grid, w1, (z2[0], a3[0], b3[0]))
        layer_output = both_sequences(y, y_far)
        encoded_gradient = both_sequences(eg, eg_far)
        input_gradient = both_sequences(dx, dx_far)
        s3 = jnp.concatenate([summed([a30] + a3[1:]), summed([b30] + b3[1:])], axis=-1)
        s2 = summed([z20] + z2[1:])
        s1 = summed(z1)
        small = s1[:, 3 * hd :]
        table_gradient = small[:heads, :NB]
        dgs = [small[:, NB + i] for i in range(3)]
        return (
            layer_output,
            input_gradient,
            encoded_gradient,
            table_gradient,
            s1[:, :hd],
            s1[:, hd : 2 * hd],
            s1[:, 2 * hd : 3 * hd],
            s2[:, :hd].T,
            s2[:, hd : 2 * hd],
            s2[:, 2 * hd : 3 * hd],
            s2[:, 3 * hd : 4 * hd],
            s2[:, 4 * hd :].T,
            s3[:, :ff],
            s3[:, ff : 2 * ff],
            s3[:, 2 * ff :].T,
            dgs[0],
            dgs[1],
            dgs[2],
        )

    return step


def solution(mesh):
    weight, turned, row, gain = P("dp", "mp"), P("mp", "dp"), P("dp", None), P("dp")
    weights = (weight, weight, weight, turned, weight, weight, weight, turned, weight, weight, turned)
    gains = (gain, gain, gain)
    return jax.shard_map(
        make(Grid(mesh.shape["dp"], mesh.shape["mp"])),
        mesh=mesh,
        in_specs=(row, row, row, P(), P("mp", None)) + weights + gains,
        out_specs=(row, row, row, P("mp", None)) + weights + gains,
        check_vma=False,
    )
```

```python
import jax
import jax.numpy as jnp
from jax import lax
from jax.experimental import pallas as pl
from jax.experimental.pallas import tpu as pltpu
from jax.sharding import PartitionSpec as P


DH = 64
NB = 32
L = 512
LANE = 128
QB = 128
EPS = 1e-06
NEG = -1e30
GELU_C = 0.7978845608028654
GELU_A = 0.044715
AXES = ("dp", "mp")
F32 = jnp.float32
BF16 = jnp.bfloat16
MIB = 1024 * 1024
VMEM_LIMIT = {"ka": 13, "kb": 16, "kca": 23, "kcb": 25, "kd1": 12, "kd2": 22, "ke1": 12, "ke2": 16}


def nn(left, right):
    return lax.dot_general(left, right, (((1,), (0,)), ((), ())), preferred_element_type=F32)


def nt(left, right):
    return lax.dot_general(left, right, (((1,), (1,)), ((), ())), preferred_element_type=F32)


class Grid:
    def __init__(self, n_dp, n_mp):
        assert n_mp == 2 and n_dp % 8 == 0
        self.n_dp, self.n_mp = n_dp, n_mp
        self.n_z = n_dp // 4

    def perm(self, move):
        pairs = []
        for z in range(self.n_z):
            for y in range(2):
                for c in range(2):
                    for m in range(2):
                        tz, ty, tc, tm = move(z, y, c, m)
                        pairs.append(
                            (
                                (((z * 2 + y) * 2) + c) * 2 + m,
                                (((tz * 2 + ty) * 2) + tc) * 2 + tm,
                            )
                        )
        return pairs

    def send(self, v, move):
        return lax.ppermute(v, AXES, self.perm(move))

    def swap_m(self, v):
        return self.send(v, lambda z, y, c, m: (z, y, c, 1 - m))

    def swap_y(self, v):
        return self.send(v, lambda z, y, c, m: (z, 1 - y, c, m))

    def swap_c(self, v):
        return self.send(v, lambda z, y, c, m: (z, y, 1 - c, m))

    def shift_z(self, v, d):
        n = self.n_z
        return self.send(v, lambda z, y, c, m: ((z + d) % n, y, c, m))


def place():
    dp = lax.axis_index("dp")
    return dp // 4, (dp // 2) % 2, dp % 2, lax.axis_index("mp")


def gather(grid, block):
    rows, cols = block.shape
    n = grid.n_z
    z, y, c, _ = place()
    got = [block] + [grid.shift_z(block, d) for d in range(1, n)]
    own = jnp.zeros((n, rows, cols), block.dtype)
    for d in range(n):
        own = lax.dynamic_update_slice(own, got[d][None], (lax.rem(z - d + n, n), 0, 0))
    half = n // 2
    by_m = grid.swap_m(own)
    by_y = grid.swap_y(own)
    part_a = by_m[:half]
    part_b = by_y[half:]
    diag_a = grid.swap_y(part_a)
    diag_b = grid.swap_m(part_b)
    pieces = [(own, 0, 0, 0), (by_y, 0, 1, 0), (by_m, 1, 0, 0), (diag_a, 1, 1, 0), (diag_b, 1, 1, half)]
    out = [(a, m, b, 0, j) for a, m, b, j in pieces]
    out += [(grid.swap_c(p[0]),) + p[1:3] + (1, p[3]) for p in pieces]
    if rows % 16 == 0:
        return out
    stacks = []
    for m in range(2):
        for b in range(2):
            for e in range(2):
                mine = sorted((p for p in out if p[1:4] == (m, b, e)), key=lambda p: p[4])
                stacks.append(jnp.concatenate([p[0] for p in mine], axis=0))
    whole = jnp.stack(stacks).reshape(2, 2, 2, n, rows, cols)
    whole = jnp.take(whole, jnp.arange(2) ^ y, axis=1)
    whole = jnp.take(whole, jnp.arange(2) ^ c, axis=2)
    whole = whole.transpose(0, 3, 1, 2, 4, 5).reshape(2, n * 4 * rows, cols)
    return [(whole[m], m, None, None, 0) for m in range(2)]


def gather_late(grid, block):
    rows, cols = block.shape
    n = grid.n_z
    z, y, c, _ = place()
    by_m = grid.swap_m(block)
    by_y = grid.swap_y(block)
    diag = grid.send(block, lambda z, y, c, m: (z, 1 - y, c, 1 - m))
    own = jnp.stack([block, by_y, by_m, diag]).reshape(2, 2, rows, cols)
    mine = jnp.stack([own] + [grid.shift_z(own, d) for d in range(1, n)])
    other = grid.swap_c(mine)
    if rows % 16 == 0:
        return [(mine, "late", 0), (other, "late", 1)]
    whole = jnp.stack([mine, other])
    whole = jnp.take(whole, (z - jnp.arange(n)) % n, axis=1)
    whole = jnp.take(whole, jnp.arange(2) ^ y, axis=3)
    whole = jnp.take(whole, jnp.arange(2) ^ c, axis=0)
    whole = whole.transpose(2, 1, 3, 0, 4, 5).reshape(2, n * 4 * rows, cols)
    return [(whole[m], m, None, None, 0) for m in range(2)]


class Weights:
    def __init__(self, pieces, n_z, half=None):
        chosen = [p for p in pieces if half is None or p[1] in (half, "late")]
        self.arrays = [p[0] for p in chosen]
        self.metas = [p[1:] for p in chosen]
        self.late = self.metas[0][0] == "late"
        self.packed = not self.late and self.metas[0][1] is None
        self.n_z = n_z
        self.rows = pieces[0][0].shape[-2] if not self.packed else pieces[0][0].shape[0] // (4 * n_z)
        self.half = half
        self.each = len(self.arrays) * (2 * n_z if self.late else 1)

    def specs(self):
        return [(a, True) for a in self.arrays]

    def scratch(self, n, count=None):
        lead = () if count is None else (count,)
        if self.packed:
            return pltpu.VMEM(lead + (4 * self.n_z * self.rows, n), BF16)
        return pltpu.VMEM(lead + (self.n_z, 2, 2, self.rows, n), BF16)

    def sems(self, count=1):
        return pltpu.SemaphoreType.DMA((count * self.each,))

    def start(self, refs, dest, sems, src, n, at=0, slot=0):
        z, y, c, _ = place()
        copies = []
        if self.late:
            for (_, e), ref in zip(self.metas, refs):
                for d in range(self.n_z):
                    for b in range(2):
                        cp = pltpu.make_async_copy(
                            ref.at[d, self.half, b, :, pl.ds(src, n)],
                            dest.at[lax.rem(z - d + self.n_z, self.n_z), y ^ b, c ^ e, :, pl.ds(at, n)],
                            sems.at[slot * self.each + len(copies)],
                        )
                        cp.start()
                        copies.append(cp)
            return copies
        for (m, b, e, j), ref in zip(self.metas, refs):
            to = pl.ds(at + (0 if self.half is not None else m * n), n)
            if self.packed:
                cp = pltpu.make_async_copy(ref.at[:, pl.ds(src, n)], dest.at[:, to], sems.at[slot * self.each + len(copies)])
            else:
                k = ref.shape[0]
                cp = pltpu.make_async_copy(
                    ref.at[:, :, pl.ds(src, n)], dest.at[pl.ds(j, k), y ^ b, c ^ e, :, to], sems.at[slot * self.each + len(copies)]
                )
            cp.start()
            copies.append(cp)
        return copies

    def value(self, dest, first, last):
        if self.packed:
            return dest[:, first:last]
        return dest[:, :, :, :, first:last].reshape(4 * self.n_z * self.rows, last - first)

    def columns(self, dest, first, size):
        if self.packed:
            return dest[:, pl.ds(first, size)]
        return dest[:, :, :, :, pl.ds(first, size)].reshape(4 * self.n_z * self.rows, size)


def wait(copies):
    for cp in copies:
        cp.wait()


def wait_for(turn, groups):
    for i, copies in enumerate(groups):

        @pl.when(turn == i)
        def _(copies=copies):
            wait(copies)


def rms(values, gain):
    return values * lax.rsqrt(jnp.mean(values * values, axis=-1, keepdims=True) + EPS) * gain


def rms_back(values, gain, back):
    scale = lax.rsqrt(jnp.mean(values * values, axis=-1, keepdims=True) + EPS)
    unit = values * scale
    incoming = back * gain
    grad = scale * (incoming - unit * jnp.mean(incoming * unit, axis=-1, keepdims=True))
    return grad, jnp.sum(back * unit, axis=0, keepdims=True)


def lane_masks():
    lane = lax.broadcasted_iota(jnp.int32, (1, LANE), 1)
    low = (lane < DH).astype(F32)
    return [low.astype(BF16), (1.0 - low).astype(BF16)]


def bias_strip(base):
    first = pltpu.roll(jnp.broadcast_to(base, (8, L)), 0, 1, stride=1, stride_axis=0)
    return jnp.concatenate([first] + [pltpu.roll(first, 8 * g, 1) for g in range(1, QB // 8)], axis=0)


def fold_band(band):
    total = band[0:8]
    for g in range(1, QB // 8):
        total = total + pltpu.roll(band[8 * g : 8 * g + 8], L - 8 * g, 1)
    row = lax.broadcasted_iota(jnp.int32, (8, L), 0)
    for bit in range(3):
        total = jnp.where(((row >> bit) & 1) == 1, pltpu.roll(total, L - (1 << bit), 1), total)
    return jnp.sum(total, axis=0, keepdims=True)


WIDE = 256


def masked_strip(base_ref, row):
    strip = bias_strip(base_ref[pl.ds(row, 1), :])
    at_row = lax.broadcasted_iota(jnp.int32, (QB, L), 0)
    at_col = lax.broadcasted_iota(jnp.int32, (QB, L), 1)
    return jnp.where(at_col >= at_row, strip, NEG)


def bias_tile(strip, first_key, keys, first_query):
    parts = []
    for k in range(first_key, first_key + keys, QB):
        lo = first_query - k
        if lo >= 0:
            parts.append(strip[:, lo : lo + WIDE])
        else:
            parts.append(jnp.concatenate([jnp.full((QB, -lo), NEG, F32), strip[:, : WIDE + lo]], axis=1))
    return jnp.concatenate(parts, axis=0)


def half_rows(turned):
    none = jnp.zeros_like(turned[:DH])
    return [jnp.concatenate([turned[:DH], none], axis=0), jnp.concatenate([none, turned[DH:]], axis=0)]


def attend_loop(q_ref, k_ref, v_ref, o_ref, lse_ref, base_ref):
    masks = lane_masks()
    causal = base_ref is not None

    def step(t, carry):
        at = pl.ds(pl.multiple_of(t * LANE, LANE), LANE)
        q, k, v = q_ref[:, at], k_ref[:, at], v_ref[:, at]
        vt = half_rows(v.T)
        outs = [None] * (L // WIDE)
        keys = [k * masks[hh] for hh in range(2)]
        strips = [masked_strip(base_ref, t * 2 + hh) if causal else None for hh in range(2)]
        order = [(hh, b) for b in range(L // WIDE) for hh in range(2)]

        def scores(hh, b):
            n = (b + 1) * WIDE if causal else k.shape[0]
            s = nt(keys[hh][:n], q[b * WIDE : (b + 1) * WIDE])
            return s + bias_tile(strips[hh], 0, n, b * WIDE) if causal else s

        ahead = scores(*order[0])
        for i, (hh, b) in enumerate(order):
            s = ahead
            if i + 1 < len(order):
                ahead = scores(*order[i + 1])
            top = jnp.max(s, axis=0, keepdims=True)
            e = jnp.exp(s - top)
            total = jnp.sum(e, axis=0, keepdims=True)
            mixed = nn(vt[hh][:, : s.shape[0]], e.astype(BF16)) * (1.0 / total)
            outs[b] = mixed if outs[b] is None else outs[b] + mixed
            lse_ref[pl.ds(t * 2 + hh, 1), b * WIDE : (b + 1) * WIDE] = top + jnp.log(total)
        o_ref[:, at] = jnp.concatenate(outs, axis=1).T.astype(BF16)
        return carry

    lax.fori_loop(0, q_ref.shape[1] // LANE, step, 0)


def attend_back_loop(q_ref, k_ref, v_ref, o_ref, do_ref, lse_ref, dq_ref, dk_ref, dv_ref, p_ref, ds_ref, base_ref, off_ref, band_ref):
    masks = lane_masks()
    causal = base_ref is not None
    blocks = L // WIDE

    def step(t, carry):
        at = pl.ds(pl.multiple_of(t * LANE, LANE), LANE)
        q, k, v, do = q_ref[:, at], k_ref[:, at], v_ref[:, at], do_ref[:, at]
        prod = (do.astype(F32) * o_ref[:, at].astype(F32)).T
        kt = half_rows(k.T)
        for hh in range(2):
            km, vm = k * masks[hh], v * masks[hh]
            lse = lse_ref[pl.ds(t * 2 + hh, 1), :]
            delta = jnp.sum(prod[hh * DH : (hh + 1) * DH], axis=0, keepdims=True)
            if causal:
                strip = masked_strip(base_ref, t * 2 + hh)
                band_ref[...] = jnp.zeros_like(band_ref)
            for b in range(blocks):
                cols = slice(b * WIDE, (b + 1) * WIDE)
                to = slice((b * 2 + hh) * WIDE, (b * 2 + hh + 1) * WIDE)
                for kb in range(b + 1 if causal else k.shape[0] // WIDE):
                    rows = slice(kb * WIDE, (kb + 1) * WIDE)
                    s = nt(km[rows], q[cols])
                    if causal:
                        s = s + bias_tile(strip, kb * WIDE, WIDE, b * WIDE)
                    prob = jnp.exp(s - lse[:, cols])
                    p_ref[rows, to] = prob.astype(BF16)
                    ds = prob * (nt(vm[rows], do[cols]) - delta[:, cols])
                    ds_ref[rows, to] = ds.astype(BF16)
                    if causal:
                        for i in range(WIDE // QB):
                            lo = b * WIDE - kb * WIDE - i * QB
                            part = ds[i * QB : (i + 1) * QB]
                            if lo < 0:
                                part, lo = part[:, -lo:], 0
                            band_ref[:, lo : lo + part.shape[1]] += part
            if causal:
                off_ref[pl.ds(t * 2 + hh, 1), :] = fold_band(band_ref[...])
        do2 = jnp.concatenate([do[b * WIDE : (b + 1) * WIDE] * masks[hh] for b in range(blocks) for hh in range(2)], axis=0)
        q2 = jnp.concatenate([q[b * WIDE : (b + 1) * WIDE] * masks[hh] for b in range(blocks) for hh in range(2)], axis=0)
        if causal:
            for kb in range(blocks):
                rows = slice(kb * WIDE, (kb + 1) * WIDE)
                dv_ref[rows, at] = nn(p_ref[rows, kb * 2 * WIDE :], do2[kb * 2 * WIDE :]).astype(BF16)
                dk_ref[rows, at] = nn(ds_ref[rows, kb * 2 * WIDE :], q2[kb * 2 * WIDE :]).astype(BF16)
        else:
            dv_ref[:, at] = nn(p_ref[...], do2).astype(BF16)
            dk_ref[:, at] = nn(ds_ref[...], q2).astype(BF16)
        dq = []
        for b in range(blocks):
            n = (b + 1) * WIDE if causal else k.shape[0]
            dq.append(
                sum(nn(kt[hh][:, :n], ds_ref[:n, (b * 2 + hh) * WIDE : (b * 2 + hh + 1) * WIDE]) for hh in range(2))
            )
        dq_ref[:, at] = jnp.concatenate(dq, axis=1).T.astype(BF16)
        return carry

    lax.fori_loop(0, q_ref.shape[1] // LANE, step, 0)


def call(body, outs, args, scratch, name, flops):
    return pl.pallas_call(
        body,
        out_shape=tuple(jax.ShapeDtypeStruct(s, d) for s, d in outs),
        in_specs=[pl.BlockSpec(memory_space=pltpu.HBM if far else pltpu.VMEM) for _, far in args],
        out_specs=tuple(pl.BlockSpec(memory_space=pltpu.VMEM) for _ in outs),
        scratch_shapes=scratch,
        compiler_params=pltpu.CompilerParams(vmem_limit_bytes=VMEM_LIMIT[name] * MIB),
        cost_estimate=pl.CostEstimate(flops=flops, transcendentals=0, bytes_accessed=10_000_000),
    )(*[pltpu.with_memory_space_constraint(a, pltpu.HBM) if far else a for a, far in args])


def sequence_copy(ref, dest, sem):
    m = lax.axis_index("mp")
    cp = pltpu.make_async_copy(ref.at[pl.ds(pl.multiple_of(m * L, L), L), :], dest, sem)
    cp.start()
    return cp


def near(*arrays):
    return [(a, False) for a in arrays]


class Parts:
    def __init__(self, grid, d, cols, halves):
        self.n = grid.n_z
        self.rows = d // (4 * self.n)
        self.sorted = self.rows % 16 == 0
        self.d, self.cols, self.halves = d, cols, halves

    def outs(self):
        lead = (2,) if self.halves else ()
        if self.sorted:
            return [(lead + (2, self.n, self.rows, self.cols), BF16)] * 2
        return [(lead + (self.d, self.cols), BF16)]

    def count(self):
        return 2 if self.sorted else 1

    def put(self, refs, half, at, value):
        low = value.astype(BF16)
        size = low.shape[1]
        cols = pl.ds(at, size)
        if not self.sorted:
            if half is None:
                refs[0][:, cols] = low
            else:
                refs[0][half, :, cols] = low
            return
        z, y, c, _ = place()
        low = low.reshape(self.n, 2, 2, self.rows, size)
        for i in range(self.n):
            for b in range(2):
                first, second = low[i, b, 0], low[i, b, 1]
                where = (b ^ y, lax.rem(i - z + self.n, self.n), slice(None), cols)
                if half is not None:
                    where = (half,) + where
                refs[0][where] = lax.select(c == 0, first, second)
                refs[1][where] = lax.select(c == 0, second, first)

    def put_halves(self, refs, at, n, value):
        self.put(refs, 0, at, value[:, :n])
        self.put(refs, 1, at, value[:, n:])

    def split(self, arrays):
        if self.sorted:
            return arrays
        z, y, c, _ = place()
        v = arrays[0]
        v = v.reshape(v.shape[:-2] + (self.n, 2, 2, self.rows, self.cols))
        lead = v.ndim - 5
        v = jnp.moveaxis(v, (lead + 2, lead + 1, lead), (0, lead + 1, lead + 2))
        v = jnp.take(v, (z + jnp.arange(self.n)) % self.n, axis=lead + 2)
        v = jnp.take(v, jnp.arange(2) ^ y, axis=lead + 1)
        v = jnp.take(v, jnp.arange(2) ^ c, axis=0)
        return v[0], v[1]


DMA = pltpu.SemaphoreType.DMA


def self_forward(grid, inputs, base_hot, pieces, d, hd, heads):
    ws = Weights(pieces, grid.n_z)
    k = len(ws.arrays)
    w2 = 2 * hd

    def body(*refs):
        x_ref, hot_ref = refs[:2]
        w_refs = refs[2 : 2 + k]
        n1_ref, qkv_ref, o_ref, gain_ref, base_ref, lse_ref = refs[2 + k : 8 + k]
        x_v, we, w, sem_x, s_e, s_w = refs[8 + k :]
        cx = sequence_copy(x_ref, x_v, sem_x)
        ce = ws.start(w_refs, we, s_e, 3 * hd, LANE)
        cw = [ws.start(w_refs, w.at[g], s_w, g * hd, hd, slot=g) for g in range(3)]
        cx.wait()
        wait(ce)
        extra = ws.value(we, 0, 2 * LANE)
        rows = ws.rows
        shards = d // rows
        column = lax.broadcasted_iota(jnp.int32, (3 * shards, d), 1)
        row = lax.broadcasted_iota(jnp.int32, (3 * shards, d), 0)
        wanted = lax.rem(row, shards) * rows + heads + row // shards
        packed = nn((column == wanted).astype(F32).astype(BF16), extra[:, :LANE]).astype(BF16)
        lane = lax.broadcasted_iota(jnp.int32, (LANE, d), 0)
        column = lax.broadcasted_iota(jnp.int32, (LANE, d), 1)
        wide = nn(packed, (lane == lax.rem(column, rows)).astype(F32).astype(BF16))
        column = lax.broadcasted_iota(jnp.int32, (shards, d), 1)
        mine = column // rows == lax.broadcasted_iota(jnp.int32, (shards, d), 0)
        gains = [
            jnp.sum(jnp.where(mine, wide[i * shards : (i + 1) * shards], 0.0), axis=0, keepdims=True) for i in range(3)
        ]
        gains = jnp.concatenate(gains + [jnp.zeros((5, d), F32)], axis=0)
        gain_ref[...] = gains
        lse_ref[...] = jnp.zeros_like(lse_ref)
        base_ref[...] = jnp.zeros_like(base_ref)
        for a in range(2):
            base_ref[a * heads : (a + 1) * heads, :] = nn(extra[0:16, a * LANE : (a + 1) * LANE], hot_ref[...])[:heads]

        def normalize(t, carry):
            rows = pl.ds(pl.multiple_of(t * QB, QB), QB)
            n1_ref[rows, :] = rms(x_v[rows, :].astype(F32), gain_ref[0:1, :]).astype(BF16)
            return carry

        lax.fori_loop(0, L // QB, normalize, 0)

        def project(g, carry):
            wait_for(g, cw)
            qkv_ref[g] = nn(n1_ref[...], ws.value(w.at[g], 0, w2)).astype(BF16)
            return carry

        lax.fori_loop(0, 3, project, 0)
        attend_loop(qkv_ref.at[0], qkv_ref.at[1], qkv_ref.at[2], o_ref, lse_ref, base_ref)

    row = ((L, w2), BF16)
    return call(
        body,
        [((L, d), BF16), ((3, L, w2), BF16), row, ((8, d), F32), ((16, L), F32), ((16, L), F32)],
        [(inputs, True), (base_hot, False)] + ws.specs(),
        [
            pltpu.VMEM((L, d), BF16),
            ws.scratch(2 * LANE),
            ws.scratch(w2, 3),
            DMA,
            ws.sems(),
            ws.sems(3),
        ],
        "ka",
        3_000_000_000,
    )


def cross_forward(grid, inputs, encoded, attn_one, gains, pieces, d, hd):
    ws = Weights(pieces, grid.n_z)
    k = len(ws.arrays)
    w2 = 2 * hd

    def body(*refs):
        x_ref, enc_ref, a1_ref, gain_ref = refs[:4]
        w_refs = refs[4 : 4 + k]
        r1_ref, r2_ref, n2_ref, qkv_ref, o_ref, n3_ref, lse_ref = refs[4 + k : 11 + k]
        x_v, enc_v, w, sem_x, sem_e, s_w = refs[11 + k :]
        ce = sequence_copy(enc_ref, enc_v, sem_e)
        cw = {g: ws.start(w_refs, w.at[g], s_w, g * hd, hd, slot=g) for g in (2, 3)}
        cx = sequence_copy(x_ref, x_v, sem_x)
        cw.update({g: ws.start(w_refs, w.at[g], s_w, g * hd, hd, slot=g) for g in (0, 1, 4)})
        ce.wait()

        def project(g, carry):
            wait_for(g, [cw[2], cw[3]])
            qkv_ref[g + 1] = nn(enc_v[...], ws.value(w.at[g + 2], 0, w2)).astype(BF16)
            return carry

        lax.fori_loop(0, 2, project, 0)
        cx.wait()
        wait(cw[0])
        wait(cw[1])

        def resume(t, carry):
            rows = pl.ds(pl.multiple_of(t * WIDE, WIDE), WIDE)
            r1 = x_v[rows, :].astype(F32) + nt(a1_ref[rows, :], ws.value(w.at[0], 0, w2))
            r1_ref[rows, :] = r1
            n2 = rms(r1, gain_ref[1:2, :]).astype(BF16)
            n2_ref[rows, :] = n2
            qkv_ref[0, rows, :] = nn(n2, ws.value(w.at[1], 0, w2)).astype(BF16)
            return carry

        lax.fori_loop(0, L // WIDE, resume, 0)
        lse_ref[...] = jnp.zeros_like(lse_ref)
        attend_loop(qkv_ref.at[0], qkv_ref.at[1], qkv_ref.at[2], o_ref, lse_ref, None)
        wait(cw[4])

        def close(t, carry):
            rows = pl.ds(pl.multiple_of(t * WIDE, WIDE), WIDE)
            r2 = r1_ref[rows, :] + nt(o_ref[rows, :], ws.value(w.at[4], 0, w2))
            r2_ref[rows, :] = r2
            n3_ref[rows, :] = rms(r2, gain_ref[2:3, :]).astype(BF16)
            return carry

        lax.fori_loop(0, L // WIDE, close, 0)

    row = ((L, w2), BF16)
    wide = ((L, d), BF16)
    return call(
        body,
        [((L, d), F32), ((L, d), F32), wide, ((3, L, w2), BF16), row, wide, ((16, L), F32)],
        [(inputs, True), (encoded, True)] + near(attn_one, gains) + ws.specs(),
        [
            pltpu.VMEM((L, d), BF16),
            pltpu.VMEM((L, d), BF16),
            ws.scratch(w2, 5),
            DMA,
            DMA,
            ws.sems(5),
        ],
        "kb",
        5_000_000_000,
    )


def late_columns(ff):
    return ff // 2 // LANE * LANE


def feed_forward(grid, cotangent, n3, r2, gains, carried, pieces, late, half, d, ff, others=()):
    ws = Weights(pieces, grid.n_z, half)
    wl = Weights(late, grid.n_z, half)
    ks = len(ws.arrays)
    k = ks + len(wl.arrays)
    tile = min(256, ff)
    wide = min(512, ff)
    late_cols = late_columns(ff)
    last = carried is not None
    extra_in = 5 if last else len(others)
    parts = Parts(grid, d, 3 * ff, False)
    ng = parts.count()

    def body(*refs):
        cot_ref, n3_ref = refs[:2]
        w_refs = refs[2 + extra_in : 2 + extra_in + k]
        rest = refs[2 + extra_in + k :]
        if last:
            r2_ref, gain_ref, yin_ref, bin_ref, turned = refs[2:7]
            y_ref, b2_ref, dg_ref, y_acc, b3_acc = rest[ng : ng + 5]
        else:
            enc_ref, *other_refs = refs[2 : 2 + extra_in]
            y_acc, b3_acc, turned, turned_others = rest[ng : ng + 4]
        g_refs, rest = rest[:ng], rest[ng + (5 if last else 4) :]
        cot_v, enc_v, wg, wu, wd, lows, pending, sem_c, sem_e, s_g, s_u, s_d, s_l = rest
        cc = sequence_copy(cot_ref, cot_v, sem_c)
        cg = ws.start(w_refs[:ks], wg, s_g, 0, ff)
        cu = ws.start(w_refs[:ks], wu, s_u, ff, ff)
        cd = ws.start(w_refs[:ks], wd, s_d, 2 * ff, ff - late_cols)
        cd += wl.start(w_refs[ks:], wd, s_l, 0, late_cols, at=ff - late_cols)
        if last:
            y_acc[...] = r2_ref[...] + yin_ref[...]
            b3_acc[...] = bin_ref[...]
        else:
            ce = sequence_copy(enc_ref, enc_v, sem_e)
            y_acc[...] = jnp.zeros_like(y_acc)
            b3_acc[...] = jnp.zeros_like(b3_acc)
            ce.wait()
        cc.wait()
        if not last:

            def turn(t, carry):
                rows = pl.ds(pl.multiple_of(t * QB, QB), QB)
                turned[0, :, rows] = n3_ref[rows, :].T
                turned[1, :, rows] = cot_v[rows, :].T
                for i, ref in enumerate(other_refs):
                    turned_others[i, :, rows] = ref[rows, :].T
                turned_others[len(others) - 1, :, rows] = enc_v[rows, :].T
                return carry

            lax.fori_loop(0, L // QB, turn, 0)
        wait(cg)
        wait(cu)
        wait(cd)

        def step(t, carry):
            at = pl.multiple_of(t * tile, LANE)
            gate, upw, down = ws.columns(wg, at, tile), ws.columns(wu, at, tile), wl.columns(wd, at, tile)
            u = nn(n3_ref[...], gate)
            up = nn(n3_ref[...], upw)
            bh = nn(cot_v[...], down)
            sq = u * u
            th = jnp.tanh(GELU_C * (u + GELU_A * (sq * u)))
            both = 0.5 * (1.0 + th)
            gelu = u * both
            slope = both + 0.5 * u * (1.0 - th * th) * (GELU_C * (1.0 + (3.0 * GELU_A) * sq))
            hidden = (gelu * up).astype(BF16)
            gate_low = (bh * up * slope).astype(BF16)
            up_low = (bh * gelu).astype(BF16)
            y_acc[...] += nt(hidden, down)
            b3_acc[...] += nt(gate_low, gate) + nt(up_low, upw)
            for g, low in enumerate((gate_low, up_low, hidden)):
                lows[g, :, pl.ds(at, tile)] = low
            return carry

        lax.fori_loop(0, ff // tile, step, 0)
        pending[...] = jnp.zeros_like(pending)

        def weight(t, before):
            parts.put(g_refs, None, pl.multiple_of(before, LANE), pending[...])
            g = t // (ff // wide)
            at = pl.multiple_of(lax.rem(t, ff // wide) * wide, LANE)
            pending[...] = nn(turned[g // 2], lows[g, :, pl.ds(at, wide)]).astype(BF16)
            return g * ff + at

        at_last = lax.fori_loop(0, 3 * ff // wide, weight, jnp.int32(0))
        parts.put(g_refs, None, pl.multiple_of(at_last, LANE), pending[...])
        if last:
            dg_ref[...] = jnp.zeros_like(dg_ref)

            def finish(t, carry):
                rows = pl.ds(pl.multiple_of(t * QB, QB), QB)
                y_ref[rows, :] = y_acc[rows, :].astype(BF16)
                grad, dg = rms_back(r2_ref[rows, :], gain_ref[2:3, :], b3_acc[rows, :])
                b2_ref[rows, :] = cot_v[rows, :].astype(F32) + grad
                dg_ref[...] += dg
                return carry

            lax.fori_loop(0, L // QB, finish, 0)

    full = ((L, d), F32)
    outs = parts.outs()
    if last:
        outs += [((L, d), BF16), full, ((1, d), F32)]
    else:
        outs += [full, full, ((2, d, L), BF16), ((len(others), d, L), BF16)]
    scratch = [pltpu.VMEM((L, d), F32), pltpu.VMEM((L, d), F32)] if last else []
    result = call(
        body,
        outs,
        [(cotangent, True)]
        + near(n3)
        + (near(r2, gains, *carried) if last else [(others[0], True)] + near(*others[1:]))
        + ws.specs()
        + wl.specs(),
        scratch
        + [
            pltpu.VMEM((L, d), BF16),
            pltpu.VMEM((8, LANE) if last else (L, d), BF16),
            ws.scratch(ff),
            ws.scratch(ff),
            ws.scratch(ff),
            pltpu.VMEM((3, L, ff), BF16),
            pltpu.VMEM((d, wide), BF16),
            DMA,
            DMA,
            ws.sems(),
            ws.sems(),
            ws.sems(),
            wl.sems(),
        ],
        "kcb" if last else "kca",
        7_500_000_000,
    )
    return parts.split(result[:ng]), result[ng:]


def attention_backward(grid, back, qkv, attn, lse, base, pieces, first_col, hd, name):
    ws = Weights(pieces, grid.n_z)
    n = len(ws.arrays)
    w2 = 2 * hd
    causal = base is not None

    def body(*refs):
        b_ref, qkv_ref, o_ref, lse_ref = refs[:4]
        base_ref = refs[4] if causal else None
        refs = refs[5 if causal else 4 :]
        w_refs = refs[:n]
        out_ref = refs[n]
        off_ref = refs[n + 1] if causal else None
        wo, do, p_ref, ds_ref, band_ref, s_o = refs[-6:]
        co = ws.start(w_refs, wo, s_o, first_col, hd)
        if causal:
            off_ref[...] = jnp.zeros_like(off_ref)
        low = b_ref[...].astype(BF16)
        wait(co)
        do[...] = nn(low, ws.value(wo, 0, w2)).astype(BF16)
        attend_back_loop(
            qkv_ref.at[0],
            qkv_ref.at[1],
            qkv_ref.at[2],
            o_ref,
            do,
            lse_ref,
            out_ref.at[0],
            out_ref.at[1],
            out_ref.at[2],
            p_ref,
            ds_ref,
            base_ref,
            off_ref,
            band_ref,
        )

    return call(
        body,
        [((3, L, w2), BF16)] + ([((16, L), F32)] if causal else []),
        near(back, qkv, attn, lse) + (near(base) if causal else []) + ws.specs(),
        [
            ws.scratch(w2),
            pltpu.VMEM((L, w2), BF16),
            pltpu.VMEM((L, 2 * L), BF16),
            pltpu.VMEM((L, 2 * L), BF16),
            pltpu.VMEM((QB, L), F32),
            ws.sems(),
        ],
        name,
        3_000_000_000,
    )


def cross_finish(grid, b2, r1, ready, grads, attn_one, attn_two, gains, pieces, d, hd):
    ws = Weights(pieces, grid.n_z)
    k = len(ws.arrays)
    w2 = 2 * hd
    parts = Parts(grid, d, 5 * hd, True)
    ng = parts.count()

    def body(*refs):
        b2_ref, r1_ref, ready_ref, dy_ref, a1_ref, a2_ref, gain_ref = refs[:7]
        w_refs = refs[7 : 7 + k]
        b1_ref, eg_ref, dg_ref = refs[7 + k : 10 + k]
        g_refs = refs[10 + k : 10 + k + ng]
        w, turned, right, s_w = refs[10 + k + ng :]
        cw = [ws.start(w_refs, w.at[g], s_w, (g + 1) * hd, hd, slot=g) for g in range(3)]
        turned[1] = b2_ref[...].astype(BF16).T
        right[0] = a1_ref[...]
        for g in range(3):
            right[g + 1] = dy_ref[g]
        right[4] = a2_ref[...]
        wait(cw[0])
        dg_ref[...] = jnp.zeros_like(dg_ref)

        def resume(t, carry):
            rows = pl.ds(pl.multiple_of(t * WIDE, WIDE), WIDE)
            grad, dg = rms_back(r1_ref[rows, :], gain_ref[1:2, :], nt(dy_ref[0, rows, :], ws.value(w.at[0], 0, w2)))
            dg_ref[...] += dg
            b1_ref[rows, :] = b2_ref[rows, :] + grad
            return carry

        lax.fori_loop(0, L // WIDE, resume, 0)
        turned[0] = b1_ref[...].astype(BF16).T
        turned[2] = ready_ref[1]
        turned[3] = ready_ref[2]

        def weight(t, carry):
            parts.put_halves(g_refs, pl.multiple_of(2 * t * hd, LANE), hd, nn(turned[3 * t], right[2 * t]))
            parts.put_halves(g_refs, pl.multiple_of((2 * t + 1) * hd, LANE), hd, nn(turned[2 + t], right[2 * t + 1]))
            return carry

        lax.fori_loop(0, 2, weight, 0)
        parts.put_halves(g_refs, 4 * hd, hd, nn(turned[1], right[4]))
        wait(cw[1])
        wait(cw[2])

        def encoder(t, carry):
            rows = pl.ds(pl.multiple_of(t * WIDE, WIDE), WIDE)
            eg = nt(dy_ref[1, rows, :], ws.value(w.at[1], 0, w2)) + nt(dy_ref[2, rows, :], ws.value(w.at[2], 0, w2))
            eg_ref[rows, :] = eg.astype(BF16)
            return carry

        lax.fori_loop(0, L // WIDE, encoder, 0)

    result = call(
        body,
        [((L, d), F32), ((L, d), BF16), ((1, d), F32)] + parts.outs(),
        near(b2, r1, ready, grads, attn_one, attn_two, gains) + ws.specs(),
        [
            ws.scratch(w2, 3),
            pltpu.VMEM((4, d, L), BF16),
            pltpu.VMEM((5, L, w2), BF16),
            ws.sems(3),
        ],
        "kd2",
        5_000_000_000,
    )
    return result[:3], parts.split(result[3:])


def self_finish(grid, inputs, b1, ready, grads, off, dg2, dg3, base_hot, gains, pieces, d, hd, heads):
    ws = Weights(pieces, grid.n_z)
    k = len(ws.arrays)
    w2 = 2 * hd
    parts = Parts(grid, d, 3 * hd + LANE, True)
    ng = parts.count()

    def body(*refs):
        x_ref, b1_ref, ready_ref, dy_ref, off_ref, dg2_ref, dg3_ref, hot_ref, gain_ref = refs[:9]
        w_refs = refs[9 : 9 + k]
        dx_ref = refs[9 + k]
        g_refs = refs[10 + k : 10 + k + ng]
        x_v, w, back, pending, sem_x, s_w = refs[10 + k + ng :]
        cw = [ws.start(w_refs, w.at[g], s_w, g * hd, hd, slot=g) for g in range(3)]
        cx = sequence_copy(x_ref, x_v, sem_x)
        back[...] = jnp.zeros_like(back)

        def inner(g, carry):
            wait_for(g, cw)
            parts.put_halves(g_refs, pl.multiple_of(jnp.maximum(g - 1, 0) * hd, LANE), hd, pending[...])
            pending[...] = nn(ready_ref[0], dy_ref[g]).astype(BF16)
            back[...] += nt(dy_ref[g], ws.value(w.at[g], 0, w2))
            return carry

        pending[...] = jnp.zeros_like(pending)
        lax.fori_loop(0, 3, inner, 0)
        parts.put_halves(g_refs, 2 * hd, hd, pending[...])
        cx.wait()

        def finish(t, dg):
            rows = pl.ds(pl.multiple_of(t * QB, QB), QB)
            grad, own = rms_back(x_v[rows, :].astype(F32), gain_ref[0:1, :], back[rows, :])
            dx_ref[rows, :] = (b1_ref[rows, :] + grad).astype(BF16)
            return dg + own

        dg = lax.fori_loop(0, L // QB, finish, jnp.zeros((1, d), F32))
        dgs = jnp.concatenate([dg, dg2_ref[...], dg3_ref[...], jnp.zeros((5, d), F32)], axis=0)
        columns = jnp.concatenate([jnp.zeros((NB, d), F32), dgs, jnp.zeros((LANE - NB - 8, d), F32)], axis=0).T
        hot = hot_ref[...]
        sums = off_ref[...]
        table = jnp.zeros((16, LANE), F32)
        for _ in range(3):
            low = sums.astype(BF16)
            table = table + nt(low, hot)
            sums = sums - low.astype(F32)
        table = table.astype(BF16)
        shard_row = lax.rem(lax.broadcasted_iota(jnp.int32, (d, 16), 0), parts.rows)
        column = lax.broadcasted_iota(jnp.int32, (d, 16), 1)
        for a in range(2):
            spread = ((shard_row + a * heads == column) & (shard_row < heads)).astype(F32).astype(BF16)
            parts.put(g_refs, a, 3 * hd, nn(spread, table) + columns)

    result = call(
        body,
        [((L, d), BF16)] + parts.outs(),
        [(inputs, True)] + near(b1, ready, grads, off, dg2, dg3, base_hot, gains) + ws.specs(),
        [
            pltpu.VMEM((L, d), BF16),
            ws.scratch(w2, 3),
            pltpu.VMEM((L, d), F32),
            pltpu.VMEM((d, w2), BF16),
            DMA,
            ws.sems(3),
        ],
        "ke2",
        4_000_000_000,
    )
    return result[0], parts.split(result[1:])


def added(left, right):
    return (left.astype(F32) + right.astype(F32)).astype(BF16)


def scatter(grid, own, own_got, other, other_got, first, held=None):
    sent_a = added(other[..., :first], other_got[..., :first])
    sent_b = jnp.stack([added(v[1, ..., first:], g[1, ..., first:]) for v, g in ((own, own_got), (other, other_got))])
    if held is not None:
        sent_a, sent_b, held = lax.optimization_barrier((sent_a, sent_b, held))
    got = grid.swap_m(sent_a)
    got_b = grid.swap_y(sent_b)

    def a_sum(i):
        return added3(own[i, ..., :first], own_got[i, ..., :first], got[i])

    far_a = grid.swap_y(a_sum(1))
    far_b = grid.swap_m(added3(other[0, ..., first:], other_got[0, ..., first:], got_b[1]))
    wa, wb = a_sum(0), added3(own[0, ..., first:], own_got[0, ..., first:], got_b[0])
    return (wa, wb), (far_a, far_b), held


def joined(kept, far):
    return [
        jnp.concatenate([added(v[d], f[d]) for v, f in zip(kept, far)], axis=-1) for d in range(kept[0].shape[0])
    ]


def scatter_wide(grid, own, own_got, other, other_got, first):
    n = grid.n_z
    got_own = grid.swap_y(added(own[1, ..., first:], own_got[1, ..., first:]))
    got_other = grid.swap_y(added(other[1, ..., first:], other_got[1, ..., first:]))
    got = grid.swap_m(added(other[..., :first], other_got[..., :first]))

    def a_sum(i):
        return added3(own[i, ..., :first], own_got[i, ..., :first], got[i])

    far_a = grid.swap_y(a_sum(1))
    wa = a_sum(0)
    parts = []
    for v, g, far in ((own, own_got, got_own), (other, other_got, got_other)):
        w = [added3(v[0, d, :, first:], g[0, d, :, first:], far[d]) for d in range(n)]
        parts.append([w[0]] + [grid.shift_z(w[d], d) for d in range(1, n)])
    a = [added(wa[d], far_a[d]) for d in range(n)]
    a = [a[0]] + [grid.shift_z(a[d], d) for d in range(1, n)]
    return a, parts[0], parts[1]


def settle(grid, w, gate=None):
    sent = w[1:]
    if gate is not None:
        sent, gate = lax.optimization_barrier((sent, gate))
    return [w[0]] + [grid.shift_z(v, d + 1) for d, v in enumerate(sent)], gate


def summed(arrays):
    out = arrays[0].astype(F32)
    for v in arrays[1:]:
        out = out + v.astype(F32)
    return out


def added3(a, b, c):
    return (a.astype(F32) + b.astype(F32) + c.astype(F32)).astype(BF16)


def both_sequences(mine, other):
    first = lax.axis_index("mp") == 0
    low = jnp.where(first, mine, other)
    high = jnp.where(first, other, mine)
    return jnp.concatenate([low, high], axis=0).astype(F32)


def make(grid):
    def step(
        inputs,
        encoded,
        cotangent,
        buckets,
        rel_table,
        query_self,
        keys_self,
        values_self,
        output_self,
        query_cross,
        keys_cross,
        values_cross,
        output_cross,
        gate_weight,
        up_weight,
        down_weight,
        gain_first,
        gain_second,
        gain_third,
    ):
        d = inputs.shape[1]
        hd = query_self.shape[1]
        ff = gate_weight.shape[1]
        rows = query_self.shape[0]
        heads = rel_table.shape[0]
        assert inputs.shape[0] == 2 * L and heads + 3 <= rows <= LANE and heads <= 8
        extra = jnp.concatenate(
            [
                jnp.pad(rel_table, ((0, 0), (0, LANE - NB))),
                jnp.pad(jnp.stack([gain_first, gain_second, gain_third]), ((0, rows - heads - 3), (0, LANE - rows))),
            ],
            axis=0,
        )
        group_one = jnp.concatenate([query_self, keys_self, values_self, extra], axis=1)
        group_two = jnp.concatenate([output_self.T, query_cross, keys_cross, values_cross, output_cross.T], axis=1)
        turned = down_weight.T
        early = ff - late_columns(ff)
        group_three = jnp.concatenate([gate_weight, up_weight, turned[:, :early]], axis=1)
        pieces_one = gather(grid, group_one)
        pieces_two = gather(grid, group_two)
        pieces_three = gather(grid, group_three)
        pieces_four = gather_late(grid, turned[:, early:])

        base_hot = (buckets[None, :] == lax.broadcasted_iota(jnp.int32, (LANE, L), 0)).astype(BF16)

        n1, qkv1, at1, gains, base, lse1 = self_forward(grid, inputs, base_hot, pieces_one, d, hd, heads)
        r1, r2, n2, qkv2, at2, n3, lse2 = cross_forward(grid, inputs, encoded, at1, gains, pieces_two, d, hd)
        (own3, gone), (ya, ba, turned, turned_others) = feed_forward(
            grid, cotangent, n3, r2, gains, None, pieces_three, pieces_four, 0, d, ff, (encoded, n1, n2)
        )
        own3_got = grid.swap_c(gone)
        (other3, gone), (y, b2, dg3) = feed_forward(
            grid, cotangent, n3, r2, gains, (ya, ba, turned), pieces_three, pieces_four, 1, d, ff
        )
        other3_got = grid.swap_c(gone)
        y_far = grid.swap_m(y)
        a3, bo3, bt3 = scatter_wide(grid, own3, own3_got, other3, other3_got, 6 * LANE)
        (dy,) = attention_backward(grid, b2, qkv2, at2, lse2, None, pieces_two, 4 * hd, hd, "kd1")
        (b1, eg, dg2), (kept, gone) = cross_finish(
            grid, b2, r1, turned_others, dy, at1, at2, gains, pieces_two, d, hd
        )
        eg_far = grid.swap_m(eg)
        got = grid.swap_c(gone)
        kept2, far2, _ = scatter(grid, kept[0], got[0], kept[1], got[1], 7 * LANE)
        dy, off = attention_backward(grid, b1, qkv1, at1, lse1, base, pieces_two, 0, hd, "ke1")
        dx, (kept, gone) = self_finish(
            grid, inputs, b1, turned_others, dy, off, dg2, dg3, base_hot, gains, pieces_one, d, hd, heads
        )
        got = grid.swap_c(gone)
        kept1, far1, (kept2, bt30, y, eg) = scatter(
            grid, kept[0], got[0], kept[1], got[1], 5 * LANE, (kept2, bt3[0], y, eg)
        )
        b3 = bo3 + [grid.swap_m(summed([bt30] + bt3[1:]).astype(BF16))]
        z2, _ = settle(grid, joined(kept2, far2))
        w1 = joined(kept1, far1)
        dx_far = grid.swap_m(dx)
        layer_output = both_sequences(y, y_far)
        encoded_gradient = both_sequences(eg, eg_far)
        z1, (z20, a30, b30) = settle(grid, w1, (z2[0], a3[0], b3[0]))
        input_gradient = both_sequences(dx, dx_far)
        s3 = jnp.concatenate([summed([a30] + a3[1:]), summed([b30] + b3[1:])], axis=-1)
        s2 = summed([z20] + z2[1:])
        s1 = summed(z1)
        small = s1[:, 3 * hd :]
        table_gradient = small[:heads, :NB]
        dgs = [small[:, NB + i] for i in range(3)]
        return (
            layer_output,
            input_gradient,
            encoded_gradient,
            table_gradient,
            s1[:, :hd],
            s1[:, hd : 2 * hd],
            s1[:, 2 * hd : 3 * hd],
            s2[:, :hd].T,
            s2[:, hd : 2 * hd],
            s2[:, 2 * hd : 3 * hd],
            s2[:, 3 * hd : 4 * hd],
            s2[:, 4 * hd :].T,
            s3[:, :ff],
            s3[:, ff : 2 * ff],
            s3[:, 2 * ff :].T,
            dgs[0],
            dgs[1],
            dgs[2],
        )

    return step


def solution(mesh):
    weight, turned, row, gain = P("dp", "mp"), P("mp", "dp"), P("dp", None), P("dp")
    weights = (weight, weight, weight, turned, weight, weight, weight, turned, weight, weight, turned)
    gains = (gain, gain, gain)
    return jax.shard_map(
        make(Grid(mesh.shape["dp"], mesh.shape["mp"])),
        mesh=mesh,
        in_specs=(row, row, row, P(), P("mp", None)) + weights + gains,
        out_specs=(row, row, row, P("mp", None)) + weights + gains,
        check_vma=False,
    )
```

```python
import jax
import jax.numpy as jnp
from jax import lax
from jax.experimental import pallas as pl
from jax.experimental.pallas import tpu as pltpu
from jax.sharding import PartitionSpec as P


DH = 64
NB = 32
L = 512
LANE = 128
QB = 128
EPS = 1e-06
NEG = -1e30
GELU_C = 0.7978845608028654
GELU_A = 0.044715
AXES = ("dp", "mp")
F32 = jnp.float32
BF16 = jnp.bfloat16
MIB = 1024 * 1024
VMEM_LIMIT = {"ka": 11, "kb": 14, "kca": 20, "kcb": 20, "kd1": 10, "kd2": 20, "ke1": 10, "ke2": 13}


def nn(left, right):
    return lax.dot_general(left, right, (((1,), (0,)), ((), ())), preferred_element_type=F32)


def nt(left, right):
    return lax.dot_general(left, right, (((1,), (1,)), ((), ())), preferred_element_type=F32)


class Grid:
    def __init__(self, n_dp, n_mp):
        assert n_mp == 2 and n_dp % 8 == 0
        self.n_dp, self.n_mp = n_dp, n_mp
        self.n_z = n_dp // 4

    def perm(self, move):
        pairs = []
        for z in range(self.n_z):
            for y in range(2):
                for c in range(2):
                    for m in range(2):
                        tz, ty, tc, tm = move(z, y, c, m)
                        pairs.append(
                            (
                                (((z * 2 + y) * 2) + c) * 2 + m,
                                (((tz * 2 + ty) * 2) + tc) * 2 + tm,
                            )
                        )
        return pairs

    def send(self, v, move):
        return lax.ppermute(v, AXES, self.perm(move))

    def swap_m(self, v):
        return self.send(v, lambda z, y, c, m: (z, y, c, 1 - m))

    def swap_y(self, v):
        return self.send(v, lambda z, y, c, m: (z, 1 - y, c, m))

    def swap_c(self, v):
        return self.send(v, lambda z, y, c, m: (z, y, 1 - c, m))

    def shift_z(self, v, d):
        n = self.n_z
        return self.send(v, lambda z, y, c, m: ((z + d) % n, y, c, m))


def place():
    dp = lax.axis_index("dp")
    return dp // 4, (dp // 2) % 2, dp % 2, lax.axis_index("mp")


def gather(grid, block):
    rows, cols = block.shape
    n = grid.n_z
    z, y, c, _ = place()
    got = [block] + [grid.shift_z(block, d) for d in range(1, n)]
    own = jnp.zeros((n, rows, cols), block.dtype)
    for d in range(n):
        own = lax.dynamic_update_slice(own, got[d][None], (lax.rem(z - d + n, n), 0, 0))
    half = n // 2
    by_m = grid.swap_m(own)
    by_y = grid.swap_y(own)
    part_a = by_m[:half]
    part_b = by_y[half:]
    diag_a = grid.swap_y(part_a)
    diag_b = grid.swap_m(part_b)
    pieces = [(own, 0, 0, 0), (by_y, 0, 1, 0), (by_m, 1, 0, 0), (diag_a, 1, 1, 0), (diag_b, 1, 1, half)]
    out = [(a, m, b, 0, j) for a, m, b, j in pieces]
    out += [(grid.swap_c(p[0]),) + p[1:3] + (1, p[3]) for p in pieces]
    if rows % 16 == 0:
        return out
    stacks = []
    for m in range(2):
        for b in range(2):
            for e in range(2):
                mine = sorted((p for p in out if p[1:4] == (m, b, e)), key=lambda p: p[4])
                stacks.append(jnp.concatenate([p[0] for p in mine], axis=0))
    whole = jnp.stack(stacks).reshape(2, 2, 2, n, rows, cols)
    whole = jnp.take(whole, jnp.arange(2) ^ y, axis=1)
    whole = jnp.take(whole, jnp.arange(2) ^ c, axis=2)
    whole = whole.transpose(0, 3, 1, 2, 4, 5).reshape(2, n * 4 * rows, cols)
    return [(whole[m], m, None, None, 0) for m in range(2)]


def gather_late(grid, block):
    rows, cols = block.shape
    n = grid.n_z
    z, y, c, _ = place()
    by_m = grid.swap_m(block)
    by_y = grid.swap_y(block)
    diag = grid.send(block, lambda z, y, c, m: (z, 1 - y, c, 1 - m))
    own = jnp.stack([block, by_y, by_m, diag]).reshape(2, 2, rows, cols)
    mine = jnp.stack([own] + [grid.shift_z(own, d) for d in range(1, n)])
    other = grid.swap_c(mine)
    if rows % 16 == 0:
        return [(mine, "late", 0), (other, "late", 1)]
    whole = jnp.stack([mine, other])
    whole = jnp.take(whole, (z - jnp.arange(n)) % n, axis=1)
    whole = jnp.take(whole, jnp.arange(2) ^ y, axis=3)
    whole = jnp.take(whole, jnp.arange(2) ^ c, axis=0)
    whole = whole.transpose(2, 1, 3, 0, 4, 5).reshape(2, n * 4 * rows, cols)
    return [(whole[m], m, None, None, 0) for m in range(2)]


class Weights:
    def __init__(self, pieces, n_z, half=None):
        chosen = [p for p in pieces if half is None or p[1] in (half, "late")]
        self.arrays = [p[0] for p in chosen]
        self.metas = [p[1:] for p in chosen]
        self.late = self.metas[0][0] == "late"
        self.packed = not self.late and self.metas[0][1] is None
        self.n_z = n_z
        self.rows = pieces[0][0].shape[-2] if not self.packed else pieces[0][0].shape[0] // (4 * n_z)
        self.half = half
        self.each = len(self.arrays) * (2 * n_z if self.late else 1)

    def specs(self):
        return [(a, True) for a in self.arrays]

    def scratch(self, n, count=None):
        lead = () if count is None else (count,)
        if self.packed:
            return pltpu.VMEM(lead + (4 * self.n_z * self.rows, n), BF16)
        return pltpu.VMEM(lead + (self.n_z, 2, 2, self.rows, n), BF16)

    def sems(self, count=1):
        return pltpu.SemaphoreType.DMA((count * self.each,))

    def start(self, refs, dest, sems, src, n, at=0, slot=0):
        z, y, c, _ = place()
        copies = []
        if self.late:
            for (_, e), ref in zip(self.metas, refs):
                for d in range(self.n_z):
                    for b in range(2):
                        cp = pltpu.make_async_copy(
                            ref.at[d, self.half, b, :, pl.ds(src, n)],
                            dest.at[lax.rem(z - d + self.n_z, self.n_z), y ^ b, c ^ e, :, pl.ds(at, n)],
                            sems.at[slot * self.each + len(copies)],
                        )
                        cp.start()
                        copies.append(cp)
            return copies
        for (m, b, e, j), ref in zip(self.metas, refs):
            to = pl.ds(at + (0 if self.half is not None else m * n), n)
            if self.packed:
                cp = pltpu.make_async_copy(ref.at[:, pl.ds(src, n)], dest.at[:, to], sems.at[slot * self.each + len(copies)])
            else:
                k = ref.shape[0]
                cp = pltpu.make_async_copy(
                    ref.at[:, :, pl.ds(src, n)], dest.at[pl.ds(j, k), y ^ b, c ^ e, :, to], sems.at[slot * self.each + len(copies)]
                )
            cp.start()
            copies.append(cp)
        return copies

    def value(self, dest, first, last):
        if self.packed:
            return dest[:, first:last]
        return dest[:, :, :, :, first:last].reshape(4 * self.n_z * self.rows, last - first)

    def columns(self, dest, first, size):
        if self.packed:
            return dest[:, pl.ds(first, size)]
        return dest[:, :, :, :, pl.ds(first, size)].reshape(4 * self.n_z * self.rows, size)


def wait(copies):
    for cp in copies:
        cp.wait()


def wait_for(turn, groups):
    for i, copies in enumerate(groups):

        @pl.when(turn == i)
        def _(copies=copies):
            wait(copies)


def rms(values, gain):
    return values * lax.rsqrt(jnp.mean(values * values, axis=-1, keepdims=True) + EPS) * gain


def rms_back(values, gain, back):
    scale = lax.rsqrt(jnp.mean(values * values, axis=-1, keepdims=True) + EPS)
    unit = values * scale
    incoming = back * gain
    grad = scale * (incoming - unit * jnp.mean(incoming * unit, axis=-1, keepdims=True))
    return grad, jnp.sum(back * unit, axis=0, keepdims=True)


def lane_masks():
    lane = lax.broadcasted_iota(jnp.int32, (1, LANE), 1)
    low = (lane < DH).astype(F32)
    return [low.astype(BF16), (1.0 - low).astype(BF16)]


def bias_strip(base):
    first = pltpu.roll(jnp.broadcast_to(base, (8, L)), 0, 1, stride=1, stride_axis=0)
    return jnp.concatenate([first] + [pltpu.roll(first, 8 * g, 1) for g in range(1, QB // 8)], axis=0)


def fold_band(band):
    total = band[0:8]
    for g in range(1, QB // 8):
        total = total + pltpu.roll(band[8 * g : 8 * g + 8], L - 8 * g, 1)
    row = lax.broadcasted_iota(jnp.int32, (8, L), 0)
    for bit in range(3):
        total = jnp.where(((row >> bit) & 1) == 1, pltpu.roll(total, L - (1 << bit), 1), total)
    return jnp.sum(total, axis=0, keepdims=True)


WIDE = 256


def masked_strip(base_ref, row):
    strip = bias_strip(base_ref[pl.ds(row, 1), :])
    at_row = lax.broadcasted_iota(jnp.int32, (QB, L), 0)
    at_col = lax.broadcasted_iota(jnp.int32, (QB, L), 1)
    return jnp.where(at_col >= at_row, strip, NEG)


def bias_tile(strip, first_key, keys, first_query):
    parts = []
    for k in range(first_key, first_key + keys, QB):
        lo = first_query - k
        if lo >= 0:
            parts.append(strip[:, lo : lo + WIDE])
        else:
            parts.append(jnp.concatenate([jnp.full((QB, -lo), NEG, F32), strip[:, : WIDE + lo]], axis=1))
    return jnp.concatenate(parts, axis=0)


def half_rows(turned):
    none = jnp.zeros_like(turned[:DH])
    return [jnp.concatenate([turned[:DH], none], axis=0), jnp.concatenate([none, turned[DH:]], axis=0)]


def attend_loop(q_ref, k_ref, v_ref, o_ref, lse_ref, base_ref):
    masks = lane_masks()
    causal = base_ref is not None

    def step(t, carry):
        at = pl.ds(pl.multiple_of(t * LANE, LANE), LANE)
        q, k, v = q_ref[:, at], k_ref[:, at], v_ref[:, at]
        vt = half_rows(v.T)
        outs = [None] * (L // WIDE)
        keys = [k * masks[hh] for hh in range(2)]
        strips = [masked_strip(base_ref, t * 2 + hh) if causal else None for hh in range(2)]
        order = [(hh, b) for b in range(L // WIDE) for hh in range(2)]

        def scores(hh, b):
            n = (b + 1) * WIDE if causal else k.shape[0]
            s = nt(keys[hh][:n], q[b * WIDE : (b + 1) * WIDE])
            return s + bias_tile(strips[hh], 0, n, b * WIDE) if causal else s

        ahead = scores(*order[0])
        for i, (hh, b) in enumerate(order):
            s = ahead
            if i + 1 < len(order):
                ahead = scores(*order[i + 1])
            top = jnp.max(s, axis=0, keepdims=True)
            e = jnp.exp(s - top)
            total = jnp.sum(e, axis=0, keepdims=True)
            mixed = nn(vt[hh][:, : s.shape[0]], e.astype(BF16)) * (1.0 / total)
            outs[b] = mixed if outs[b] is None else outs[b] + mixed
            lse_ref[pl.ds(t * 2 + hh, 1), b * WIDE : (b + 1) * WIDE] = top + jnp.log(total)
        o_ref[:, at] = jnp.concatenate(outs, axis=1).T.astype(BF16)
        return carry

    lax.fori_loop(0, q_ref.shape[1] // LANE, step, 0)


def attend_back_loop(q_ref, k_ref, v_ref, o_ref, do_ref, lse_ref, dq_ref, dk_ref, dv_ref, p_ref, ds_ref, base_ref, off_ref, band_ref):
    masks = lane_masks()
    causal = base_ref is not None
    blocks = L // WIDE

    def step(t, carry):
        at = pl.ds(pl.multiple_of(t * LANE, LANE), LANE)
        q, k, v, do = q_ref[:, at], k_ref[:, at], v_ref[:, at], do_ref[:, at]
        prod = (do.astype(F32) * o_ref[:, at].astype(F32)).T
        kt = half_rows(k.T)
        for hh in range(2):
            km, vm = k * masks[hh], v * masks[hh]
            lse = lse_ref[pl.ds(t * 2 + hh, 1), :]
            delta = jnp.sum(prod[hh * DH : (hh + 1) * DH], axis=0, keepdims=True)
            if causal:
                strip = masked_strip(base_ref, t * 2 + hh)
                band_ref[...] = jnp.zeros_like(band_ref)
            for b in range(blocks):
                cols = slice(b * WIDE, (b + 1) * WIDE)
                to = slice((b * 2 + hh) * WIDE, (b * 2 + hh + 1) * WIDE)
                for kb in range(b + 1 if causal else k.shape[0] // WIDE):
                    rows = slice(kb * WIDE, (kb + 1) * WIDE)
                    s = nt(km[rows], q[cols])
                    if causal:
                        s = s + bias_tile(strip, kb * WIDE, WIDE, b * WIDE)
                    prob = jnp.exp(s - lse[:, cols])
                    p_ref[rows, to] = prob.astype(BF16)
                    ds = prob * (nt(vm[rows], do[cols]) - delta[:, cols])
                    ds_ref[rows, to] = ds.astype(BF16)
                    if causal:
                        for i in range(WIDE // QB):
                            lo = b * WIDE - kb * WIDE - i * QB
                            part = ds[i * QB : (i + 1) * QB]
                            if lo < 0:
                                part, lo = part[:, -lo:], 0
                            band_ref[:, lo : lo + part.shape[1]] += part
            if causal:
                off_ref[pl.ds(t * 2 + hh, 1), :] = fold_band(band_ref[...])
        do2 = jnp.concatenate([do[b * WIDE : (b + 1) * WIDE] * masks[hh] for b in range(blocks) for hh in range(2)], axis=0)
        q2 = jnp.concatenate([q[b * WIDE : (b + 1) * WIDE] * masks[hh] for b in range(blocks) for hh in range(2)], axis=0)
        if causal:
            for kb in range(blocks):
                rows = slice(kb * WIDE, (kb + 1) * WIDE)
                dv_ref[rows, at] = nn(p_ref[rows, kb * 2 * WIDE :], do2[kb * 2 * WIDE :]).astype(BF16)
                dk_ref[rows, at] = nn(ds_ref[rows, kb * 2 * WIDE :], q2[kb * 2 * WIDE :]).astype(BF16)
        else:
            dv_ref[:, at] = nn(p_ref[...], do2).astype(BF16)
            dk_ref[:, at] = nn(ds_ref[...], q2).astype(BF16)
        dq = []
        for b in range(blocks):
            n = (b + 1) * WIDE if causal else k.shape[0]
            dq.append(
                sum(nn(kt[hh][:, :n], ds_ref[:n, (b * 2 + hh) * WIDE : (b * 2 + hh + 1) * WIDE]) for hh in range(2))
            )
        dq_ref[:, at] = jnp.concatenate(dq, axis=1).T.astype(BF16)
        return carry

    lax.fori_loop(0, q_ref.shape[1] // LANE, step, 0)


def call(body, outs, args, scratch, name, flops):
    return pl.pallas_call(
        body,
        out_shape=tuple(jax.ShapeDtypeStruct(s, d) for s, d in outs),
        in_specs=[pl.BlockSpec(memory_space=pltpu.HBM if far else pltpu.VMEM) for _, far in args],
        out_specs=tuple(pl.BlockSpec(memory_space=pltpu.VMEM) for _ in outs),
        scratch_shapes=scratch,
        compiler_params=pltpu.CompilerParams(vmem_limit_bytes=VMEM_LIMIT[name] * MIB),
        cost_estimate=pl.CostEstimate(flops=flops, transcendentals=0, bytes_accessed=10_000_000),
    )(*[pltpu.with_memory_space_constraint(a, pltpu.HBM) if far else a for a, far in args])


def sequence_copy(ref, dest, sem):
    m = lax.axis_index("mp")
    cp = pltpu.make_async_copy(ref.at[pl.ds(pl.multiple_of(m * L, L), L), :], dest, sem)
    cp.start()
    return cp


def near(*arrays):
    return [(a, False) for a in arrays]


class Parts:
    def __init__(self, grid, d, cols, halves):
        self.n = grid.n_z
        self.rows = d // (4 * self.n)
        self.sorted = self.rows % 16 == 0
        self.d, self.cols, self.halves = d, cols, halves

    def outs(self):
        lead = (2,) if self.halves else ()
        if self.sorted:
            return [(lead + (2, self.n, self.rows, self.cols), BF16)] * 2
        return [(lead + (self.d, self.cols), BF16)]

    def count(self):
        return 2 if self.sorted else 1

    def put(self, refs, half, at, value):
        low = value.astype(BF16)
        size = low.shape[1]
        cols = pl.ds(at, size)
        if not self.sorted:
            if half is None:
                refs[0][:, cols] = low
            else:
                refs[0][half, :, cols] = low
            return
        z, y, c, _ = place()
        low = low.reshape(self.n, 2, 2, self.rows, size)
        for i in range(self.n):
            for b in range(2):
                first, second = low[i, b, 0], low[i, b, 1]
                where = (b ^ y, lax.rem(i - z + self.n, self.n), slice(None), cols)
                if half is not None:
                    where = (half,) + where
                refs[0][where] = lax.select(c == 0, first, second)
                refs[1][where] = lax.select(c == 0, second, first)

    def put_halves(self, refs, at, n, value):
        self.put(refs, 0, at, value[:, :n])
        self.put(refs, 1, at, value[:, n:])

    def split(self, arrays):
        if self.sorted:
            return arrays
        z, y, c, _ = place()
        v = arrays[0]
        v = v.reshape(v.shape[:-2] + (self.n, 2, 2, self.rows, self.cols))
        lead = v.ndim - 5
        v = jnp.moveaxis(v, (lead + 2, lead + 1, lead), (0, lead + 1, lead + 2))
        v = jnp.take(v, (z + jnp.arange(self.n)) % self.n, axis=lead + 2)
        v = jnp.take(v, jnp.arange(2) ^ y, axis=lead + 1)
        v = jnp.take(v, jnp.arange(2) ^ c, axis=0)
        return v[0], v[1]


DMA = pltpu.SemaphoreType.DMA


def self_forward(grid, inputs, base_hot, pieces, d, hd, heads):
    ws = Weights(pieces, grid.n_z)
    k = len(ws.arrays)
    w2 = 2 * hd

    def body(*refs):
        x_ref, hot_ref = refs[:2]
        w_refs = refs[2 : 2 + k]
        n1_ref, qkv_ref, o_ref, gain_ref, base_ref, lse_ref = refs[2 + k : 8 + k]
        x_v, we, w, sem_x, s_e, s_w = refs[8 + k :]
        cx = sequence_copy(x_ref, x_v, sem_x)
        ce = ws.start(w_refs, we, s_e, 3 * hd, LANE)
        cw = [ws.start(w_refs, w.at[g], s_w, g * hd, hd, slot=g) for g in range(3)]
        cx.wait()
        wait(ce)
        extra = ws.value(we, 0, 2 * LANE)
        rows = ws.rows
        shards = d // rows
        column = lax.broadcasted_iota(jnp.int32, (3 * shards, d), 1)
        row = lax.broadcasted_iota(jnp.int32, (3 * shards, d), 0)
        wanted = lax.rem(row, shards) * rows + heads + row // shards
        packed = nn((column == wanted).astype(F32).astype(BF16), extra[:, :LANE]).astype(BF16)
        lane = lax.broadcasted_iota(jnp.int32, (LANE, d), 0)
        column = lax.broadcasted_iota(jnp.int32, (LANE, d), 1)
        wide = nn(packed, (lane == lax.rem(column, rows)).astype(F32).astype(BF16))
        column = lax.broadcasted_iota(jnp.int32, (shards, d), 1)
        mine = column // rows == lax.broadcasted_iota(jnp.int32, (shards, d), 0)
        gains = [
            jnp.sum(jnp.where(mine, wide[i * shards : (i + 1) * shards], 0.0), axis=0, keepdims=True) for i in range(3)
        ]
        gains = jnp.concatenate(gains + [jnp.zeros((5, d), F32)], axis=0)
        gain_ref[...] = gains
        lse_ref[...] = jnp.zeros_like(lse_ref)
        base_ref[...] = jnp.zeros_like(base_ref)
        for a in range(2):
            base_ref[a * heads : (a + 1) * heads, :] = nn(extra[0:16, a * LANE : (a + 1) * LANE], hot_ref[...])[:heads]

        def normalize(t, carry):
            rows = pl.ds(pl.multiple_of(t * QB, QB), QB)
            n1_ref[rows, :] = rms(x_v[rows, :].astype(F32), gain_ref[0:1, :]).astype(BF16)
            return carry

        lax.fori_loop(0, L // QB, normalize, 0)

        def project(g, carry):
            wait_for(g, cw)
            qkv_ref[g] = nn(n1_ref[...], ws.value(w.at[g], 0, w2)).astype(BF16)
            return carry

        lax.fori_loop(0, 3, project, 0)
        attend_loop(qkv_ref.at[0], qkv_ref.at[1], qkv_ref.at[2], o_ref, lse_ref, base_ref)

    row = ((L, w2), BF16)
    return call(
        body,
        [((L, d), BF16), ((3, L, w2), BF16), row, ((8, d), F32), ((16, L), F32), ((16, L), F32)],
        [(inputs, True), (base_hot, False)] + ws.specs(),
        [
            pltpu.VMEM((L, d), BF16),
            ws.scratch(2 * LANE),
            ws.scratch(w2, 3),
            DMA,
            ws.sems(),
            ws.sems(3),
        ],
        "ka",
        3_000_000_000,
    )


def cross_forward(grid, inputs, encoded, attn_one, gains, pieces, d, hd):
    ws = Weights(pieces, grid.n_z)
    k = len(ws.arrays)
    w2 = 2 * hd

    def body(*refs):
        x_ref, enc_ref, a1_ref, gain_ref = refs[:4]
        w_refs = refs[4 : 4 + k]
        r1_ref, r2_ref, n2_ref, qkv_ref, o_ref, n3_ref, lse_ref = refs[4 + k : 11 + k]
        x_v, enc_v, w, sem_x, sem_e, s_w = refs[11 + k :]
        ce = sequence_copy(enc_ref, enc_v, sem_e)
        cw = {g: ws.start(w_refs, w.at[g], s_w, g * hd, hd, slot=g) for g in (2, 3)}
        cx = sequence_copy(x_ref, x_v, sem_x)
        cw.update({g: ws.start(w_refs, w.at[g], s_w, g * hd, hd, slot=g) for g in (0, 1, 4)})
        ce.wait()

        def project(g, carry):
            wait_for(g, [cw[2], cw[3]])
            qkv_ref[g + 1] = nn(enc_v[...], ws.value(w.at[g + 2], 0, w2)).astype(BF16)
            return carry

        lax.fori_loop(0, 2, project, 0)
        cx.wait()
        wait(cw[0])
        wait(cw[1])

        def resume(t, carry):
            rows = pl.ds(pl.multiple_of(t * WIDE, WIDE), WIDE)
            r1 = x_v[rows, :].astype(F32) + nt(a1_ref[rows, :], ws.value(w.at[0], 0, w2))
            r1_ref[rows, :] = r1
            n2 = rms(r1, gain_ref[1:2, :]).astype(BF16)
            n2_ref[rows, :] = n2
            qkv_ref[0, rows, :] = nn(n2, ws.value(w.at[1], 0, w2)).astype(BF16)
            return carry

        lax.fori_loop(0, L // WIDE, resume, 0)
        lse_ref[...] = jnp.zeros_like(lse_ref)
        attend_loop(qkv_ref.at[0], qkv_ref.at[1], qkv_ref.at[2], o_ref, lse_ref, None)
        wait(cw[4])

        def close(t, carry):
            rows = pl.ds(pl.multiple_of(t * WIDE, WIDE), WIDE)
            r2 = r1_ref[rows, :] + nt(o_ref[rows, :], ws.value(w.at[4], 0, w2))
            r2_ref[rows, :] = r2
            n3_ref[rows, :] = rms(r2, gain_ref[2:3, :]).astype(BF16)
            return carry

        lax.fori_loop(0, L // WIDE, close, 0)

    row = ((L, w2), BF16)
    wide = ((L, d), BF16)
    return call(
        body,
        [((L, d), F32), ((L, d), F32), wide, ((3, L, w2), BF16), row, wide, ((16, L), F32)],
        [(inputs, True), (encoded, True)] + near(attn_one, gains) + ws.specs(),
        [
            pltpu.VMEM((L, d), BF16),
            pltpu.VMEM((L, d), BF16),
            ws.scratch(w2, 5),
            DMA,
            DMA,
            ws.sems(5),
        ],
        "kb",
        5_000_000_000,
    )


def late_columns(ff):
    return ff // 2 // LANE * LANE


def feed_forward(grid, cotangent, n3, r2, gains, carried, pieces, late, half, d, ff, others=()):
    ws = Weights(pieces, grid.n_z, half)
    wl = Weights(late, grid.n_z, half)
    ks = len(ws.arrays)
    k = ks + len(wl.arrays)
    tile = min(256, ff)
    wide = min(512, ff)
    late_cols = late_columns(ff)
    last = carried is not None
    extra_in = 5 if last else len(others)
    parts = Parts(grid, d, 3 * ff, False)
    ng = parts.count()

    def body(*refs):
        cot_ref, n3_ref = refs[:2]
        w_refs = refs[2 + extra_in : 2 + extra_in + k]
        rest = refs[2 + extra_in + k :]
        if last:
            r2_ref, gain_ref, yin_ref, bin_ref, turned = refs[2:7]
            y_ref, b2_ref, dg_ref, y_acc, b3_acc = rest[ng : ng + 5]
        else:
            enc_ref, *other_refs = refs[2 : 2 + extra_in]
            y_acc, b3_acc, turned, turned_others = rest[ng : ng + 4]
        g_refs, rest = rest[:ng], rest[ng + (5 if last else 4) :]
        cot_v, enc_v, wg, wu, wd, lows, pending, sem_c, sem_e, s_g, s_u, s_d, s_l = rest
        cc = sequence_copy(cot_ref, cot_v, sem_c)
        cg = ws.start(w_refs[:ks], wg, s_g, 0, ff)
        cu = ws.start(w_refs[:ks], wu, s_u, ff, ff)
        cd = ws.start(w_refs[:ks], wd, s_d, 2 * ff, ff - late_cols)
        cd += wl.start(w_refs[ks:], wd, s_l, 0, late_cols, at=ff - late_cols)
        if last:
            y_acc[...] = r2_ref[...] + yin_ref[...]
            b3_acc[...] = bin_ref[...]
        else:
            ce = sequence_copy(enc_ref, enc_v, sem_e)
            y_acc[...] = jnp.zeros_like(y_acc)
            b3_acc[...] = jnp.zeros_like(b3_acc)
            ce.wait()
        cc.wait()
        if not last:

            def turn(t, carry):
                rows = pl.ds(pl.multiple_of(t * QB, QB), QB)
                turned[0, :, rows] = n3_ref[rows, :].T
                turned[1, :, rows] = cot_v[rows, :].T
                for i, ref in enumerate(other_refs):
                    turned_others[i, :, rows] = ref[rows, :].T
                turned_others[len(others) - 1, :, rows] = enc_v[rows, :].T
                return carry

            lax.fori_loop(0, L // QB, turn, 0)
        wait(cg)
        wait(cu)
        wait(cd)

        def step(t, carry):
            at = pl.multiple_of(t * tile, LANE)
            gate, upw, down = ws.columns(wg, at, tile), ws.columns(wu, at, tile), wl.columns(wd, at, tile)
            u = nn(n3_ref[...], gate)
            up = nn(n3_ref[...], upw)
            bh = nn(cot_v[...], down)
            sq = u * u
            th = jnp.tanh(GELU_C * (u + GELU_A * (sq * u)))
            both = 0.5 * (1.0 + th)
            gelu = u * both
            slope = both + 0.5 * u * (1.0 - th * th) * (GELU_C * (1.0 + (3.0 * GELU_A) * sq))
            hidden = (gelu * up).astype(BF16)
            gate_low = (bh * up * slope).astype(BF16)
            up_low = (bh * gelu).astype(BF16)
            y_acc[...] += nt(hidden, down)
            b3_acc[...] += nt(gate_low, gate) + nt(up_low, upw)
            for g, low in enumerate((gate_low, up_low, hidden)):
                lows[g, :, pl.ds(at, tile)] = low
            return carry

        lax.fori_loop(0, ff // tile, step, 0)
        pending[...] = jnp.zeros_like(pending)

        def weight(t, before):
            parts.put(g_refs, None, pl.multiple_of(before, LANE), pending[...])
            g = t // (ff // wide)
            at = pl.multiple_of(lax.rem(t, ff // wide) * wide, LANE)
            pending[...] = nn(turned[g // 2], lows[g, :, pl.ds(at, wide)]).astype(BF16)
            return g * ff + at

        at_last = lax.fori_loop(0, 3 * ff // wide, weight, jnp.int32(0))
        parts.put(g_refs, None, pl.multiple_of(at_last, LANE), pending[...])
        if last:
            dg_ref[...] = jnp.zeros_like(dg_ref)

            def finish(t, carry):
                rows = pl.ds(pl.multiple_of(t * QB, QB), QB)
                y_ref[rows, :] = y_acc[rows, :].astype(BF16)
                grad, dg = rms_back(r2_ref[rows, :], gain_ref[2:3, :], b3_acc[rows, :])
                b2_ref[rows, :] = cot_v[rows, :].astype(F32) + grad
                dg_ref[...] += dg
                return carry

            lax.fori_loop(0, L // QB, finish, 0)

    full = ((L, d), F32)
    outs = parts.outs()
    if last:
        outs += [((L, d), BF16), full, ((1, d), F32)]
    else:
        outs += [full, full, ((2, d, L), BF16), ((len(others), d, L), BF16)]
    scratch = [pltpu.VMEM((L, d), F32), pltpu.VMEM((L, d), F32)] if last else []
    result = call(
        body,
        outs,
        [(cotangent, True)]
        + near(n3)
        + (near(r2, gains, *carried) if last else [(others[0], True)] + near(*others[1:]))
        + ws.specs()
        + wl.specs(),
        scratch
        + [
            pltpu.VMEM((L, d), BF16),
            pltpu.VMEM((8, LANE) if last else (L, d), BF16),
            ws.scratch(ff),
            ws.scratch(ff),
            ws.scratch(ff),
            pltpu.VMEM((3, L, ff), BF16),
            pltpu.VMEM((d, wide), BF16),
            DMA,
            DMA,
            ws.sems(),
            ws.sems(),
            ws.sems(),
            wl.sems(),
        ],
        "kcb" if last else "kca",
        7_500_000_000,
    )
    return parts.split(result[:ng]), result[ng:]


def attention_backward(grid, back, qkv, attn, lse, base, pieces, first_col, hd, name):
    ws = Weights(pieces, grid.n_z)
    n = len(ws.arrays)
    w2 = 2 * hd
    causal = base is not None

    def body(*refs):
        b_ref, qkv_ref, o_ref, lse_ref = refs[:4]
        base_ref = refs[4] if causal else None
        refs = refs[5 if causal else 4 :]
        w_refs = refs[:n]
        out_ref = refs[n]
        off_ref = refs[n + 1] if causal else None
        wo, do, p_ref, ds_ref, band_ref, s_o = refs[-6:]
        co = ws.start(w_refs, wo, s_o, first_col, hd)
        if causal:
            off_ref[...] = jnp.zeros_like(off_ref)
        low = b_ref[...].astype(BF16)
        wait(co)
        do[...] = nn(low, ws.value(wo, 0, w2)).astype(BF16)
        attend_back_loop(
            qkv_ref.at[0],
            qkv_ref.at[1],
            qkv_ref.at[2],
            o_ref,
            do,
            lse_ref,
            out_ref.at[0],
            out_ref.at[1],
            out_ref.at[2],
            p_ref,
            ds_ref,
            base_ref,
            off_ref,
            band_ref,
        )

    return call(
        body,
        [((3, L, w2), BF16)] + ([((16, L), F32)] if causal else []),
        near(back, qkv, attn, lse) + (near(base) if causal else []) + ws.specs(),
        [
            ws.scratch(w2),
            pltpu.VMEM((L, w2), BF16),
            pltpu.VMEM((L, 2 * L), BF16),
            pltpu.VMEM((L, 2 * L), BF16),
            pltpu.VMEM((QB, L), F32),
            ws.sems(),
        ],
        name,
        3_000_000_000,
    )


def cross_finish(grid, b2, r1, ready, grads, attn_one, attn_two, gains, pieces, d, hd):
    ws = Weights(pieces, grid.n_z)
    k = len(ws.arrays)
    w2 = 2 * hd
    parts = Parts(grid, d, 5 * hd, True)
    ng = parts.count()

    def body(*refs):
        b2_ref, r1_ref, ready_ref, dy_ref, a1_ref, a2_ref, gain_ref = refs[:7]
        w_refs = refs[7 : 7 + k]
        b1_ref, eg_ref, dg_ref = refs[7 + k : 10 + k]
        g_refs = refs[10 + k : 10 + k + ng]
        w, turned, right, s_w = refs[10 + k + ng :]
        cw = [ws.start(w_refs, w.at[g], s_w, (g + 1) * hd, hd, slot=g) for g in range(3)]
        turned[1] = b2_ref[...].astype(BF16).T
        right[0] = a1_ref[...]
        for g in range(3):
            right[g + 1] = dy_ref[g]
        right[4] = a2_ref[...]
        wait(cw[0])
        dg_ref[...] = jnp.zeros_like(dg_ref)

        def resume(t, carry):
            rows = pl.ds(pl.multiple_of(t * WIDE, WIDE), WIDE)
            grad, dg = rms_back(r1_ref[rows, :], gain_ref[1:2, :], nt(dy_ref[0, rows, :], ws.value(w.at[0], 0, w2)))
            dg_ref[...] += dg
            b1_ref[rows, :] = b2_ref[rows, :] + grad
            return carry

        lax.fori_loop(0, L // WIDE, resume, 0)
        turned[0] = b1_ref[...].astype(BF16).T
        turned[2] = ready_ref[1]
        turned[3] = ready_ref[2]

        def weight(t, carry):
            parts.put_halves(g_refs, pl.multiple_of(2 * t * hd, LANE), hd, nn(turned[3 * t], right[2 * t]))
            parts.put_halves(g_refs, pl.multiple_of((2 * t + 1) * hd, LANE), hd, nn(turned[2 + t], right[2 * t + 1]))
            return carry

        lax.fori_loop(0, 2, weight, 0)
        parts.put_halves(g_refs, 4 * hd, hd, nn(turned[1], right[4]))
        wait(cw[1])
        wait(cw[2])

        def encoder(t, carry):
            rows = pl.ds(pl.multiple_of(t * WIDE, WIDE), WIDE)
            eg = nt(dy_ref[1, rows, :], ws.value(w.at[1], 0, w2)) + nt(dy_ref[2, rows, :], ws.value(w.at[2], 0, w2))
            eg_ref[rows, :] = eg.astype(BF16)
            return carry

        lax.fori_loop(0, L // WIDE, encoder, 0)

    result = call(
        body,
        [((L, d), F32), ((L, d), BF16), ((1, d), F32)] + parts.outs(),
        near(b2, r1, ready, grads, attn_one, attn_two, gains) + ws.specs(),
        [
            ws.scratch(w2, 3),
            pltpu.VMEM((4, d, L), BF16),
            pltpu.VMEM((5, L, w2), BF16),
            ws.sems(3),
        ],
        "kd2",
        5_000_000_000,
    )
    return result[:3], parts.split(result[3:])


def self_finish(grid, inputs, b1, ready, grads, off, dg2, dg3, base_hot, gains, pieces, d, hd, heads):
    ws = Weights(pieces, grid.n_z)
    k = len(ws.arrays)
    w2 = 2 * hd
    parts = Parts(grid, d, 3 * hd + LANE, True)
    ng = parts.count()

    def body(*refs):
        x_ref, b1_ref, ready_ref, dy_ref, off_ref, dg2_ref, dg3_ref, hot_ref, gain_ref = refs[:9]
        w_refs = refs[9 : 9 + k]
        dx_ref = refs[9 + k]
        g_refs = refs[10 + k : 10 + k + ng]
        x_v, w, back, pending, sem_x, s_w = refs[10 + k + ng :]
        cw = [ws.start(w_refs, w.at[g], s_w, g * hd, hd, slot=g) for g in range(3)]
        cx = sequence_copy(x_ref, x_v, sem_x)
        back[...] = jnp.zeros_like(back)

        def inner(g, carry):
            wait_for(g, cw)
            parts.put_halves(g_refs, pl.multiple_of(jnp.maximum(g - 1, 0) * hd, LANE), hd, pending[...])
            pending[...] = nn(ready_ref[0], dy_ref[g]).astype(BF16)
            back[...] += nt(dy_ref[g], ws.value(w.at[g], 0, w2))
            return carry

        pending[...] = jnp.zeros_like(pending)
        lax.fori_loop(0, 3, inner, 0)
        parts.put_halves(g_refs, 2 * hd, hd, pending[...])
        cx.wait()

        def finish(t, dg):
            rows = pl.ds(pl.multiple_of(t * QB, QB), QB)
            grad, own = rms_back(x_v[rows, :].astype(F32), gain_ref[0:1, :], back[rows, :])
            dx_ref[rows, :] = (b1_ref[rows, :] + grad).astype(BF16)
            return dg + own

        dg = lax.fori_loop(0, L // QB, finish, jnp.zeros((1, d), F32))
        dgs = jnp.concatenate([dg, dg2_ref[...], dg3_ref[...], jnp.zeros((5, d), F32)], axis=0)
        columns = jnp.concatenate([jnp.zeros((NB, d), F32), dgs, jnp.zeros((LANE - NB - 8, d), F32)], axis=0).T
        hot = hot_ref[...]
        sums = off_ref[...]
        table = jnp.zeros((16, LANE), F32)
        for _ in range(3):
            low = sums.astype(BF16)
            table = table + nt(low, hot)
            sums = sums - low.astype(F32)
        table = table.astype(BF16)
        shard_row = lax.rem(lax.broadcasted_iota(jnp.int32, (d, 16), 0), parts.rows)
        column = lax.broadcasted_iota(jnp.int32, (d, 16), 1)
        for a in range(2):
            spread = ((shard_row + a * heads == column) & (shard_row < heads)).astype(F32).astype(BF16)
            parts.put(g_refs, a, 3 * hd, nn(spread, table) + columns)

    result = call(
        body,
        [((L, d), BF16)] + parts.outs(),
        [(inputs, True)] + near(b1, ready, grads, off, dg2, dg3, base_hot, gains) + ws.specs(),
        [
            pltpu.VMEM((L, d), BF16),
            ws.scratch(w2, 3),
            pltpu.VMEM((L, d), F32),
            pltpu.VMEM((d, w2), BF16),
            DMA,
            ws.sems(3),
        ],
        "ke2",
        4_000_000_000,
    )
    return result[0], parts.split(result[1:])


def added(left, right):
    return (left.astype(F32) + right.astype(F32)).astype(BF16)


def scatter(grid, own, own_got, other, other_got, first, held=None, later=None):
    sent_a = added(other[..., :first], other_got[..., :first])
    sent_b = jnp.stack([added(v[1, ..., first:], g[1, ..., first:]) for v, g in ((own, own_got), (other, other_got))])
    if held is not None:
        sent_a, sent_b, held = lax.optimization_barrier((sent_a, sent_b, held))
    got = grid.swap_m(sent_a)
    got_b = grid.swap_y(sent_b)

    def a_sum(i):
        return added3(own[i, ..., :first], own_got[i, ..., :first], got[i])

    sent_a, sent_b = a_sum(1), added3(other[0, ..., first:], other_got[0, ..., first:], got_b[1])
    if later is not None:
        sent_a, sent_b, later = lax.optimization_barrier((sent_a, sent_b, later))
    far_a = grid.swap_y(sent_a)
    far_b = grid.swap_m(sent_b)
    wa, wb = a_sum(0), added3(own[0, ..., first:], own_got[0, ..., first:], got_b[0])
    return (wa, wb), (far_a, far_b), held, later


def joined(kept, far):
    return [
        jnp.concatenate([added(v[d], f[d]) for v, f in zip(kept, far)], axis=-1) for d in range(kept[0].shape[0])
    ]


def scatter_wide(grid, own, own_got, other, other_got, first):
    n = grid.n_z
    got_own = grid.swap_y(added(own[1, ..., first:], own_got[1, ..., first:]))
    got_other = grid.swap_y(added(other[1, ..., first:], other_got[1, ..., first:]))
    got = grid.swap_m(added(other[..., :first], other_got[..., :first]))

    def a_sum(i):
        return added3(own[i, ..., :first], own_got[i, ..., :first], got[i])

    far_a = grid.swap_y(a_sum(1))
    wa = a_sum(0)
    parts = []
    for v, g, far in ((own, own_got, got_own), (other, other_got, got_other)):
        w = [added3(v[0, d, :, first:], g[0, d, :, first:], far[d]) for d in range(n)]
        parts.append([w[0]] + [grid.shift_z(w[d], d) for d in range(1, n)])
    a = [added(wa[d], far_a[d]) for d in range(n)]
    a = [a[0]] + [grid.shift_z(a[d], d) for d in range(1, n)]
    return a, parts[0], parts[1]


def settle(grid, w, gate=None):
    sent = w[1:]
    if gate is not None:
        sent, gate = lax.optimization_barrier((sent, gate))
    return [w[0]] + [grid.shift_z(v, d + 1) for d, v in enumerate(sent)], gate


def summed(arrays):
    out = arrays[0].astype(F32)
    for v in arrays[1:]:
        out = out + v.astype(F32)
    return out


def added3(a, b, c):
    return (a.astype(F32) + b.astype(F32) + c.astype(F32)).astype(BF16)


def both_sequences(mine, other):
    first = lax.axis_index("mp") == 0
    low = jnp.where(first, mine, other)
    high = jnp.where(first, other, mine)
    return jnp.concatenate([low, high], axis=0).astype(F32)


def make(grid):
    def step(
        inputs,
        encoded,
        cotangent,
        buckets,
        rel_table,
        query_self,
        keys_self,
        values_self,
        output_self,
        query_cross,
        keys_cross,
        values_cross,
        output_cross,
        gate_weight,
        up_weight,
        down_weight,
        gain_first,
        gain_second,
        gain_third,
    ):
        d = inputs.shape[1]
        hd = query_self.shape[1]
        ff = gate_weight.shape[1]
        rows = query_self.shape[0]
        heads = rel_table.shape[0]
        assert inputs.shape[0] == 2 * L and heads + 3 <= rows <= LANE and heads <= 8
        extra = jnp.concatenate(
            [
                jnp.pad(rel_table, ((0, 0), (0, LANE - NB))),
                jnp.pad(jnp.stack([gain_first, gain_second, gain_third]), ((0, rows - heads - 3), (0, LANE - rows))),
            ],
            axis=0,
        )
        group_one = jnp.concatenate([query_self, keys_self, values_self, extra], axis=1)
        group_two = jnp.concatenate([output_self.T, query_cross, keys_cross, values_cross, output_cross.T], axis=1)
        turned = down_weight.T
        early = ff - late_columns(ff)
        group_three = jnp.concatenate([gate_weight, up_weight, turned[:, :early]], axis=1)
        pieces_one = gather(grid, group_one)
        pieces_two = gather(grid, group_two)
        pieces_three = gather(grid, group_three)
        pieces_four = gather_late(grid, turned[:, early:])

        base_hot = (buckets[None, :] == lax.broadcasted_iota(jnp.int32, (LANE, L), 0)).astype(BF16)

        n1, qkv1, at1, gains, base, lse1 = self_forward(grid, inputs, base_hot, pieces_one, d, hd, heads)
        r1, r2, n2, qkv2, at2, n3, lse2 = cross_forward(grid, inputs, encoded, at1, gains, pieces_two, d, hd)
        (own3, gone), (ya, ba, turned, turned_others) = feed_forward(
            grid, cotangent, n3, r2, gains, None, pieces_three, pieces_four, 0, d, ff, (encoded, n1, n2)
        )
        own3_got = grid.swap_c(gone)
        (other3, gone), (y, b2, dg3) = feed_forward(
            grid, cotangent, n3, r2, gains, (ya, ba, turned), pieces_three, pieces_four, 1, d, ff
        )
        other3_got = grid.swap_c(gone)
        y_far = grid.swap_m(y)
        a3, bo3, bt3 = scatter_wide(grid, own3, own3_got, other3, other3_got, 6 * LANE)
        (dy,) = attention_backward(grid, b2, qkv2, at2, lse2, None, pieces_two, 4 * hd, hd, "kd1")
        (b1, eg, dg2), (kept, gone) = cross_finish(
            grid, b2, r1, turned_others, dy, at1, at2, gains, pieces_two, d, hd
        )
        eg_far = grid.swap_m(eg)
        got = grid.swap_c(gone)
        kept2, far2, _, _ = scatter(grid, kept[0], got[0], kept[1], got[1], 7 * LANE)
        dy, off = attention_backward(grid, b1, qkv1, at1, lse1, base, pieces_two, 0, hd, "ke1")
        dx, (kept, gone) = self_finish(
            grid, inputs, b1, turned_others, dy, off, dg2, dg3, base_hot, gains, pieces_one, d, hd, heads
        )
        got = grid.swap_c(gone)
        kept1, far1, (kept2, bt30), (y, eg) = scatter(
            grid, kept[0], got[0], kept[1], got[1], 5 * LANE, (kept2, bt3[0]), (y, eg)
        )
        b3 = bo3 + [grid.swap_m(summed([bt30] + bt3[1:]).astype(BF16))]
        z2, _ = settle(grid, joined(kept2, far2))
        w1 = joined(kept1, far1)
        dx_far = grid.swap_m(dx)
        layer_output = both_sequences(y, y_far)
        encoded_gradient = both_sequences(eg, eg_far)
        z1, (z20, a30, b30) = settle(grid, w1, (z2[0], a3[0], b3[0]))
        input_gradient = both_sequences(dx, dx_far)
        s3 = jnp.concatenate([summed([a30] + a3[1:]), summed([b30] + b3[1:])], axis=-1)
        s2 = summed([z20] + z2[1:])
        s1 = summed(z1)
        small = s1[:, 3 * hd :]
        table_gradient = small[:heads, :NB]
        dgs = [small[:, NB + i] for i in range(3)]
        return (
            layer_output,
            input_gradient,
            encoded_gradient,
            table_gradient,
            s1[:, :hd],
            s1[:, hd : 2 * hd],
            s1[:, 2 * hd : 3 * hd],
            s2[:, :hd].T,
            s2[:, hd : 2 * hd],
            s2[:, 2 * hd : 3 * hd],
            s2[:, 3 * hd : 4 * hd],
            s2[:, 4 * hd :].T,
            s3[:, :ff],
            s3[:, ff : 2 * ff],
            s3[:, 2 * ff :].T,
            dgs[0],
            dgs[1],
            dgs[2],
        )

    return step


def solution(mesh):
    weight, turned, row, gain = P("dp", "mp"), P("mp", "dp"), P("dp", None), P("dp")
    weights = (weight, weight, weight, turned, weight, weight, weight, turned, weight, weight, turned)
    gains = (gain, gain, gain)
    return jax.shard_map(
        make(Grid(mesh.shape["dp"], mesh.shape["mp"])),
        mesh=mesh,
        in_specs=(row, row, row, P(), P("mp", None)) + weights + gains,
        out_specs=(row, row, row, P("mp", None)) + weights + gains,
        check_vma=False,
    )
```

```python
import jax
import jax.numpy as jnp
from jax import lax
from jax.experimental import pallas as pl
from jax.experimental.pallas import tpu as pltpu
from jax.sharding import PartitionSpec as P


DH = 64
NB = 32
L = 512
LANE = 128
QB = 128
EPS = 1e-06
NEG = -1e30
GELU_C = 0.7978845608028654
GELU_A = 0.044715
AXES = ("dp", "mp")
F32 = jnp.float32
BF16 = jnp.bfloat16
MIB = 1024 * 1024
VMEM_LIMIT = {"ka": 13, "kb": 16, "kca": 23, "kcb": 25, "kd1": 12, "kd2": 22, "ke1": 12, "ke2": 16}


def nn(left, right):
    return lax.dot_general(left, right, (((1,), (0,)), ((), ())), preferred_element_type=F32)


def nt(left, right):
    return lax.dot_general(left, right, (((1,), (1,)), ((), ())), preferred_element_type=F32)


class Grid:
    def __init__(self, n_dp, n_mp):
        assert n_mp == 2 and n_dp % 8 == 0
        self.n_dp, self.n_mp = n_dp, n_mp
        self.n_z = n_dp // 4

    def perm(self, move):
        pairs = []
        for z in range(self.n_z):
            for y in range(2):
                for c in range(2):
                    for m in range(2):
                        tz, ty, tc, tm = move(z, y, c, m)
                        pairs.append(
                            (
                                (((z * 2 + y) * 2) + c) * 2 + m,
                                (((tz * 2 + ty) * 2) + tc) * 2 + tm,
                            )
                        )
        return pairs

    def send(self, v, move):
        return lax.ppermute(v, AXES, self.perm(move))

    def swap_m(self, v):
        return self.send(v, lambda z, y, c, m: (z, y, c, 1 - m))

    def swap_y(self, v):
        return self.send(v, lambda z, y, c, m: (z, 1 - y, c, m))

    def swap_c(self, v):
        return self.send(v, lambda z, y, c, m: (z, y, 1 - c, m))

    def shift_z(self, v, d):
        n = self.n_z
        return self.send(v, lambda z, y, c, m: ((z + d) % n, y, c, m))


def place():
    dp = lax.axis_index("dp")
    return dp // 4, (dp // 2) % 2, dp % 2, lax.axis_index("mp")


def gather(grid, block):
    rows, cols = block.shape
    n = grid.n_z
    z, y, c, _ = place()
    got = [block] + [grid.shift_z(block, d) for d in range(1, n)]
    own = jnp.zeros((n, rows, cols), block.dtype)
    for d in range(n):
        own = lax.dynamic_update_slice(own, got[d][None], (lax.rem(z - d + n, n), 0, 0))
    half = n // 2
    by_m = grid.swap_m(own)
    by_y = grid.swap_y(own)
    part_a = by_m[:half]
    part_b = by_y[half:]
    diag_a = grid.swap_y(part_a)
    diag_b = grid.swap_m(part_b)
    pieces = [(own, 0, 0, 0), (by_y, 0, 1, 0), (by_m, 1, 0, 0), (diag_a, 1, 1, 0), (diag_b, 1, 1, half)]
    out = [(a, m, b, 0, j) for a, m, b, j in pieces]
    out += [(grid.swap_c(p[0]),) + p[1:3] + (1, p[3]) for p in pieces]
    if rows % 16 == 0:
        return out
    stacks = []
    for m in range(2):
        for b in range(2):
            for e in range(2):
                mine = sorted((p for p in out if p[1:4] == (m, b, e)), key=lambda p: p[4])
                stacks.append(jnp.concatenate([p[0] for p in mine], axis=0))
    whole = jnp.stack(stacks).reshape(2, 2, 2, n, rows, cols)
    whole = jnp.take(whole, jnp.arange(2) ^ y, axis=1)
    whole = jnp.take(whole, jnp.arange(2) ^ c, axis=2)
    whole = whole.transpose(0, 3, 1, 2, 4, 5).reshape(2, n * 4 * rows, cols)
    return [(whole[m], m, None, None, 0) for m in range(2)]


def gather_late(grid, block):
    rows, cols = block.shape
    n = grid.n_z
    z, y, c, _ = place()
    by_m = grid.swap_m(block)
    by_y = grid.swap_y(block)
    diag = grid.send(block, lambda z, y, c, m: (z, 1 - y, c, 1 - m))
    own = jnp.stack([block, by_y, by_m, diag]).reshape(2, 2, rows, cols)
    mine = jnp.stack([own] + [grid.shift_z(own, d) for d in range(1, n)])
    other = grid.swap_c(mine)
    if rows % 16 == 0:
        return [(mine, "late", 0), (other, "late", 1)]
    whole = jnp.stack([mine, other])
    whole = jnp.take(whole, (z - jnp.arange(n)) % n, axis=1)
    whole = jnp.take(whole, jnp.arange(2) ^ y, axis=3)
    whole = jnp.take(whole, jnp.arange(2) ^ c, axis=0)
    whole = whole.transpose(2, 1, 3, 0, 4, 5).reshape(2, n * 4 * rows, cols)
    return [(whole[m], m, None, None, 0) for m in range(2)]


class Weights:
    def __init__(self, pieces, n_z, half=None):
        chosen = [p for p in pieces if half is None or p[1] in (half, "late")]
        self.arrays = [p[0] for p in chosen]
        self.metas = [p[1:] for p in chosen]
        self.late = self.metas[0][0] == "late"
        self.packed = not self.late and self.metas[0][1] is None
        self.n_z = n_z
        self.rows = pieces[0][0].shape[-2] if not self.packed else pieces[0][0].shape[0] // (4 * n_z)
        self.half = half
        self.each = len(self.arrays) * (2 * n_z if self.late else 1)

    def specs(self):
        return [(a, True) for a in self.arrays]

    def scratch(self, n, count=None):
        lead = () if count is None else (count,)
        if self.packed:
            return pltpu.VMEM(lead + (4 * self.n_z * self.rows, n), BF16)
        return pltpu.VMEM(lead + (self.n_z, 2, 2, self.rows, n), BF16)

    def sems(self, count=1):
        return pltpu.SemaphoreType.DMA((count * self.each,))

    def start(self, refs, dest, sems, src, n, at=0, slot=0):
        z, y, c, _ = place()
        copies = []
        if self.late:
            for (_, e), ref in zip(self.metas, refs):
                for d in range(self.n_z):
                    for b in range(2):
                        cp = pltpu.make_async_copy(
                            ref.at[d, self.half, b, :, pl.ds(src, n)],
                            dest.at[lax.rem(z - d + self.n_z, self.n_z), y ^ b, c ^ e, :, pl.ds(at, n)],
                            sems.at[slot * self.each + len(copies)],
                        )
                        cp.start()
                        copies.append(cp)
            return copies
        for (m, b, e, j), ref in zip(self.metas, refs):
            to = pl.ds(at + (0 if self.half is not None else m * n), n)
            if self.packed:
                cp = pltpu.make_async_copy(ref.at[:, pl.ds(src, n)], dest.at[:, to], sems.at[slot * self.each + len(copies)])
            else:
                k = ref.shape[0]
                cp = pltpu.make_async_copy(
                    ref.at[:, :, pl.ds(src, n)], dest.at[pl.ds(j, k), y ^ b, c ^ e, :, to], sems.at[slot * self.each + len(copies)]
                )
            cp.start()
            copies.append(cp)
        return copies

    def value(self, dest, first, last):
        if self.packed:
            return dest[:, first:last]
        return dest[:, :, :, :, first:last].reshape(4 * self.n_z * self.rows, last - first)

    def columns(self, dest, first, size):
        if self.packed:
            return dest[:, pl.ds(first, size)]
        return dest[:, :, :, :, pl.ds(first, size)].reshape(4 * self.n_z * self.rows, size)


def wait(copies):
    for cp in copies:
        cp.wait()


def wait_for(turn, groups):
    for i, copies in enumerate(groups):

        @pl.when(turn == i)
        def _(copies=copies):
            wait(copies)


def rms(values, gain):
    return values * lax.rsqrt(jnp.mean(values * values, axis=-1, keepdims=True) + EPS) * gain


def rms_back(values, gain, back):
    scale = lax.rsqrt(jnp.mean(values * values, axis=-1, keepdims=True) + EPS)
    unit = values * scale
    incoming = back * gain
    grad = scale * (incoming - unit * jnp.mean(incoming * unit, axis=-1, keepdims=True))
    return grad, jnp.sum(back * unit, axis=0, keepdims=True)


def lane_masks():
    lane = lax.broadcasted_iota(jnp.int32, (1, LANE), 1)
    low = (lane < DH).astype(F32)
    return [low.astype(BF16), (1.0 - low).astype(BF16)]


def bias_strip(base):
    first = pltpu.roll(jnp.broadcast_to(base, (8, L)), 0, 1, stride=1, stride_axis=0)
    return jnp.concatenate([first] + [pltpu.roll(first, 8 * g, 1) for g in range(1, QB // 8)], axis=0)


def fold_band(band):
    total = band[0:8]
    for g in range(1, QB // 8):
        total = total + pltpu.roll(band[8 * g : 8 * g + 8], L - 8 * g, 1)
    row = lax.broadcasted_iota(jnp.int32, (8, L), 0)
    for bit in range(3):
        total = jnp.where(((row >> bit) & 1) == 1, pltpu.roll(total, L - (1 << bit), 1), total)
    return jnp.sum(total, axis=0, keepdims=True)


WIDE = 256


def masked_strip(base_ref, row):
    strip = bias_strip(base_ref[pl.ds(row, 1), :])
    at_row = lax.broadcasted_iota(jnp.int32, (QB, L), 0)
    at_col = lax.broadcasted_iota(jnp.int32, (QB, L), 1)
    return jnp.where(at_col >= at_row, strip, NEG)


def bias_tile(strip, first_key, keys, first_query):
    parts = []
    for k in range(first_key, first_key + keys, QB):
        lo = first_query - k
        if lo >= 0:
            parts.append(strip[:, lo : lo + WIDE])
        else:
            parts.append(jnp.concatenate([jnp.full((QB, -lo), NEG, F32), strip[:, : WIDE + lo]], axis=1))
    return jnp.concatenate(parts, axis=0)


def half_rows(turned):
    none = jnp.zeros_like(turned[:DH])
    return [jnp.concatenate([turned[:DH], none], axis=0), jnp.concatenate([none, turned[DH:]], axis=0)]


def attend_loop(q_ref, k_ref, v_ref, o_ref, lse_ref, base_ref):
    masks = lane_masks()
    causal = base_ref is not None

    def step(t, carry):
        at = pl.ds(pl.multiple_of(t * LANE, LANE), LANE)
        q, k, v = q_ref[:, at], k_ref[:, at], v_ref[:, at]
        vt = half_rows(v.T)
        outs = [None] * (L // WIDE)
        keys = [k * masks[hh] for hh in range(2)]
        strips = [masked_strip(base_ref, t * 2 + hh) if causal else None for hh in range(2)]
        order = [(hh, b) for b in range(L // WIDE) for hh in range(2)]

        def scores(hh, b):
            n = (b + 1) * WIDE if causal else k.shape[0]
            s = nt(keys[hh][:n], q[b * WIDE : (b + 1) * WIDE])
            return s + bias_tile(strips[hh], 0, n, b * WIDE) if causal else s

        ahead = scores(*order[0])
        for i, (hh, b) in enumerate(order):
            s = ahead
            if i + 1 < len(order):
                ahead = scores(*order[i + 1])
            top = jnp.max(s, axis=0, keepdims=True)
            e = jnp.exp(s - top)
            total = jnp.sum(e, axis=0, keepdims=True)
            mixed = nn(vt[hh][:, : s.shape[0]], e.astype(BF16)) * (1.0 / total)
            outs[b] = mixed if outs[b] is None else outs[b] + mixed
            lse_ref[pl.ds(t * 2 + hh, 1), b * WIDE : (b + 1) * WIDE] = top + jnp.log(total)
        o_ref[:, at] = jnp.concatenate(outs, axis=1).T.astype(BF16)
        return carry

    lax.fori_loop(0, q_ref.shape[1] // LANE, step, 0)


def attend_back_loop(q_ref, k_ref, v_ref, o_ref, do_ref, lse_ref, dq_ref, dk_ref, dv_ref, p_ref, ds_ref, base_ref, off_ref, band_ref):
    masks = lane_masks()
    causal = base_ref is not None
    blocks = L // WIDE

    def step(t, carry):
        at = pl.ds(pl.multiple_of(t * LANE, LANE), LANE)
        q, k, v, do = q_ref[:, at], k_ref[:, at], v_ref[:, at], do_ref[:, at]
        prod = (do.astype(F32) * o_ref[:, at].astype(F32)).T
        kt = half_rows(k.T)
        for hh in range(2):
            km, vm = k * masks[hh], v * masks[hh]
            lse = lse_ref[pl.ds(t * 2 + hh, 1), :]
            delta = jnp.sum(prod[hh * DH : (hh + 1) * DH], axis=0, keepdims=True)
            if causal:
                strip = masked_strip(base_ref, t * 2 + hh)
                band_ref[...] = jnp.zeros_like(band_ref)
            for b in range(blocks):
                cols = slice(b * WIDE, (b + 1) * WIDE)
                to = slice((b * 2 + hh) * WIDE, (b * 2 + hh + 1) * WIDE)
                for kb in range(b + 1 if causal else k.shape[0] // WIDE):
                    rows = slice(kb * WIDE, (kb + 1) * WIDE)
                    s = nt(km[rows], q[cols])
                    if causal:
                        s = s + bias_tile(strip, kb * WIDE, WIDE, b * WIDE)
                    prob = jnp.exp(s - lse[:, cols])
                    p_ref[rows, to] = prob.astype(BF16)
                    ds = prob * (nt(vm[rows], do[cols]) - delta[:, cols])
                    ds_ref[rows, to] = ds.astype(BF16)
                    if causal:
                        for i in range(WIDE // QB):
                            lo = b * WIDE - kb * WIDE - i * QB
                            part = ds[i * QB : (i + 1) * QB]
                            if lo < 0:
                                part, lo = part[:, -lo:], 0
                            band_ref[:, lo : lo + part.shape[1]] += part
            if causal:
                off_ref[pl.ds(t * 2 + hh, 1), :] = fold_band(band_ref[...])
        do2 = jnp.concatenate([do[b * WIDE : (b + 1) * WIDE] * masks[hh] for b in range(blocks) for hh in range(2)], axis=0)
        q2 = jnp.concatenate([q[b * WIDE : (b + 1) * WIDE] * masks[hh] for b in range(blocks) for hh in range(2)], axis=0)
        if causal:
            for kb in range(blocks):
                rows = slice(kb * WIDE, (kb + 1) * WIDE)
                dv_ref[rows, at] = nn(p_ref[rows, kb * 2 * WIDE :], do2[kb * 2 * WIDE :]).astype(BF16)
                dk_ref[rows, at] = nn(ds_ref[rows, kb * 2 * WIDE :], q2[kb * 2 * WIDE :]).astype(BF16)
        else:
            dv_ref[:, at] = nn(p_ref[...], do2).astype(BF16)
            dk_ref[:, at] = nn(ds_ref[...], q2).astype(BF16)
        dq = []
        for b in range(blocks):
            n = (b + 1) * WIDE if causal else k.shape[0]
            dq.append(
                sum(nn(kt[hh][:, :n], ds_ref[:n, (b * 2 + hh) * WIDE : (b * 2 + hh + 1) * WIDE]) for hh in range(2))
            )
        dq_ref[:, at] = jnp.concatenate(dq, axis=1).T.astype(BF16)
        return carry

    lax.fori_loop(0, q_ref.shape[1] // LANE, step, 0)


def call(body, outs, args, scratch, name, flops):
    return pl.pallas_call(
        body,
        out_shape=tuple(jax.ShapeDtypeStruct(s, d) for s, d in outs),
        in_specs=[pl.BlockSpec(memory_space=pltpu.HBM if far else pltpu.VMEM) for _, far in args],
        out_specs=tuple(pl.BlockSpec(memory_space=pltpu.VMEM) for _ in outs),
        scratch_shapes=scratch,
        compiler_params=pltpu.CompilerParams(vmem_limit_bytes=VMEM_LIMIT[name] * MIB),
        cost_estimate=pl.CostEstimate(flops=flops, transcendentals=0, bytes_accessed=10_000_000),
    )(*[pltpu.with_memory_space_constraint(a, pltpu.HBM) if far else a for a, far in args])


def sequence_copy(ref, dest, sem):
    m = lax.axis_index("mp")
    cp = pltpu.make_async_copy(ref.at[pl.ds(pl.multiple_of(m * L, L), L), :], dest, sem)
    cp.start()
    return cp


def near(*arrays):
    return [(a, False) for a in arrays]


class Parts:
    def __init__(self, grid, d, cols, halves):
        self.n = grid.n_z
        self.rows = d // (4 * self.n)
        self.sorted = self.rows % 16 == 0
        self.d, self.cols, self.halves = d, cols, halves

    def outs(self):
        lead = (2,) if self.halves else ()
        if self.sorted:
            return [(lead + (2, self.n, self.rows, self.cols), BF16)] * 2
        return [(lead + (self.d, self.cols), BF16)]

    def count(self):
        return 2 if self.sorted else 1

    def put(self, refs, half, at, value):
        low = value.astype(BF16)
        size = low.shape[1]
        cols = pl.ds(at, size)
        if not self.sorted:
            if half is None:
                refs[0][:, cols] = low
            else:
                refs[0][half, :, cols] = low
            return
        z, y, c, _ = place()
        low = low.reshape(self.n, 2, 2, self.rows, size)
        for i in range(self.n):
            for b in range(2):
                first, second = low[i, b, 0], low[i, b, 1]
                where = (b ^ y, lax.rem(i - z + self.n, self.n), slice(None), cols)
                if half is not None:
                    where = (half,) + where
                refs[0][where] = lax.select(c == 0, first, second)
                refs[1][where] = lax.select(c == 0, second, first)

    def put_halves(self, refs, at, n, value):
        self.put(refs, 0, at, value[:, :n])
        self.put(refs, 1, at, value[:, n:])

    def split(self, arrays):
        if self.sorted:
            return arrays
        z, y, c, _ = place()
        v = arrays[0]
        v = v.reshape(v.shape[:-2] + (self.n, 2, 2, self.rows, self.cols))
        lead = v.ndim - 5
        v = jnp.moveaxis(v, (lead + 2, lead + 1, lead), (0, lead + 1, lead + 2))
        v = jnp.take(v, (z + jnp.arange(self.n)) % self.n, axis=lead + 2)
        v = jnp.take(v, jnp.arange(2) ^ y, axis=lead + 1)
        v = jnp.take(v, jnp.arange(2) ^ c, axis=0)
        return v[0], v[1]


DMA = pltpu.SemaphoreType.DMA


def one_hot(bucket_row):
    return (lax.broadcasted_iota(jnp.int32, (LANE, L), 0) == bucket_row).astype(F32).astype(BF16)


def self_forward(grid, inputs, bucket_row, pieces, d, hd, heads):
    ws = Weights(pieces, grid.n_z)
    k = len(ws.arrays)
    w2 = 2 * hd

    def body(*refs):
        x_ref, hot_ref = refs[:2]
        w_refs = refs[2 : 2 + k]
        n1_ref, qkv_ref, o_ref, gain_ref, base_ref, lse_ref = refs[2 + k : 8 + k]
        x_v, we, w, sem_x, s_e, s_w = refs[8 + k :]
        cx = sequence_copy(x_ref, x_v, sem_x)
        ce = ws.start(w_refs, we, s_e, 3 * hd, LANE)
        cw = [ws.start(w_refs, w.at[g], s_w, g * hd, hd, slot=g) for g in range(3)]
        cx.wait()
        wait(ce)
        extra = ws.value(we, 0, 2 * LANE)
        rows = ws.rows
        shards = d // rows
        column = lax.broadcasted_iota(jnp.int32, (3 * shards, d), 1)
        row = lax.broadcasted_iota(jnp.int32, (3 * shards, d), 0)
        wanted = lax.rem(row, shards) * rows + heads + row // shards
        packed = nn((column == wanted).astype(F32).astype(BF16), extra[:, :LANE]).astype(BF16)
        lane = lax.broadcasted_iota(jnp.int32, (LANE, d), 0)
        column = lax.broadcasted_iota(jnp.int32, (LANE, d), 1)
        wide = nn(packed, (lane == lax.rem(column, rows)).astype(F32).astype(BF16))
        column = lax.broadcasted_iota(jnp.int32, (shards, d), 1)
        mine = column // rows == lax.broadcasted_iota(jnp.int32, (shards, d), 0)
        gains = [
            jnp.sum(jnp.where(mine, wide[i * shards : (i + 1) * shards], 0.0), axis=0, keepdims=True) for i in range(3)
        ]
        gains = jnp.concatenate(gains + [jnp.zeros((5, d), F32)], axis=0)
        gain_ref[...] = gains
        lse_ref[...] = jnp.zeros_like(lse_ref)
        base_ref[...] = jnp.zeros_like(base_ref)
        hot = one_hot(hot_ref[...])
        for a in range(2):
            base_ref[a * heads : (a + 1) * heads, :] = nn(extra[0:16, a * LANE : (a + 1) * LANE], hot)[:heads]

        def normalize(t, carry):
            rows = pl.ds(pl.multiple_of(t * QB, QB), QB)
            n1_ref[rows, :] = rms(x_v[rows, :].astype(F32), gain_ref[0:1, :]).astype(BF16)
            return carry

        lax.fori_loop(0, L // QB, normalize, 0)

        def project(g, carry):
            wait_for(g, cw)
            qkv_ref[g] = nn(n1_ref[...], ws.value(w.at[g], 0, w2)).astype(BF16)
            return carry

        lax.fori_loop(0, 3, project, 0)
        attend_loop(qkv_ref.at[0], qkv_ref.at[1], qkv_ref.at[2], o_ref, lse_ref, base_ref)

    row = ((L, w2), BF16)
    return call(
        body,
        [((L, d), BF16), ((3, L, w2), BF16), row, ((8, d), F32), ((16, L), F32), ((16, L), F32)],
        [(inputs, True), (bucket_row, False)] + ws.specs(),
        [
            pltpu.VMEM((L, d), BF16),
            ws.scratch(2 * LANE),
            ws.scratch(w2, 3),
            DMA,
            ws.sems(),
            ws.sems(3),
        ],
        "ka",
        3_000_000_000,
    )


def cross_forward(grid, inputs, encoded, attn_one, gains, pieces, d, hd):
    ws = Weights(pieces, grid.n_z)
    k = len(ws.arrays)
    w2 = 2 * hd

    def body(*refs):
        x_ref, enc_ref, a1_ref, gain_ref = refs[:4]
        w_refs = refs[4 : 4 + k]
        r1_ref, r2_ref, n2_ref, qkv_ref, o_ref, n3_ref, lse_ref = refs[4 + k : 11 + k]
        x_v, enc_v, w, sem_x, sem_e, s_w = refs[11 + k :]
        ce = sequence_copy(enc_ref, enc_v, sem_e)
        cw = {g: ws.start(w_refs, w.at[g], s_w, g * hd, hd, slot=g) for g in (2, 3)}
        cx = sequence_copy(x_ref, x_v, sem_x)
        cw.update({g: ws.start(w_refs, w.at[g], s_w, g * hd, hd, slot=g) for g in (0, 1, 4)})
        ce.wait()

        def project(g, carry):
            wait_for(g, [cw[2], cw[3]])
            qkv_ref[g + 1] = nn(enc_v[...], ws.value(w.at[g + 2], 0, w2)).astype(BF16)
            return carry

        lax.fori_loop(0, 2, project, 0)
        cx.wait()
        wait(cw[0])
        wait(cw[1])

        def resume(t, carry):
            rows = pl.ds(pl.multiple_of(t * WIDE, WIDE), WIDE)
            r1 = x_v[rows, :].astype(F32) + nt(a1_ref[rows, :], ws.value(w.at[0], 0, w2))
            r1_ref[rows, :] = r1
            n2 = rms(r1, gain_ref[1:2, :]).astype(BF16)
            n2_ref[rows, :] = n2
            qkv_ref[0, rows, :] = nn(n2, ws.value(w.at[1], 0, w2)).astype(BF16)
            return carry

        lax.fori_loop(0, L // WIDE, resume, 0)
        lse_ref[...] = jnp.zeros_like(lse_ref)
        attend_loop(qkv_ref.at[0], qkv_ref.at[1], qkv_ref.at[2], o_ref, lse_ref, None)
        wait(cw[4])

        def close(t, carry):
            rows = pl.ds(pl.multiple_of(t * WIDE, WIDE), WIDE)
            r2 = r1_ref[rows, :] + nt(o_ref[rows, :], ws.value(w.at[4], 0, w2))
            r2_ref[rows, :] = r2
            n3_ref[rows, :] = rms(r2, gain_ref[2:3, :]).astype(BF16)
            return carry

        lax.fori_loop(0, L // WIDE, close, 0)

    row = ((L, w2), BF16)
    wide = ((L, d), BF16)
    return call(
        body,
        [((L, d), F32), ((L, d), F32), wide, ((3, L, w2), BF16), row, wide, ((16, L), F32)],
        [(inputs, True), (encoded, True)] + near(attn_one, gains) + ws.specs(),
        [
            pltpu.VMEM((L, d), BF16),
            pltpu.VMEM((L, d), BF16),
            ws.scratch(w2, 5),
            DMA,
            DMA,
            ws.sems(5),
        ],
        "kb",
        5_000_000_000,
    )


def late_columns(ff):
    return ff // 2 // LANE * LANE


def feed_forward(grid, cotangent, n3, r2, gains, carried, pieces, late, half, d, ff, others=()):
    ws = Weights(pieces, grid.n_z, half)
    wl = Weights(late, grid.n_z, half)
    ks = len(ws.arrays)
    k = ks + len(wl.arrays)
    tile = min(256, ff)
    wide = min(512, ff)
    late_cols = late_columns(ff)
    last = carried is not None
    extra_in = 5 if last else len(others)
    parts = Parts(grid, d, 3 * ff, False)
    ng = parts.count()

    def body(*refs):
        cot_ref, n3_ref = refs[:2]
        w_refs = refs[2 + extra_in : 2 + extra_in + k]
        rest = refs[2 + extra_in + k :]
        if last:
            r2_ref, gain_ref, yin_ref, bin_ref, turned = refs[2:7]
            y_ref, b2_ref, dg_ref, y_acc, b3_acc = rest[ng : ng + 5]
        else:
            enc_ref, *other_refs = refs[2 : 2 + extra_in]
            y_acc, b3_acc, turned, turned_others = rest[ng : ng + 4]
        g_refs, rest = rest[:ng], rest[ng + (5 if last else 4) :]
        cot_v, enc_v, wg, wu, wd, lows, pending, sem_c, sem_e, s_g, s_u, s_d, s_l = rest
        cc = sequence_copy(cot_ref, cot_v, sem_c)
        cg = ws.start(w_refs[:ks], wg, s_g, 0, ff)
        cu = ws.start(w_refs[:ks], wu, s_u, ff, ff)
        cd = ws.start(w_refs[:ks], wd, s_d, 2 * ff, ff - late_cols)
        cd += wl.start(w_refs[ks:], wd, s_l, 0, late_cols, at=ff - late_cols)
        if last:
            y_acc[...] = r2_ref[...] + yin_ref[...]
            b3_acc[...] = bin_ref[...]
        else:
            ce = sequence_copy(enc_ref, enc_v, sem_e)
            y_acc[...] = jnp.zeros_like(y_acc)
            b3_acc[...] = jnp.zeros_like(b3_acc)
            ce.wait()
        cc.wait()
        if not last:

            def turn(t, carry):
                rows = pl.ds(pl.multiple_of(t * QB, QB), QB)
                turned[0, :, rows] = n3_ref[rows, :].T
                turned[1, :, rows] = cot_v[rows, :].T
                for i, ref in enumerate(other_refs):
                    turned_others[i, :, rows] = ref[rows, :].T
                turned_others[len(others) - 1, :, rows] = enc_v[rows, :].T
                return carry

            lax.fori_loop(0, L // QB, turn, 0)
        wait(cg)
        wait(cu)
        wait(cd)

        def step(t, carry):
            at = pl.multiple_of(t * tile, LANE)
            gate, upw, down = ws.columns(wg, at, tile), ws.columns(wu, at, tile), wl.columns(wd, at, tile)
            u = nn(n3_ref[...], gate)
            up = nn(n3_ref[...], upw)
            bh = nn(cot_v[...], down)
            sq = u * u
            th = jnp.tanh(GELU_C * (u + GELU_A * (sq * u)))
            both = 0.5 * (1.0 + th)
            gelu = u * both
            slope = both + 0.5 * u * (1.0 - th * th) * (GELU_C * (1.0 + (3.0 * GELU_A) * sq))
            hidden = (gelu * up).astype(BF16)
            gate_low = (bh * up * slope).astype(BF16)
            up_low = (bh * gelu).astype(BF16)
            y_acc[...] += nt(hidden, down)
            b3_acc[...] += nt(gate_low, gate) + nt(up_low, upw)
            for g, low in enumerate((gate_low, up_low, hidden)):
                lows[g, :, pl.ds(at, tile)] = low
            return carry

        lax.fori_loop(0, ff // tile, step, 0)
        pending[...] = jnp.zeros_like(pending)

        def weight(t, before):
            parts.put(g_refs, None, pl.multiple_of(before, LANE), pending[...])
            g = t // (ff // wide)
            at = pl.multiple_of(lax.rem(t, ff // wide) * wide, LANE)
            pending[...] = nn(turned[g // 2], lows[g, :, pl.ds(at, wide)]).astype(BF16)
            return g * ff + at

        at_last = lax.fori_loop(0, 3 * ff // wide, weight, jnp.int32(0))
        parts.put(g_refs, None, pl.multiple_of(at_last, LANE), pending[...])
        if last:
            dg_ref[...] = jnp.zeros_like(dg_ref)

            def finish(t, carry):
                rows = pl.ds(pl.multiple_of(t * QB, QB), QB)
                y_ref[rows, :] = y_acc[rows, :].astype(BF16)
                grad, dg = rms_back(r2_ref[rows, :], gain_ref[2:3, :], b3_acc[rows, :])
                b2_ref[rows, :] = cot_v[rows, :].astype(F32) + grad
                dg_ref[...] += dg
                return carry

            lax.fori_loop(0, L // QB, finish, 0)

    full = ((L, d), F32)
    outs = parts.outs()
    if last:
        outs += [((L, d), BF16), full, ((1, d), F32)]
    else:
        outs += [full, full, ((2, d, L), BF16), ((len(others), d, L), BF16)]
    scratch = [pltpu.VMEM((L, d), F32), pltpu.VMEM((L, d), F32)] if last else []
    result = call(
        body,
        outs,
        [(cotangent, True)]
        + near(n3)
        + (near(r2, gains, *carried) if last else [(others[0], True)] + near(*others[1:]))
        + ws.specs()
        + wl.specs(),
        scratch
        + [
            pltpu.VMEM((L, d), BF16),
            pltpu.VMEM((8, LANE) if last else (L, d), BF16),
            ws.scratch(ff),
            ws.scratch(ff),
            ws.scratch(ff),
            pltpu.VMEM((3, L, ff), BF16),
            pltpu.VMEM((d, wide), BF16),
            DMA,
            DMA,
            ws.sems(),
            ws.sems(),
            ws.sems(),
            wl.sems(),
        ],
        "kcb" if last else "kca",
        7_500_000_000,
    )
    return parts.split(result[:ng]), result[ng:]


def attention_backward(grid, back, qkv, attn, lse, base, pieces, first_col, hd, name):
    ws = Weights(pieces, grid.n_z)
    n = len(ws.arrays)
    w2 = 2 * hd
    causal = base is not None

    def body(*refs):
        b_ref, qkv_ref, o_ref, lse_ref = refs[:4]
        base_ref = refs[4] if causal else None
        refs = refs[5 if causal else 4 :]
        w_refs = refs[:n]
        out_ref = refs[n]
        off_ref = refs[n + 1] if causal else None
        wo, do, p_ref, ds_ref, band_ref, s_o = refs[-6:]
        co = ws.start(w_refs, wo, s_o, first_col, hd)
        if causal:
            off_ref[...] = jnp.zeros_like(off_ref)
        low = b_ref[...].astype(BF16)
        wait(co)
        do[...] = nn(low, ws.value(wo, 0, w2)).astype(BF16)
        attend_back_loop(
            qkv_ref.at[0],
            qkv_ref.at[1],
            qkv_ref.at[2],
            o_ref,
            do,
            lse_ref,
            out_ref.at[0],
            out_ref.at[1],
            out_ref.at[2],
            p_ref,
            ds_ref,
            base_ref,
            off_ref,
            band_ref,
        )

    return call(
        body,
        [((3, L, w2), BF16)] + ([((16, L), F32)] if causal else []),
        near(back, qkv, attn, lse) + (near(base) if causal else []) + ws.specs(),
        [
            ws.scratch(w2),
            pltpu.VMEM((L, w2), BF16),
            pltpu.VMEM((L, 2 * L), BF16),
            pltpu.VMEM((L, 2 * L), BF16),
            pltpu.VMEM((QB, L), F32),
            ws.sems(),
        ],
        name,
        3_000_000_000,
    )


def cross_finish(grid, b2, r1, ready, grads, attn_one, attn_two, gains, pieces, d, hd):
    ws = Weights(pieces, grid.n_z)
    k = len(ws.arrays)
    w2 = 2 * hd
    parts = Parts(grid, d, 5 * hd, True)
    ng = parts.count()

    def body(*refs):
        b2_ref, r1_ref, ready_ref, dy_ref, a1_ref, a2_ref, gain_ref = refs[:7]
        w_refs = refs[7 : 7 + k]
        b1_ref, eg_ref, dg_ref = refs[7 + k : 10 + k]
        g_refs = refs[10 + k : 10 + k + ng]
        w, turned, right, s_w = refs[10 + k + ng :]
        cw = [ws.start(w_refs, w.at[g], s_w, (g + 1) * hd, hd, slot=g) for g in range(3)]
        turned[1] = b2_ref[...].astype(BF16).T
        right[0] = a1_ref[...]
        for g in range(3):
            right[g + 1] = dy_ref[g]
        right[4] = a2_ref[...]
        wait(cw[0])
        dg_ref[...] = jnp.zeros_like(dg_ref)

        def resume(t, carry):
            rows = pl.ds(pl.multiple_of(t * WIDE, WIDE), WIDE)
            grad, dg = rms_back(r1_ref[rows, :], gain_ref[1:2, :], nt(dy_ref[0, rows, :], ws.value(w.at[0], 0, w2)))
            dg_ref[...] += dg
            b1_ref[rows, :] = b2_ref[rows, :] + grad
            return carry

        lax.fori_loop(0, L // WIDE, resume, 0)
        turned[0] = b1_ref[...].astype(BF16).T
        turned[2] = ready_ref[1]
        turned[3] = ready_ref[2]

        def weight(t, carry):
            parts.put_halves(g_refs, pl.multiple_of(2 * t * hd, LANE), hd, nn(turned[3 * t], right[2 * t]))
            parts.put_halves(g_refs, pl.multiple_of((2 * t + 1) * hd, LANE), hd, nn(turned[2 + t], right[2 * t + 1]))
            return carry

        lax.fori_loop(0, 2, weight, 0)
        parts.put_halves(g_refs, 4 * hd, hd, nn(turned[1], right[4]))
        wait(cw[1])
        wait(cw[2])

        def encoder(t, carry):
            rows = pl.ds(pl.multiple_of(t * WIDE, WIDE), WIDE)
            eg = nt(dy_ref[1, rows, :], ws.value(w.at[1], 0, w2)) + nt(dy_ref[2, rows, :], ws.value(w.at[2], 0, w2))
            eg_ref[rows, :] = eg.astype(BF16)
            return carry

        lax.fori_loop(0, L // WIDE, encoder, 0)

    result = call(
        body,
        [((L, d), F32), ((L, d), BF16), ((1, d), F32)] + parts.outs(),
        near(b2, r1, ready, grads, attn_one, attn_two, gains) + ws.specs(),
        [
            ws.scratch(w2, 3),
            pltpu.VMEM((4, d, L), BF16),
            pltpu.VMEM((5, L, w2), BF16),
            ws.sems(3),
        ],
        "kd2",
        5_000_000_000,
    )
    return result[:3], parts.split(result[3:])


def self_finish(grid, inputs, b1, ready, grads, off, dg2, dg3, bucket_row, gains, pieces, d, hd, heads):
    ws = Weights(pieces, grid.n_z)
    k = len(ws.arrays)
    w2 = 2 * hd
    parts = Parts(grid, d, 3 * hd + LANE, True)
    ng = parts.count()

    def body(*refs):
        x_ref, b1_ref, ready_ref, dy_ref, off_ref, dg2_ref, dg3_ref, hot_ref, gain_ref = refs[:9]
        w_refs = refs[9 : 9 + k]
        dx_ref = refs[9 + k]
        g_refs = refs[10 + k : 10 + k + ng]
        x_v, w, back, pending, sem_x, s_w = refs[10 + k + ng :]
        cw = [ws.start(w_refs, w.at[g], s_w, g * hd, hd, slot=g) for g in range(3)]
        cx = sequence_copy(x_ref, x_v, sem_x)
        back[...] = jnp.zeros_like(back)

        def inner(g, carry):
            wait_for(g, cw)
            parts.put_halves(g_refs, pl.multiple_of(jnp.maximum(g - 1, 0) * hd, LANE), hd, pending[...])
            pending[...] = nn(ready_ref[0], dy_ref[g]).astype(BF16)
            back[...] += nt(dy_ref[g], ws.value(w.at[g], 0, w2))
            return carry

        pending[...] = jnp.zeros_like(pending)
        lax.fori_loop(0, 3, inner, 0)
        parts.put_halves(g_refs, 2 * hd, hd, pending[...])
        cx.wait()

        def finish(t, dg):
            rows = pl.ds(pl.multiple_of(t * QB, QB), QB)
            grad, own = rms_back(x_v[rows, :].astype(F32), gain_ref[0:1, :], back[rows, :])
            dx_ref[rows, :] = (b1_ref[rows, :] + grad).astype(BF16)
            return dg + own

        dg = lax.fori_loop(0, L // QB, finish, jnp.zeros((1, d), F32))
        dgs = jnp.concatenate([dg, dg2_ref[...], dg3_ref[...], jnp.zeros((5, d), F32)], axis=0)
        columns = jnp.concatenate([jnp.zeros((NB, d), F32), dgs, jnp.zeros((LANE - NB - 8, d), F32)], axis=0).T
        hot = one_hot(hot_ref[...])
        sums = off_ref[...]
        table = jnp.zeros((16, LANE), F32)
        for _ in range(3):
            low = sums.astype(BF16)
            table = table + nt(low, hot)
            sums = sums - low.astype(F32)
        table = table.astype(BF16)
        shard_row = lax.rem(lax.broadcasted_iota(jnp.int32, (d, 16), 0), parts.rows)
        column = lax.broadcasted_iota(jnp.int32, (d, 16), 1)
        for a in range(2):
            spread = ((shard_row + a * heads == column) & (shard_row < heads)).astype(F32).astype(BF16)
            parts.put(g_refs, a, 3 * hd, nn(spread, table) + columns)

    result = call(
        body,
        [((L, d), BF16)] + parts.outs(),
        [(inputs, True)] + near(b1, ready, grads, off, dg2, dg3, bucket_row, gains) + ws.specs(),
        [
            pltpu.VMEM((L, d), BF16),
            ws.scratch(w2, 3),
            pltpu.VMEM((L, d), F32),
            pltpu.VMEM((d, w2), BF16),
            DMA,
            ws.sems(3),
        ],
        "ke2",
        4_000_000_000,
    )
    return result[0], parts.split(result[1:])


def added(left, right):
    return (left.astype(F32) + right.astype(F32)).astype(BF16)


def scatter(grid, own, own_got, other, other_got, first, held=None):
    sent_a = added(other[..., :first], other_got[..., :first])
    sent_b = jnp.stack([added(v[1, ..., first:], g[1, ..., first:]) for v, g in ((own, own_got), (other, other_got))])
    if held is not None:
        sent_a, sent_b, held = lax.optimization_barrier((sent_a, sent_b, held))
    got = grid.swap_m(sent_a)
    got_b = grid.swap_y(sent_b)

    def a_sum(i):
        return added3(own[i, ..., :first], own_got[i, ..., :first], got[i])

    far_a = grid.swap_y(a_sum(1))
    far_b = grid.swap_m(added3(other[0, ..., first:], other_got[0, ..., first:], got_b[1]))
    wa, wb = a_sum(0), added3(own[0, ..., first:], own_got[0, ..., first:], got_b[0])
    return (wa, wb), (far_a, far_b), held


def joined(kept, far):
    return [
        jnp.concatenate([added(v[d], f[d]) for v, f in zip(kept, far)], axis=-1) for d in range(kept[0].shape[0])
    ]


def scatter_wide(grid, own, own_got, other, other_got, first):
    n = grid.n_z
    got_own = grid.swap_y(added(own[1, ..., first:], own_got[1, ..., first:]))
    got_other = grid.swap_y(added(other[1, ..., first:], other_got[1, ..., first:]))
    got = grid.swap_m(added(other[..., :first], other_got[..., :first]))

    def a_sum(i):
        return added3(own[i, ..., :first], own_got[i, ..., :first], got[i])

    far_a = grid.swap_y(a_sum(1))
    wa = a_sum(0)
    parts = []
    for v, g, far in ((own, own_got, got_own), (other, other_got, got_other)):
        w = [added3(v[0, d, :, first:], g[0, d, :, first:], far[d]) for d in range(n)]
        parts.append([w[0]] + [grid.shift_z(w[d], d) for d in range(1, n)])
    a = [added(wa[d], far_a[d]) for d in range(n)]
    a = [a[0]] + [grid.shift_z(a[d], d) for d in range(1, n)]
    return a, parts[0], parts[1]


def settle(grid, w, gate=None):
    sent = w[1:]
    if gate is not None:
        sent, gate = lax.optimization_barrier((sent, gate))
    return [w[0]] + [grid.shift_z(v, d + 1) for d, v in enumerate(sent)], gate


def summed(arrays):
    out = arrays[0].astype(F32)
    for v in arrays[1:]:
        out = out + v.astype(F32)
    return out


def added3(a, b, c):
    return (a.astype(F32) + b.astype(F32) + c.astype(F32)).astype(BF16)


def both_sequences(mine, other):
    first = lax.axis_index("mp") == 0
    low = jnp.where(first, mine, other)
    high = jnp.where(first, other, mine)
    return jnp.concatenate([low, high], axis=0).astype(F32)


def make(grid):
    def step(
        inputs,
        encoded,
        cotangent,
        buckets,
        rel_table,
        query_self,
        keys_self,
        values_self,
        output_self,
        query_cross,
        keys_cross,
        values_cross,
        output_cross,
        gate_weight,
        up_weight,
        down_weight,
        gain_first,
        gain_second,
        gain_third,
    ):
        d = inputs.shape[1]
        hd = query_self.shape[1]
        ff = gate_weight.shape[1]
        rows = query_self.shape[0]
        heads = rel_table.shape[0]
        assert inputs.shape[0] == 2 * L and heads + 3 <= rows <= LANE and heads <= 8
        extra = jnp.concatenate(
            [
                jnp.pad(rel_table, ((0, 0), (0, LANE - NB))),
                jnp.pad(jnp.stack([gain_first, gain_second, gain_third]), ((0, rows - heads - 3), (0, LANE - rows))),
            ],
            axis=0,
        )
        group_one = jnp.concatenate([query_self, keys_self, values_self, extra], axis=1)
        group_two = jnp.concatenate([output_self.T, query_cross, keys_cross, values_cross, output_cross.T], axis=1)
        turned = down_weight.T
        early = ff - late_columns(ff)
        group_three = jnp.concatenate([gate_weight, up_weight, turned[:, :early]], axis=1)
        pieces_one = gather(grid, group_one)
        pieces_two = gather(grid, group_two)
        pieces_three = gather(grid, group_three)
        pieces_four = gather_late(grid, turned[:, early:])

        bucket_row = buckets[None, :]

        n1, qkv1, at1, gains, base, lse1 = self_forward(grid, inputs, bucket_row, pieces_one, d, hd, heads)
        r1, r2, n2, qkv2, at2, n3, lse2 = cross_forward(grid, inputs, encoded, at1, gains, pieces_two, d, hd)
        (own3, gone), (ya, ba, turned, turned_others) = feed_forward(
            grid, cotangent, n3, r2, gains, None, pieces_three, pieces_four, 0, d, ff, (encoded, n1, n2)
        )
        own3_got = grid.swap_c(gone)
        (other3, gone), (y, b2, dg3) = feed_forward(
            grid, cotangent, n3, r2, gains, (ya, ba, turned), pieces_three, pieces_four, 1, d, ff
        )
        other3_got = grid.swap_c(gone)
        y_far = grid.swap_m(y)
        a3, bo3, bt3 = scatter_wide(grid, own3, own3_got, other3, other3_got, 6 * LANE)
        (dy,) = attention_backward(grid, b2, qkv2, at2, lse2, None, pieces_two, 4 * hd, hd, "kd1")
        (b1, eg, dg2), (kept, gone) = cross_finish(
            grid, b2, r1, turned_others, dy, at1, at2, gains, pieces_two, d, hd
        )
        eg_far = grid.swap_m(eg)
        got = grid.swap_c(gone)
        kept2, far2, _ = scatter(grid, kept[0], got[0], kept[1], got[1], 7 * LANE)
        dy, off = attention_backward(grid, b1, qkv1, at1, lse1, base, pieces_two, 0, hd, "ke1")
        dx, (kept, gone) = self_finish(
            grid, inputs, b1, turned_others, dy, off, dg2, dg3, bucket_row, gains, pieces_one, d, hd, heads
        )
        got = grid.swap_c(gone)
        kept1, far1, (kept2, bt30, y, eg) = scatter(
            grid, kept[0], got[0], kept[1], got[1], 5 * LANE, (kept2, bt3[0], y, eg)
        )
        b3 = bo3 + [grid.swap_m(summed([bt30] + bt3[1:]).astype(BF16))]
        z2, _ = settle(grid, joined(kept2, far2))
        w1 = joined(kept1, far1)
        dx_far = grid.swap_m(dx)
        layer_output = both_sequences(y, y_far)
        encoded_gradient = both_sequences(eg, eg_far)
        z1, (z20, a30, b30) = settle(grid, w1, (z2[0], a3[0], b3[0]))
        input_gradient = both_sequences(dx, dx_far)
        s3 = jnp.concatenate([summed([a30] + a3[1:]), summed([b30] + b3[1:])], axis=-1)
        s2 = summed([z20] + z2[1:])
        s1 = summed(z1)
        small = s1[:, 3 * hd :]
        table_gradient = small[:heads, :NB]
        dgs = [small[:, NB + i] for i in range(3)]
        return (
            layer_output,
            input_gradient,
            encoded_gradient,
            table_gradient,
            s1[:, :hd],
            s1[:, hd : 2 * hd],
            s1[:, 2 * hd : 3 * hd],
            s2[:, :hd].T,
            s2[:, hd : 2 * hd],
            s2[:, 2 * hd : 3 * hd],
            s2[:, 3 * hd : 4 * hd],
            s2[:, 4 * hd :].T,
            s3[:, :ff],
            s3[:, ff : 2 * ff],
            s3[:, 2 * ff :].T,
            dgs[0],
            dgs[1],
            dgs[2],
        )

    return step


def solution(mesh):
    weight, turned, row, gain = P("dp", "mp"), P("mp", "dp"), P("dp", None), P("dp")
    weights = (weight, weight, weight, turned, weight, weight, weight, turned, weight, weight, turned)
    gains = (gain, gain, gain)
    return jax.shard_map(
        make(Grid(mesh.shape["dp"], mesh.shape["mp"])),
        mesh=mesh,
        in_specs=(row, row, row, P(), P("mp", None)) + weights + gains,
        out_specs=(row, row, row, P("mp", None)) + weights + gains,
        check_vma=False,
    )
```
